128 devices in a mesh: dp: 8 (over z_lo, y), pipe: 16 (over z_hi, x, core).
Axes of the slice: x: 4, y: 4, z: 4 (z_hi: 2, z_lo: 2; z = z_hi * 2 + z_lo), core: 2. Of those that a mesh axis runs over, the one named last changes fastest.
Arguments:
- activations: bfloat16 [16, 4096, 8192], P('pipe', 'dp'), may hold values from -6 to 6
- cotangent: bfloat16 [4096, 8192], P('dp'), may hold values from -6 to 6
- adapter_down: bfloat16 [16, 8192, 512], P('pipe'), may hold values from -0.0625 to 0.0625
- adapter_expand: bfloat16 [16, 512, 8192], P('pipe'), may hold values from -0.25 to 0.25
- value_rows: bfloat16 [16, 32, 8192], P('pipe', 'dp'), may hold values from -0.0625 to 0.0625
- input_rows: bfloat16 [16, 32, 8192], P('pipe', 'dp'), may hold values from -0.0625 to 0.0625
- hidden_cols: bfloat16 [16, 32, 512], P('pipe'), may hold values from -0.25 to 0.25
- inner_cols: bfloat16 [16, 32, 512], P('pipe'), may hold values from -0.25 to 0.25
- lengths: int32 [32], P('dp'), may hold values from 1 to 128, as said below
- query_example: int32 [32], replicated, may hold values from 0 to 31
Outputs:
- scores: float32 [32, 32], P('dp')
The draws below stay inside these ranges and needn't reach their ends.
Inputs may be any that keep to these rules, and one draw needn't show every extreme that they name: `lengths`: live tokens of each example; the rest of its 128 positions is padding.
All inputs are finite; a program needn't handle non-finite values.
Results may differ from the reference program's by a relative error of at most 0.022.
Values may be sent and summed in bfloat16 or wider, within the bound.
A program may use at most 128 MiB of HBM per device.

```python
import jax
import jax.numpy as jnp

D = 8192
R = 512
Q = 32
SLOT = 128
LAYERS = 16
TOKENS = 4096
EXAMPLES = 32


def draw_lengths(key, part):
    drawn = jax.random.randint(key, (EXAMPLES,), SLOT // 2, 2 * SLOT, dtype=jnp.int32)
    return jnp.minimum(drawn, SLOT).astype(jnp.int32)


def plant(result, stream_key, least, high):
    spot = [jax.random.randint(jax.random.fold_in(stream_key, axis), (), 0, length) for axis, length in enumerate(result.shape)]
    widest = result.shape.index(max(result.shape))
    neighbour = spot[:widest] + [(spot[widest] + 1) % result.shape[widest]] + spot[widest + 1:]
    return result.at[tuple(spot)].set(least).at[tuple(neighbour)].set(high)


def block_scale(stream_key, dims, shards, smallest, top_value):
    factor_of = 1.0
    for position, shards_of in shards:
        steps = jax.random.uniform(jax.random.fold_in(jax.random.fold_in(stream_key, 6), position), (shards_of,), jnp.float32, smallest / len(shards), top_value / len(shards))
        factor_of = factor_of * jnp.repeat(jnp.exp(steps), dims[position] // shards_of).reshape((-1,) + (1,) * (len(dims) - 1 - position))
    return factor_of


def centred(own_key, dims, width, bound, pieces=(), kind=jnp.bfloat16):
    entries = jax.random.normal(own_key, dims, jnp.float32) * width
    if len(pieces) > 0:
        entries = block_scale(own_key, dims, pieces, -0.22, 0.18) * entries
    return jnp.clip(entries, min=-bound, max=bound).astype(kind)


def setup_inputs(seed: int = 0) -> dict:
    key_of = jax.random.split(jax.random.key(seed), 11)
    return {
        "activations": centred(key_of[0], (LAYERS, TOKENS, D), 1.0, 6.0, ((0, 16), (1, 8))),
        "cotangent": centred(key_of[1], (TOKENS, D), 1.0, 6.0, ((0, 8),)),
        "adapter_down": centred(key_of[2], (LAYERS, D, R), D ** -0.5, 0.0625, ((0, 16),)),
        "adapter_expand": centred(key_of[3], (LAYERS, R, D), R ** -0.5, 0.25, ((0, 16),)),
        "value_rows": centred(key_of[4], (LAYERS, Q, D), D ** -0.5, 0.0625, ((0, 16), (1, 8))),
        "input_rows": centred(key_of[5], (LAYERS, Q, D), D ** -0.5, 0.0625, ((0, 16), (1, 8))),
        "hidden_cols": centred(key_of[6], (LAYERS, Q, R), R ** -0.5, 0.25, ((0, 16),)),
        "inner_cols": centred(key_of[7], (LAYERS, Q, R), R ** -0.5, 0.25, ((0, 16),)),
        "lengths": draw_lengths(jax.random.fold_in(key_of[10], 71), 0),
        "query_example": plant(jax.random.randint(key_of[9], (Q,), 0, EXAMPLES), jax.random.fold_in(key_of[9], 1), 0, EXAMPLES - 1).astype(jnp.int32),
    }


adapter_scale = 0.25


def reference(activations, cotangent, adapter_down, adapter_expand, value_rows, input_rows, hidden_cols, inner_cols, lengths, query_example):
    offsets = jnp.arange(TOKENS, dtype=jnp.int32) % SLOT
    live_mask = (offsets < jnp.repeat(lengths, SLOT, total_repeat_length=TOKENS)).astype(jnp.float32)
    gradient_leaving = cotangent
    totals = jnp.zeros((EXAMPLES, Q), jnp.float32)
    for layer_weights in reversed(range(LAYERS)):
        act_rows = activations[layer_weights]
        hidden = jnp.dot(act_rows, adapter_down[layer_weights], preferred_element_type=jnp.float32).astype(jnp.bfloat16)
        inner_gradient = (adapter_scale * jnp.dot(gradient_leaving, adapter_expand[layer_weights].T, preferred_element_type=jnp.float32)).astype(jnp.bfloat16)
        gradient_entering = (gradient_leaving.astype(jnp.float32) + jnp.dot(inner_gradient, adapter_down[layer_weights].T, preferred_element_type=jnp.float32)).astype(jnp.bfloat16)
        hidden_projection = jnp.dot(hidden, hidden_cols[layer_weights].T, preferred_element_type=jnp.float32)
        value_projection = jnp.dot(gradient_leaving, value_rows[layer_weights].T, preferred_element_type=jnp.float32)
        input_projection = jnp.dot(act_rows, input_rows[layer_weights].T, preferred_element_type=jnp.float32)
        inner_projection = jnp.dot(inner_gradient, inner_cols[layer_weights].T, preferred_element_type=jnp.float32)
        summand_rows = adapter_scale * hidden_projection * value_projection + input_projection * inner_projection
        masked = summand_rows * live_mask[:, None]
        totals = totals + jnp.sum(masked.reshape(EXAMPLES, SLOT, Q), axis=1)
        gradient_leaving = gradient_entering
    totals = totals * (SLOT ** -0.5)
    example_ids = jnp.arange(EXAMPLES, dtype=jnp.int32)
    keep_mask = (example_ids[:, None] != query_example[None, :]).astype(jnp.float32)
    return totals * keep_mask
```

```python
import functools

import jax
import jax.numpy as jnp
from jax import lax
from jax.experimental import pallas as pl
from jax.experimental.pallas import tpu as pltpu
from jax.sharding import PartitionSpec as P

SLOT = 128
ADAPTER_SCALE = 0.25
MESH = pl.DeviceIdType.MESH
F32 = jnp.float32
BF16 = jnp.bfloat16
CHUNKS = 4
PIECES = 8
HEAD = 2


def nt(a, b):
    return lax.dot_general(a, b, (((1,), (1,)), ((), ())), preferred_element_type=F32)


def kernel(
    n_dp,
    n_pipe,
    x_hbm,
    cot_hbm,
    d_hbm,
    e_hbm,
    v_ref,
    i_ref,
    hc_ref,
    ic_ref,
    len_ref,
    qe_ref,
    out_ref,
    x_v,
    cot_v,
    d_v,
    e_v,
    z_in,
    z_out,
    a_all,
    hp_all,
    rows_all,
    u_acc,
    u_bf,
    own_acc,
    hp_acc,
    total,
    s_all,
    load_e,
    load_d,
    load_cot,
    load_x,
    rows_send,
    rows_recv,
    z_send,
    z_recv,
    a_send,
    a_recv,
    hp_send,
    hp_recv,
    s_send,
    s_recv,
):
    lane = lax.axis_index("dp")
    layer = lax.axis_index("pipe")
    width, rank = d_v.shape
    tokens = u_acc.shape[1]
    group = z_in.shape[1]
    half = group // 2
    queries = hc_ref.shape[1]
    every = group * n_dp
    wide = width // CHUNKS
    piece = width // PIECES
    n_example = len_ref.shape[0]

    def load_expand(c):
        cols = pl.ds(c * wide, wide)
        return pltpu.make_async_copy(e_hbm.at[0, :, cols], e_v.at[:, cols], load_e.at[c])

    def load_down(c):
        rows = pl.ds(c * wide, wide)
        return pltpu.make_async_copy(d_hbm.at[0, rows, :], d_v.at[rows, :], load_d.at[c])

    def load_cotangent(k):
        cols = pl.ds(pl.multiple_of(k * piece, piece), piece)
        return pltpu.make_async_copy(cot_hbm.at[:, cols], cot_v.at[k], load_cot.at[k])

    def load_activation(k):
        cols = pl.ds(pl.multiple_of(k * piece, piece), piece)
        return pltpu.make_async_copy(x_hbm.at[0, :, cols], x_v.at[k], load_x.at[k])

    for c in range(CHUNKS):
        load_expand(c).start()
    for c in range(CHUNKS):
        load_down(c).start()
    for k in range(PIECES):
        load_cotangent(k).start()
    for k in range(PIECES):
        load_activation(k).start()

    barrier = pltpu.get_barrier_semaphore()
    for k in range(1, n_dp):
        pl.semaphore_signal(
            barrier, 1, device_id={"dp": lax.rem(lane + k, n_dp)}, device_id_type=MESH
        )
    for k in range(1, n_pipe):
        pl.semaphore_signal(
            barrier, 1, device_id={"pipe": lax.rem(layer + k, n_pipe)}, device_id_type=MESH
        )
    pl.semaphore_wait(barrier, n_dp + n_pipe - 2)

    v_rows = v_ref[0].astype(F32)
    rows_all[lane] = jnp.concatenate([v_rows, i_ref[0].astype(F32)], axis=0).astype(BF16)

    def rows_copy(k):
        return pltpu.make_async_remote_copy(
            src_ref=rows_all.at[lane],
            dst_ref=rows_all.at[lane],
            send_sem=rows_send.at[k],
            recv_sem=rows_recv,
            device_id={"dp": lax.rem(lane + k, n_dp)},
            device_id_type=MESH,
        )

    for k in range(1, n_dp):
        rows_copy(k).start()

    def placed(first):
        row = lax.broadcasted_iota(jnp.int32, (every, queries), 0)
        col = lax.broadcasted_iota(jnp.int32, (every, queries), 1)
        within = lax.rem(row, group) - first
        query = (row // group) * half + within
        hit = (within >= 0) & (within < half) & (query == col)
        return jnp.where(hit, 1.0, 0.0).astype(BF16)

    hc_placed = jnp.dot(placed(0), hc_ref[0], preferred_element_type=F32).astype(BF16)
    ic_placed = jnp.dot(placed(half), ic_ref[0], preferred_element_type=F32).astype(BF16)
    row = lax.broadcasted_iota(jnp.int32, (group, queries), 0)
    col = lax.broadcasted_iota(jnp.int32, (group, queries), 1)
    pick = jnp.where((row >= half) & (lane * half + row - half == col), 1.0, 0.0).astype(BF16)
    ic_lane = jnp.dot(pick, ic_ref[0], preferred_element_type=F32).astype(BF16)
    v_wide = jnp.concatenate([v_rows, jnp.zeros_like(v_rows)], axis=0)

    def z_copy(step, c):
        cols = pl.ds(c * wide, wide)
        return pltpu.make_async_remote_copy(
            src_ref=z_out.at[lax.rem(step, 2), :, cols],
            dst_ref=z_in.at[step, :, cols],
            send_sem=z_send.at[c],
            recv_sem=z_recv.at[step, c],
            device_id={"pipe": lax.rem(layer + 1, n_pipe)},
            device_id_type=MESH,
        )

    has_next = layer < n_pipe - 1

    for c in range(CHUNKS):
        cols = slice(c * wide, (c + 1) * wide)
        load_expand(c).wait()
        born = v_wide[:, cols] + jnp.dot(ic_lane, e_v[:, cols], preferred_element_type=F32)
        z_out[0, :, cols] = born.astype(BF16)

        @pl.when(has_next)
        def _():
            z_copy(0, c).start()

    for c in range(CHUNKS):
        load_down(c).wait()

    def a_copy(step, k):
        return pltpu.make_async_remote_copy(
            src_ref=a_all.at[step, lane],
            dst_ref=a_all.at[step, lane],
            send_sem=a_send.at[k],
            recv_sem=a_recv.at[step],
            device_id={"dp": lax.rem(lane + k, n_dp)},
            device_id_type=MESH,
        )

    def chain(step):
        projected = jnp.zeros((group, rank), F32)
        for c in range(CHUNKS):
            cols = slice(c * wide, (c + 1) * wide)
            z_copy(step - 1, c).wait_recv()
            projected += jnp.dot(
                z_in[step - 1, :, cols], d_v[cols, :], preferred_element_type=F32
            )
        factor = (ADAPTER_SCALE * projected).astype(BF16)

        @pl.when(has_next)
        def _():
            slot = lax.rem(step, 2)
            for c in range(CHUNKS):
                cols = slice(c * wide, (c + 1) * wide)
                moved = z_in[step - 1, :, cols].astype(F32) + jnp.dot(
                    factor, e_v[:, cols], preferred_element_type=F32
                )
                z_out[slot, :, cols] = moved.astype(BF16)
                z_copy(step - 1, c).wait_send()
                z_copy(step, c).start()

        a_all[step, lane] = factor
        for k in range(1, n_dp):

            @pl.when(step > 1)
            def _():
                a_copy(step - 1, k).wait_send()

            a_copy(step, k).start()

    def token_part(k):
        load_cotangent(k).wait()
        cols = pl.ds(pl.multiple_of(k * piece, piece), piece)
        u_acc[...] += nt(e_v[:, cols], cot_v[k])

    def row_part(k):
        load_activation(k).wait()
        cols = pl.ds(pl.multiple_of(k * piece, piece), piece)
        gathered = rows_all[:, :, cols].astype(F32).reshape(every, piece)
        of_value = lax.rem(lax.broadcasted_iota(jnp.int32, (every, piece), 0), group) < half
        value_side = jnp.where(of_value, gathered, 0.0).astype(BF16)
        own_acc[...] += nt(value_side, cot_v[k])
        hidden_side = nt(hc_placed, d_v[cols, :])
        input_side = (hidden_side + jnp.where(of_value, 0.0, gathered)).astype(BF16)
        hp_acc[...] += nt(input_side, x_v[k])

    def hp_copy(target):
        return pltpu.make_async_remote_copy(
            src_ref=hp_all.at[layer],
            dst_ref=hp_all.at[layer],
            send_sem=hp_send.at[target],
            recv_sem=hp_recv.at[layer],
            device_id={"pipe": target},
            device_id_type=MESH,
        )

    def settle():
        token = lax.broadcasted_iota(jnp.int32, (every, tokens), 1)
        count = jnp.zeros((every, tokens), jnp.int32)
        for e in range(n_example):
            count = jnp.where(token // SLOT == e, len_ref[e], count)
        live = jnp.where(lax.rem(token, SLOT) < count, 1.0, 0.0)
        hp_all[layer] = (hp_acc[...] * live).astype(BF16)
        for target in range(1, n_pipe):

            @pl.when(layer < target)
            def _():
                hp_copy(target).start()

        u_bf[...] = u_acc[...].astype(BF16)
        own = own_acc[...] + jnp.dot(ic_placed, u_bf[...], preferred_element_type=F32)
        total[...] = own * hp_all[layer].astype(F32)

    def collect(step):
        @pl.when(layer >= step)
        def _():
            source = jnp.maximum(layer - step, 0)
            pltpu.make_async_copy(
                a_all.at[step, pl.ds(0, n_dp - 1)], a_all.at[step, pl.ds(0, n_dp - 1)], a_recv.at[step]
            ).wait()
            pltpu.make_async_copy(hp_all.at[source], hp_all.at[source], hp_recv.at[source]).wait()
            factors = a_all[step].astype(F32).reshape(every, rank).astype(BF16)
            total[...] += jnp.dot(factors, u_bf[...], preferred_element_type=F32) * hp_all[
                source
            ].astype(F32)

    u_acc[...] = jnp.zeros_like(u_acc)
    own_acc[...] = jnp.zeros_like(own_acc)
    hp_acc[...] = jnp.zeros_like(hp_acc)

    last_row = HEAD + PIECES
    per_step = 3

    def advance(step, carry):
        @pl.when(layer >= step)
        def _():
            chain(step)

        @pl.when(step <= PIECES)
        def _():
            token_part(jnp.minimum(step - 1, PIECES - 1))

        @pl.when(step == HEAD + 1)
        def _():
            rows_full = rows_all.at[pl.ds(0, n_dp - 1)]
            pltpu.make_async_copy(rows_full, rows_full, rows_recv).wait()

        @pl.when((step > HEAD) & (step <= last_row))
        def _():
            row_part(jnp.clip(step - 1 - HEAD, 0, PIECES - 1))

        @pl.when(step == last_row)
        def _():
            settle()

        return carry

    lax.fori_loop(1, last_row + 1, advance, 0)

    def advance_late(step, carry):
        @pl.when(layer >= step)
        def _():
            chain(step)

        first = (step - last_row - 1) * per_step
        for i in range(1, per_step + 1):

            @pl.when(first + i < n_pipe - per_step)
            def _():
                collect(jnp.minimum(first + i, n_pipe - 1))

        return carry

    lax.fori_loop(last_row + 1, n_pipe, advance_late, 0)
    for step in range(n_pipe - per_step, n_pipe):
        collect(step)

    row = lax.broadcasted_iota(jnp.int32, (8, tokens), 0)
    token = lax.broadcasted_iota(jnp.int32, (8, tokens), 1)
    members = jnp.where(token // SLOT == row, 1.0, 0.0)
    sums = lax.dot_general(
        members,
        total[...],
        (((1,), (1,)), ((), ())),
        precision=lax.Precision.HIGHEST,
        preferred_element_type=F32,
    )
    row = lax.broadcasted_iota(jnp.int32, (every, 128), 0)
    col = lax.broadcasted_iota(jnp.int32, (every, 128), 1)
    joined = jnp.where((row // group) * half + lax.rem(row, half) == col, 1.0, 0.0)
    s_all[layer] = jnp.dot(
        sums, joined, precision=lax.Precision.HIGHEST, preferred_element_type=F32
    )

    def s_copy(k):
        return pltpu.make_async_remote_copy(
            src_ref=s_all.at[layer],
            dst_ref=s_all.at[layer],
            send_sem=s_send.at[k],
            recv_sem=s_recv,
            device_id={"pipe": lax.rem(layer + k, n_pipe)},
            device_id_type=MESH,
        )

    for k in range(1, n_pipe):
        s_copy(k).start()

    for k in range(1, n_dp):
        rows_copy(k).wait_send()

        @pl.when(layer >= 1)
        def _():
            a_copy(layer, k).wait_send()

    @pl.when(has_next)
    def _():
        for c in range(CHUNKS):
            z_copy(layer, c).wait_send()

    for target in range(1, n_pipe):

        @pl.when(layer < target)
        def _():
            hp_copy(target).wait_send()

    for k in range(1, n_pipe):
        s_copy(k).wait_send()
    arrived = s_all.at[pl.ds(0, n_pipe - 1)]
    pltpu.make_async_copy(arrived, arrived, s_recv).wait()
    result = s_all[0]
    for source in range(1, n_pipe):
        result = result + s_all[source]
    result = result[:n_example, :queries] * (ADAPTER_SCALE * SLOT**-0.5)
    example = lane * n_example + lax.broadcasted_iota(jnp.int32, (n_example, queries), 0)
    out_ref[...] = result * jnp.where(example != qe_ref[...], 1.0, 0.0)


def solution(mesh):
    n_dp, n_pipe = mesh.shape["dp"], mesh.shape["pipe"]

    def local(act, cot, down, expand, value, inputs, hidden_cols, inner_cols, lengths, query):
        tokens, width = cot.shape
        rank = down.shape[2]
        queries = hidden_cols.shape[1]
        n_example = tokens // SLOT
        group = 2 * value.shape[1]
        every = group * n_dp
        hbm = pl.BlockSpec(memory_space=pl.ANY)
        vmem = pl.BlockSpec(memory_space=pltpu.VMEM)
        smem = pl.BlockSpec(memory_space=pltpu.SMEM)
        dma = pltpu.SemaphoreType.DMA
        return pl.pallas_call(
            functools.partial(kernel, n_dp, n_pipe),
            out_shape=jax.ShapeDtypeStruct((n_example, queries), F32),
            in_specs=[hbm, hbm, hbm, hbm, vmem, vmem, vmem, vmem, smem, vmem],
            out_specs=vmem,
            scratch_shapes=[
                pltpu.VMEM((PIECES, tokens, width // PIECES), BF16),
                pltpu.VMEM((PIECES, tokens, width // PIECES), BF16),
                pltpu.VMEM((width, rank), BF16),
                pltpu.VMEM((rank, width), BF16),
                pltpu.VMEM((n_pipe, group, width), BF16),
                pltpu.VMEM((2, group, width), BF16),
                pltpu.VMEM((n_pipe, n_dp, group, rank), BF16),
                pltpu.VMEM((n_pipe, every, tokens), BF16),
                pltpu.VMEM((n_dp, group, width), BF16),
                pltpu.VMEM((rank, tokens), F32),
                pltpu.VMEM((rank, tokens), BF16),
                pltpu.VMEM((every, tokens), F32),
                pltpu.VMEM((every, tokens), F32),
                pltpu.VMEM((every, tokens), F32),
                pltpu.VMEM((n_pipe, 8, 128), F32),
                dma((CHUNKS,)),
                dma((CHUNKS,)),
                dma((PIECES,)),
                dma((PIECES,)),
                dma((n_dp,)),
                dma,
                dma((CHUNKS,)),
                dma((n_pipe, CHUNKS)),
                dma((n_dp,)),
                dma((n_pipe,)),
                dma((n_pipe,)),
                dma((n_pipe,)),
                dma((n_pipe,)),
                dma,
            ],
            compiler_params=pltpu.CompilerParams(
                collective_id=0, has_side_effects=True, vmem_limit_bytes=58 << 20
            ),
            name="influence",
        )(
            act,
            cot,
            down,
            expand,
            value,
            inputs,
            hidden_cols,
            inner_cols,
            lengths,
            query.reshape(1, queries),
        )

    in_specs = (
        P("pipe", "dp", None),
        P("dp", None),
        P("pipe", None, None),
        P("pipe", None, None),
        P("pipe", "dp", None),
        P("pipe", "dp", None),
        P("pipe", None, None),
        P("pipe", None, None),
        P("dp"),
        P(),
    )
    return jax.shard_map(
        local, mesh=mesh, in_specs=in_specs, out_specs=P("dp", None), check_vma=False
    )
```

```python
import functools

import jax
import jax.numpy as jnp
from jax import lax
from jax.experimental import pallas as pl
from jax.experimental.pallas import tpu as pltpu
from jax.sharding import PartitionSpec as P

SLOT = 128
ADAPTER_SCALE = 0.25
MESH = pl.DeviceIdType.MESH
F32 = jnp.float32
BF16 = jnp.bfloat16
CHUNKS = 4
PIECES = 8
LOW = 6
HEAD = 2


def nt(a, b):
    return lax.dot_general(a, b, (((1,), (1,)), ((), ())), preferred_element_type=F32)


def kernel(
    n_dp,
    n_pipe,
    x_hbm,
    cot_hbm,
    d_hbm,
    e_hbm,
    v_ref,
    i_ref,
    hc_ref,
    ic_ref,
    len_ref,
    qe_ref,
    out_ref,
    x_v,
    cot_v,
    d_v,
    e_v,
    z_in,
    z_out,
    a_all,
    hp_all,
    rows_all,
    u_acc,
    u_bf,
    own_acc,
    hp_acc,
    total,
    s_all,
    load_e,
    load_d,
    load_cot,
    load_x,
    rows_send,
    rows_recv,
    z_send,
    z_recv,
    a_send,
    a_recv,
    hp_send,
    hp_recv,
    s_send,
    s_recv,
):
    lane = lax.axis_index("dp")
    layer = lax.axis_index("pipe")
    width, rank = d_v.shape
    tokens = u_acc.shape[1]
    group = z_in.shape[1]
    half = group // 2
    queries = hc_ref.shape[1]
    every = group * n_dp
    wide = width // CHUNKS
    piece = width // PIECES
    n_example = len_ref.shape[0]

    def load_expand(c):
        cols = pl.ds(c * wide, wide)
        return pltpu.make_async_copy(e_hbm.at[0, :, cols], e_v.at[:, cols], load_e.at[c])

    def load_down(c):
        rows = pl.ds(c * wide, wide)
        return pltpu.make_async_copy(d_hbm.at[0, rows, :], d_v.at[rows, :], load_d.at[c])

    def load_cotangent(k):
        cols = pl.ds(pl.multiple_of(k * piece, piece), piece)
        return pltpu.make_async_copy(cot_hbm.at[:, cols], cot_v.at[k], load_cot.at[k])

    def load_activation(k):
        cols = pl.ds(pl.multiple_of(k * piece, piece), piece)
        return pltpu.make_async_copy(x_hbm.at[0, :, cols], x_v.at[k], load_x.at[k])

    for c in range(CHUNKS):
        load_expand(c).start()
    for c in range(CHUNKS):
        load_down(c).start()
    for k in range(PIECES):
        load_cotangent(k).start()
    for k in range(PIECES):
        load_activation(k).start()

    barrier = pltpu.get_barrier_semaphore()
    for k in range(1, n_dp):
        pl.semaphore_signal(
            barrier, 1, device_id={"dp": lax.rem(lane + k, n_dp)}, device_id_type=MESH
        )
    for k in range(1, n_pipe):
        pl.semaphore_signal(
            barrier, 1, device_id={"pipe": lax.rem(layer + k, n_pipe)}, device_id_type=MESH
        )
    pl.semaphore_wait(barrier, n_dp + n_pipe - 2)

    v_rows = v_ref[0].astype(F32)
    rows_all[lane] = jnp.concatenate([v_rows, i_ref[0].astype(F32)], axis=0).astype(BF16)

    def rows_copy(k):
        return pltpu.make_async_remote_copy(
            src_ref=rows_all.at[lane],
            dst_ref=rows_all.at[lane],
            send_sem=rows_send.at[k],
            recv_sem=rows_recv,
            device_id={"dp": lax.rem(lane + k, n_dp)},
            device_id_type=MESH,
        )

    for k in range(1, n_dp):
        rows_copy(k).start()

    def placed(first):
        row = lax.broadcasted_iota(jnp.int32, (every, queries), 0)
        col = lax.broadcasted_iota(jnp.int32, (every, queries), 1)
        within = lax.rem(row, group) - first
        query = (row // group) * half + within
        hit = (within >= 0) & (within < half) & (query == col)
        return jnp.where(hit, 1.0, 0.0).astype(BF16)

    hc_placed = jnp.dot(placed(0), hc_ref[0], preferred_element_type=F32).astype(BF16)
    ic_placed = jnp.dot(placed(half), ic_ref[0], preferred_element_type=F32).astype(BF16)
    row = lax.broadcasted_iota(jnp.int32, (group, queries), 0)
    col = lax.broadcasted_iota(jnp.int32, (group, queries), 1)
    pick = jnp.where((row >= half) & (lane * half + row - half == col), 1.0, 0.0).astype(BF16)
    ic_lane = jnp.dot(pick, ic_ref[0], preferred_element_type=F32).astype(BF16)
    v_wide = jnp.concatenate([v_rows, jnp.zeros_like(v_rows)], axis=0)

    def z_copy(step, c):
        cols = pl.ds(c * wide, wide)
        return pltpu.make_async_remote_copy(
            src_ref=z_out.at[lax.rem(step, 2), :, cols],
            dst_ref=z_in.at[step, :, cols],
            send_sem=z_send.at[c],
            recv_sem=z_recv.at[step, c],
            device_id={"pipe": lax.rem(layer + 1, n_pipe)},
            device_id_type=MESH,
        )

    has_next = layer < n_pipe - 1

    for c in range(CHUNKS):
        cols = slice(c * wide, (c + 1) * wide)
        load_expand(c).wait()
        born = v_wide[:, cols] + jnp.dot(ic_lane, e_v[:, cols], preferred_element_type=F32)
        z_out[0, :, cols] = born.astype(BF16)

        @pl.when(has_next)
        def _():
            z_copy(0, c).start()

    for c in range(CHUNKS):
        load_down(c).wait()

    def a_copy(step, k):
        return pltpu.make_async_remote_copy(
            src_ref=a_all.at[step, lane],
            dst_ref=a_all.at[step, lane],
            send_sem=a_send.at[k],
            recv_sem=a_recv.at[step],
            device_id={"dp": lax.rem(lane + k, n_dp)},
            device_id_type=MESH,
        )

    def chain(step):
        projected = jnp.zeros((group, rank), F32)
        for c in range(CHUNKS):
            cols = slice(c * wide, (c + 1) * wide)
            z_copy(step - 1, c).wait_recv()
            projected += jnp.dot(
                z_in[step - 1, :, cols], d_v[cols, :], preferred_element_type=F32
            )
        factor = (ADAPTER_SCALE * projected).astype(BF16)

        @pl.when(has_next)
        def _():
            slot = lax.rem(step, 2)
            for c in range(CHUNKS):
                cols = slice(c * wide, (c + 1) * wide)
                moved = z_in[step - 1, :, cols].astype(F32) + jnp.dot(
                    factor, e_v[:, cols], preferred_element_type=F32
                )
                z_out[slot, :, cols] = moved.astype(BF16)
                z_copy(step - 1, c).wait_send()
                z_copy(step, c).start()

        a_all[step, lane] = factor
        for k in range(1, n_dp):

            @pl.when(step > 1)
            def _():
                a_copy(step - 1, k).wait_send()

            a_copy(step, k).start()

    def token_part(k):
        load_cotangent(k).wait()
        cols = pl.ds(pl.multiple_of(k * piece, piece), piece)
        u_acc[...] += nt(e_v[:, cols], cot_v[k])

    def row_part(k):
        load_activation(k).wait()
        cols = pl.ds(pl.multiple_of(k * piece, piece), piece)
        gathered = rows_all[:, :, cols].astype(F32).reshape(every, piece)
        of_value = lax.rem(lax.broadcasted_iota(jnp.int32, (every, piece), 0), group) < half
        value_side = jnp.where(of_value, gathered, 0.0).astype(BF16)
        own_acc[...] += nt(value_side, cot_v[k])
        hidden_side = nt(hc_placed, d_v[cols, :])
        input_side = (hidden_side + jnp.where(of_value, 0.0, gathered)).astype(BF16)
        hp_acc[...] += nt(input_side, x_v[k])

    def hp_copy(target):
        return pltpu.make_async_remote_copy(
            src_ref=hp_all.at[layer],
            dst_ref=hp_all.at[layer],
            send_sem=hp_send.at[target],
            recv_sem=hp_recv.at[layer],
            device_id={"pipe": target},
            device_id_type=MESH,
        )

    def settle():
        token = lax.broadcasted_iota(jnp.int32, (every, tokens), 1)
        count = jnp.zeros((every, tokens), jnp.int32)
        for e in range(n_example):
            count = jnp.where(token // SLOT == e, len_ref[e], count)
        live = jnp.where(lax.rem(token, SLOT) < count, 1.0, 0.0)
        hp_all[layer] = (hp_acc[...] * live).astype(BF16)
        for target in range(1, n_pipe):

            @pl.when(layer < target)
            def _():
                hp_copy(target).start()

        u_bf[...] = u_acc[...].astype(BF16)
        own = own_acc[...] + jnp.dot(ic_placed, u_bf[...], preferred_element_type=F32)
        total[...] = own * hp_all[layer].astype(F32)

    def collect(step):
        @pl.when(layer >= step)
        def _():
            source = jnp.maximum(layer - step, 0)
            pltpu.make_async_copy(
                a_all.at[step, pl.ds(0, n_dp - 1)], a_all.at[step, pl.ds(0, n_dp - 1)], a_recv.at[step]
            ).wait()
            pltpu.make_async_copy(hp_all.at[source], hp_all.at[source], hp_recv.at[source]).wait()
            factors = a_all[step].astype(F32).reshape(every, rank).astype(BF16)
            total[...] += jnp.dot(factors, u_bf[...], preferred_element_type=F32) * hp_all[
                source
            ].astype(F32)

    u_acc[...] = jnp.zeros_like(u_acc)
    own_acc[...] = jnp.zeros_like(own_acc)
    hp_acc[...] = jnp.zeros_like(hp_acc)

    begin = jnp.where(layer < LOW, layer, 0)
    row_begin = jnp.maximum(begin, HEAD)
    per_step = 3
    first_collect = n_pipe - n_pipe // per_step

    def advance(step, carry):
        @pl.when(layer >= step)
        def _():
            chain(step)

        @pl.when((step > begin) & (step <= begin + PIECES))
        def _():
            token_part(jnp.clip(step - 1 - begin, 0, PIECES - 1))

        @pl.when(step == row_begin + 1)
        def _():
            rows_full = rows_all.at[pl.ds(0, n_dp - 1)]
            pltpu.make_async_copy(rows_full, rows_full, rows_recv).wait()

        @pl.when((step > row_begin) & (step <= row_begin + PIECES))
        def _():
            row_part(jnp.clip(step - 1 - row_begin, 0, PIECES - 1))

        @pl.when(step == row_begin + PIECES)
        def _():
            settle()

        @pl.when((step >= first_collect) & (layer >= LOW))
        def _():
            first = (step - first_collect) * per_step
            for i in range(1, per_step + 1):

                @pl.when(first + i < n_pipe - per_step)
                def _():
                    collect(jnp.clip(first + i, 1, n_pipe - 1))

        return carry

    lax.fori_loop(1, n_pipe, advance, 0)

    @pl.when(layer < LOW)
    def _():
        for step in range(1, LOW):
            collect(step)

    @pl.when(layer >= LOW)
    def _():
        for step in range(n_pipe - per_step, n_pipe):
            collect(step)

    row = lax.broadcasted_iota(jnp.int32, (8, tokens), 0)
    token = lax.broadcasted_iota(jnp.int32, (8, tokens), 1)
    members = jnp.where(token // SLOT == row, 1.0, 0.0)
    sums = lax.dot_general(
        members,
        total[...],
        (((1,), (1,)), ((), ())),
        precision=lax.Precision.HIGHEST,
        preferred_element_type=F32,
    )
    row = lax.broadcasted_iota(jnp.int32, (every, 128), 0)
    col = lax.broadcasted_iota(jnp.int32, (every, 128), 1)
    joined = jnp.where((row // group) * half + lax.rem(row, half) == col, 1.0, 0.0)
    s_all[layer] = jnp.dot(
        sums, joined, precision=lax.Precision.HIGHEST, preferred_element_type=F32
    )

    def s_copy(k):
        return pltpu.make_async_remote_copy(
            src_ref=s_all.at[layer],
            dst_ref=s_all.at[layer],
            send_sem=s_send.at[k],
            recv_sem=s_recv,
            device_id={"pipe": lax.rem(layer + k, n_pipe)},
            device_id_type=MESH,
        )

    for k in range(1, n_pipe):
        s_copy(k).start()

    for k in range(1, n_dp):
        rows_copy(k).wait_send()

        @pl.when(layer >= 1)
        def _():
            a_copy(layer, k).wait_send()

    @pl.when(has_next)
    def _():
        for c in range(CHUNKS):
            z_copy(layer, c).wait_send()

    for target in range(1, n_pipe):

        @pl.when(layer < target)
        def _():
            hp_copy(target).wait_send()

    for k in range(1, n_pipe):
        s_copy(k).wait_send()
    arrived = s_all.at[pl.ds(0, n_pipe - 1)]
    pltpu.make_async_copy(arrived, arrived, s_recv).wait()
    result = s_all[0]
    for source in range(1, n_pipe):
        result = result + s_all[source]
    result = result[:n_example, :queries] * (ADAPTER_SCALE * SLOT**-0.5)
    example = lane * n_example + lax.broadcasted_iota(jnp.int32, (n_example, queries), 0)
    out_ref[...] = result * jnp.where(example != qe_ref[...], 1.0, 0.0)


def solution(mesh):
    n_dp, n_pipe = mesh.shape["dp"], mesh.shape["pipe"]

    def local(act, cot, down, expand, value, inputs, hidden_cols, inner_cols, lengths, query):
        tokens, width = cot.shape
        rank = down.shape[2]
        queries = hidden_cols.shape[1]
        n_example = tokens // SLOT
        group = 2 * value.shape[1]
        every = group * n_dp
        hbm = pl.BlockSpec(memory_space=pl.ANY)
        vmem = pl.BlockSpec(memory_space=pltpu.VMEM)
        smem = pl.BlockSpec(memory_space=pltpu.SMEM)
        dma = pltpu.SemaphoreType.DMA
        return pl.pallas_call(
            functools.partial(kernel, n_dp, n_pipe),
            out_shape=jax.ShapeDtypeStruct((n_example, queries), F32),
            in_specs=[hbm, hbm, hbm, hbm, vmem, vmem, vmem, vmem, smem, vmem],
            out_specs=vmem,
            scratch_shapes=[
                pltpu.VMEM((PIECES, tokens, width // PIECES), BF16),
                pltpu.VMEM((PIECES, tokens, width // PIECES), BF16),
                pltpu.VMEM((width, rank), BF16),
                pltpu.VMEM((rank, width), BF16),
                pltpu.VMEM((n_pipe, group, width), BF16),
                pltpu.VMEM((2, group, width), BF16),
                pltpu.VMEM((n_pipe, n_dp, group, rank), BF16),
                pltpu.VMEM((n_pipe, every, tokens), BF16),
                pltpu.VMEM((n_dp, group, width), BF16),
                pltpu.VMEM((rank, tokens), F32),
                pltpu.VMEM((rank, tokens), BF16),
                pltpu.VMEM((every, tokens), F32),
                pltpu.VMEM((every, tokens), F32),
                pltpu.VMEM((every, tokens), F32),
                pltpu.VMEM((n_pipe, 8, 128), F32),
                dma((CHUNKS,)),
                dma((CHUNKS,)),
                dma((PIECES,)),
                dma((PIECES,)),
                dma((n_dp,)),
                dma,
                dma((CHUNKS,)),
                dma((n_pipe, CHUNKS)),
                dma((n_dp,)),
                dma((n_pipe,)),
                dma((n_pipe,)),
                dma((n_pipe,)),
                dma((n_pipe,)),
                dma,
            ],
            compiler_params=pltpu.CompilerParams(
                collective_id=0, has_side_effects=True, vmem_limit_bytes=58 << 20
            ),
            name="influence",
        )(
            act,
            cot,
            down,
            expand,
            value,
            inputs,
            hidden_cols,
            inner_cols,
            lengths,
            query.reshape(1, queries),
        )

    in_specs = (
        P("pipe", "dp", None),
        P("dp", None),
        P("pipe", None, None),
        P("pipe", None, None),
        P("pipe", "dp", None),
        P("pipe", "dp", None),
        P("pipe", None, None),
        P("pipe", None, None),
        P("dp"),
        P(),
    )
    return jax.shard_map(
        local, mesh=mesh, in_specs=in_specs, out_specs=P("dp", None), check_vma=False
    )
```

```python
import functools

import jax
import jax.numpy as jnp
from jax import lax
from jax.experimental import pallas as pl
from jax.experimental.pallas import tpu as pltpu
from jax.sharding import PartitionSpec as P

SLOT = 128
ADAPTER_SCALE = 0.25
MESH = pl.DeviceIdType.MESH
F32 = jnp.float32
BF16 = jnp.bfloat16
CHUNKS = 4
PIECES = 8
ALONE = 1
LOW = 3


def nt(a, b):
    return lax.dot_general(a, b, (((1,), (1,)), ((), ())), preferred_element_type=F32)


def kernel(
    n_dp,
    n_pipe,
    x_hbm,
    cot_hbm,
    d_hbm,
    e_hbm,
    v_ref,
    i_ref,
    hc_ref,
    ic_ref,
    len_ref,
    qe_ref,
    out_ref,
    x_v,
    cot_v,
    d_v,
    e_v,
    z_in,
    y_in,
    sent,
    a_all,
    f_in,
    k_part,
    k_all,
    hp_all,
    rows_all,
    u_acc,
    u_bf,
    own_acc,
    hp_acc,
    total,
    s_all,
    load_e,
    load_d,
    load_cot,
    load_x,
    rows_send,
    rows_recv,
    main_send,
    pass_send,
    z_recv,
    y_recv,
    f_send,
    f_recv,
    part_send,
    part_recv,
    k_send,
    k_recv,
    a_send,
    a_recv,
    hp_send,
    pass_hp,
    hp_recv,
    s_send,
    s_recv,
):
    lane = lax.axis_index("dp")
    layer = lax.axis_index("pipe")
    core = lax.rem(layer, 2)
    chip = layer // 2
    n_chip = n_pipe // 2
    is_top = chip == n_chip - 1
    width, rank = d_v.shape
    tokens = u_acc.shape[1]
    group = z_in.shape[1]
    half = group // 2
    queries = hc_ref.shape[1]
    every = group * n_dp
    share = rank // n_dp
    wide = width // CHUNKS
    piece = width // PIECES
    n_example = len_ref.shape[0]
    sibling = {"pipe": layer + 1 - 2 * core}
    above = {"pipe": lax.rem(2 * chip + 2, n_pipe)}

    def span(c):
        return slice(c * wide, (c + 1) * wide)

    def remote(src, dst, send_sem, recv_sem, device):
        return pltpu.make_async_remote_copy(
            src_ref=src,
            dst_ref=dst,
            send_sem=send_sem,
            recv_sem=recv_sem,
            device_id=device,
            device_id_type=MESH,
        )

    def landed(ref, sem):
        pltpu.make_async_copy(ref, ref, sem).wait()

    def load_expand(c):
        cols = pl.ds(c * wide, wide)
        return pltpu.make_async_copy(e_hbm.at[0, :, cols], e_v.at[:, cols], load_e.at[c])

    def load_down(c):
        rows = pl.ds(c * wide, wide)
        return pltpu.make_async_copy(d_hbm.at[0, rows, :], d_v.at[rows, :], load_d.at[c])

    def load_cotangent(k):
        cols = pl.ds(pl.multiple_of(k * piece, piece), piece)
        return pltpu.make_async_copy(cot_hbm.at[:, cols], cot_v.at[k], load_cot.at[k])

    def load_activation(k):
        cols = pl.ds(pl.multiple_of(k * piece, piece), piece)
        return pltpu.make_async_copy(x_hbm.at[0, :, cols], x_v.at[k], load_x.at[k])

    for c in range(CHUNKS):
        load_expand(c).start()
    for c in range(CHUNKS):
        load_down(c).start()
    for k in range(PIECES):
        load_cotangent(k).start()
    for k in range(PIECES):
        load_activation(k).start()

    barrier = pltpu.get_barrier_semaphore()
    for k in range(1, n_dp):
        pl.semaphore_signal(
            barrier, 1, device_id={"dp": lax.rem(lane + k, n_dp)}, device_id_type=MESH
        )
    for k in range(1, n_pipe):
        pl.semaphore_signal(
            barrier, 1, device_id={"pipe": lax.rem(layer + k, n_pipe)}, device_id_type=MESH
        )
    pl.semaphore_wait(barrier, n_dp + n_pipe - 2)

    v_rows = v_ref[0].astype(F32)
    rows_all[lane] = jnp.concatenate([v_rows, i_ref[0].astype(F32)], axis=0).astype(BF16)

    def lane_at(k):
        return {"dp": lax.rem(lane + k, n_dp)}

    def spread_rows():
        for k in range(1, n_dp):
            remote(
                rows_all.at[lane], rows_all.at[lane], rows_send, rows_recv, lane_at(k)
            ).start()

    @pl.when(core == 0)
    def _():
        spread_rows()

    row = lax.broadcasted_iota(jnp.int32, (group, queries), 0)
    col = lax.broadcasted_iota(jnp.int32, (group, queries), 1)
    pick = jnp.where((row >= half) & (lane * half + row - half == col), 1.0, 0.0).astype(BF16)
    ic_lane = jnp.dot(pick, ic_ref[0], preferred_element_type=F32).astype(BF16)
    v_wide = jnp.concatenate([v_rows, jnp.zeros_like(v_rows)], axis=0)

    def own_copy(c):
        return remote(
            sent.at[layer, :, span(c)],
            z_in.at[layer, :, span(c)],
            main_send.at[layer, c],
            z_recv.at[layer, c],
            sibling,
        )

    def up_copy(u, n, c):
        rows = pl.ds(u, n)
        return remote(
            sent.at[rows, :, span(c)],
            z_in.at[rows, :, span(c)],
            main_send.at[u, c],
            z_recv.at[u, c],
            above,
        )

    def over_copy(u, n, c):
        rows = pl.ds(u, n)
        return remote(
            sent.at[rows, :, span(c)],
            y_in.at[rows, :, span(c)],
            main_send.at[u, c],
            y_recv.at[u, c],
            sibling,
        )

    def pass_copy(u, n, c):
        rows = pl.ds(u, n)
        return remote(
            z_in.at[rows, :, span(c)],
            z_in.at[rows, :, span(c)],
            pass_send.at[u, c],
            z_recv.at[u, c],
            sibling,
        )

    def factor_copy(u, n):
        rows = pl.ds(u, n)
        return remote(a_all.at[lane, rows], f_in.at[rows], f_send.at[u], f_recv.at[u], sibling)

    def spread_factors(u, n):
        rows = pl.ds(u, n)
        for k in range(1, n_dp):
            remote(
                a_all.at[lane, rows], a_all.at[lane, rows], a_send.at[u], a_recv.at[u], lane_at(k)
            ).start()

    others = pl.ds(0, n_dp - 1)

    def part_copy(c):
        return remote(
            e_v.at[pl.ds(pl.multiple_of(lane * share, share), share), span(c)],
            k_part.at[:, span(c)],
            part_send.at[c],
            part_recv.at[c],
            sibling,
        )

    is_lower = core == 0
    is_upper = core == 1
    pairs_up = chip >= ALONE

    for c in range(CHUNKS):
        load_expand(c).wait()
        born = v_wide[:, span(c)] + jnp.dot(ic_lane, e_v[:, span(c)], preferred_element_type=F32)
        sent[layer, :, span(c)] = born.astype(BF16)

        @pl.when(is_lower)
        def _():
            own_copy(c).start()

        @pl.when(is_lower & (chip > 0))
        def _():
            part_copy(c).start()

        @pl.when(is_upper & jnp.logical_not(pairs_up))
        def _():
            up_copy(layer, 1, c).start()

    for c in range(CHUNKS):
        load_down(c).wait()

    def take(ref, u, n, c):
        return ref[pl.ds(u, n), :, span(c)].astype(F32).reshape(n * group, wide)

    def down(z, c):
        return jnp.dot(z.astype(BF16), d_v[span(c), :], preferred_element_type=F32)

    def up(factor, c):
        return jnp.dot(factor, e_v[:, span(c)], preferred_element_type=F32)

    def keep(u, n, projected):
        factor = ADAPTER_SCALE * projected
        a_all[lane, pl.ds(u, n)] = factor.reshape(n, group, rank).astype(BF16)
        return factor.astype(BF16)

    def put(u, n, c, moved):
        sent[pl.ds(u, n), :, span(c)] = moved.reshape(n, group, wide).astype(BF16)

    def lower_stage(u, n):
        projected = jnp.zeros((n * group, rank), F32)
        for c in range(CHUNKS):
            up_copy(u, n, c).wait_recv()
            pass_copy(u, n, c).start()
            projected += down(take(z_in, u, n, c), c)
        factor = keep(u, n, projected)
        factor_copy(u, n).start()

        @pl.when(jnp.logical_not(is_top))
        def _():
            for c in range(CHUNKS):
                put(u, n, c, take(z_in, u, n, c) + up(factor, c))
                over_copy(u, n, c).start()

        spread_factors(u, n)

    def upper_stage(u, n):
        projected = jnp.zeros((n * group, rank), F32)
        for c in range(CHUNKS):
            pass_copy(u, n, c).wait_recv()
            projected += down(take(z_in, u, n, c), c)
        factor_copy(u, n).wait_recv()
        below = f_in[pl.ds(u, n)].astype(F32).reshape(n * group, rank).astype(BF16)
        projected += jnp.dot(below, k_all[...].reshape(rank, rank), preferred_element_type=F32)
        factor = keep(u, n, projected)

        @pl.when(jnp.logical_not(is_top))
        def _():
            for c in range(CHUNKS):
                over_copy(u, n, c).wait_recv()
                put(u, n, c, take(y_in, u, n, c) + up(factor, c))
                up_copy(u, n, c).start()

        spread_factors(u, n)

    @pl.when(is_upper)
    def _():
        u = layer - 1
        projected = jnp.zeros((group, rank), F32)
        for c in range(CHUNKS):
            landed(z_in.at[u, :, span(c)], z_recv.at[u, c])
            projected += down(take(z_in, u, 1, c), c)
        factor = keep(u, 1, projected)

        @pl.when(jnp.logical_not(is_top))
        def _():
            for c in range(CHUNKS):
                put(u, 1, c, take(z_in, u, 1, c) + up(factor, c))

                @pl.when(pairs_up)
                def _():
                    up_copy(u, 2, c).start()

                @pl.when(jnp.logical_not(pairs_up))
                def _():
                    up_copy(u, 1, c).start()

        @pl.when(chip > 0)
        def _():
            coupled = jnp.zeros((share, rank), F32)
            for c in range(CHUNKS):
                landed(k_part.at[:, span(c)], part_recv.at[c])
                coupled += jnp.dot(k_part[:, span(c)], d_v[span(c), :], preferred_element_type=F32)
            k_all[lane] = coupled.astype(BF16)
            for k in range(1, n_dp):
                remote(k_all.at[lane], k_all.at[lane], k_send, k_recv, lane_at(k)).start()

        spread_factors(u, 1)
        spread_rows()

    def placed(first):
        row = lax.broadcasted_iota(jnp.int32, (every, queries), 0)
        col = lax.broadcasted_iota(jnp.int32, (every, queries), 1)
        within = lax.rem(row, group) - first
        query = (row // group) * half + within
        hit = (within >= 0) & (within < half) & (query == col)
        return jnp.where(hit, 1.0, 0.0).astype(BF16)

    hc_placed = jnp.dot(placed(0), hc_ref[0], preferred_element_type=F32).astype(BF16)
    ic_placed = jnp.dot(placed(half), ic_ref[0], preferred_element_type=F32).astype(BF16)
    def token_part(k):
        load_cotangent(k).wait()
        cols = pl.ds(pl.multiple_of(k * piece, piece), piece)
        u_acc[...] += nt(e_v[:, cols], cot_v[k])

    def row_part(k):
        load_activation(k).wait()
        cols = pl.ds(pl.multiple_of(k * piece, piece), piece)
        gathered = rows_all[:, :, cols].astype(F32).reshape(every, piece)
        of_value = lax.rem(lax.broadcasted_iota(jnp.int32, (every, piece), 0), group) < half
        value_side = jnp.where(of_value, gathered, 0.0).astype(BF16)
        own_acc[...] += nt(value_side, cot_v[k])
        hidden_side = nt(hc_placed, d_v[cols, :])
        input_side = (hidden_side + jnp.where(of_value, 0.0, gathered)).astype(BF16)
        hp_acc[...] += nt(input_side, x_v[k])

    def hp_copy(target):
        return remote(
            hp_all.at[layer],
            hp_all.at[layer],
            hp_send.at[target],
            hp_recv.at[layer],
            {"pipe": 2 * target + core},
        )

    def hp_pass(source):
        return remote(
            hp_all.at[source], hp_all.at[source], pass_hp.at[source], hp_recv.at[source], sibling
        )

    def settle():
        token = lax.broadcasted_iota(jnp.int32, (every, tokens), 1)
        count = jnp.zeros((every, tokens), jnp.int32)
        for e in range(n_example):
            count = jnp.where(token // SLOT == e, len_ref[e], count)
        live = jnp.where(lax.rem(token, SLOT) < count, 1.0, 0.0)
        hp_all[layer] = (hp_acc[...] * live).astype(BF16)
        for target in range(1, n_chip):

            @pl.when(chip < target)
            def _():
                hp_copy(target).start()

        @pl.when(is_lower)
        def _():
            hp_pass(layer).start()

        u_bf[...] = u_acc[...].astype(BF16)
        own = own_acc[...] + jnp.dot(ic_placed, u_bf[...], preferred_element_type=F32)
        total[...] = own * hp_all[layer].astype(F32)

    def add(source):
        factors = a_all[:, source].astype(F32).reshape(every, rank).astype(BF16)
        total[...] += jnp.dot(factors, u_bf[...], preferred_element_type=F32) * hp_all[
            source
        ].astype(F32)

    def collect(below):
        mine, other = 2 * below + core, 2 * below + 1 - core
        landed(hp_all.at[mine], hp_recv.at[mine])
        hp_pass(mine).start()
        landed(hp_all.at[other], hp_recv.at[other])

        @pl.when(below >= ALONE)
        def _():
            landed(a_all.at[others, pl.ds(2 * below, 2)], a_recv.at[2 * below])

        @pl.when(below < ALONE)
        def _():
            landed(a_all.at[others, pl.ds(2 * below + 1, 1)], a_recv.at[2 * below + 1])

        add(2 * below + 1)

        @pl.when(below < ALONE)
        def _():
            landed(a_all.at[others, pl.ds(2 * below, 1)], a_recv.at[2 * below])

        add(2 * below)

    u_acc[...] = jnp.zeros_like(u_acc)
    own_acc[...] = jnp.zeros_like(own_acc)
    hp_acc[...] = jnp.zeros_like(hp_acc)
    hc_placed = jnp.dot(placed(0), hc_ref[0], preferred_element_type=F32).astype(BF16)
    ic_placed = jnp.dot(placed(half), ic_ref[0], preferred_element_type=F32).astype(BF16)

    is_low = chip < LOW

    def token_end(step):
        late = jnp.where(step >= chip, PIECES, 0)
        return jnp.where(is_low, late, jnp.clip(4 + 2 * step, 0, PIECES))

    def row_end(step):
        late = jnp.where(step >= chip, PIECES, 0)
        return jnp.where(is_low, late, jnp.clip(2 * step - 2, 0, PIECES))

    def token_side(step, before_token, before_row):
        end_token, end_row = token_end(step), row_end(step)

        def token_step(k, carry):
            token_part(k)
            return carry

        def row_step(k, carry):
            row_part(k)
            return carry

        lax.fori_loop(before_token, end_token, token_step, 0)

        @pl.when((before_row == 0) & (end_row > 0))
        def _():
            landed(rows_all.at[others], rows_recv)

        lax.fori_loop(before_row, end_row, row_step, 0)

        @pl.when((before_row < PIECES) & (end_row == PIECES))
        def _():
            settle()

    def stage(u, n):
        @pl.when(is_lower)
        def _():
            lower_stage(u, n)

        @pl.when(is_upper)
        def _():
            upper_stage(u, n)

    def collect_down(first, last):
        def body(i, carry):
            collect(first - i)
            return carry

        lax.fori_loop(0, jnp.maximum(first - last + 1, 0), body, 0)

    early = 2

    def advance(step, carry):
        @pl.when((step >= 1) & (step <= chip))
        def _():
            below = jnp.maximum(chip - step, 0)

            @pl.when((step == 1) & is_upper)
            def _():
                landed(k_all.at[others], k_recv)

            @pl.when(below >= ALONE)
            def _():
                stage(2 * below, 2)

            @pl.when(below < ALONE)
            def _():
                def one(i, carry):
                    stage(2 * below + 1 - i, 1)
                    return carry

                lax.fori_loop(0, 2, one, 0)

        before_token = jnp.where(step == 0, 0, token_end(step - 1))
        before_row = jnp.where(step == 0, 0, row_end(step - 1))
        token_side(step, before_token, before_row)

        @pl.when((step == n_chip - 2) & is_top)
        def _():
            collect_down(n_chip - 2, early)

        return carry

    lax.fori_loop(0, n_chip, advance, 0)

    @pl.when(is_upper)
    def _():
        own = layer - 1
        landed(hp_all.at[own], hp_recv.at[own])
        landed(a_all.at[others, pl.ds(own, 1)], a_recv.at[own])
        add(own)

    collect_down(jnp.where(is_top, early - 1, chip - 1), 0)

    row = lax.broadcasted_iota(jnp.int32, (8, tokens), 0)
    token = lax.broadcasted_iota(jnp.int32, (8, tokens), 1)
    members = jnp.where(token // SLOT == row, 1.0, 0.0)
    sums = lax.dot_general(
        members,
        total[...],
        (((1,), (1,)), ((), ())),
        precision=lax.Precision.HIGHEST,
        preferred_element_type=F32,
    )
    row = lax.broadcasted_iota(jnp.int32, (every, 128), 0)
    col = lax.broadcasted_iota(jnp.int32, (every, 128), 1)
    joined = jnp.where((row // group) * half + lax.rem(row, half) == col, 1.0, 0.0)
    s_all[layer] = jnp.dot(
        sums, joined, precision=lax.Precision.HIGHEST, preferred_element_type=F32
    )

    def s_copy(k):
        return pltpu.make_async_remote_copy(
            src_ref=s_all.at[layer],
            dst_ref=s_all.at[layer],
            send_sem=s_send.at[k],
            recv_sem=s_recv,
            device_id={"pipe": lax.rem(layer + k, n_pipe)},
            device_id_type=MESH,
        )

    for k in range(1, n_pipe):
        s_copy(k).start()

    landed(rows_all.at[others], rows_send)

    def sent_unit(u, n):
        rows = pl.ds(u, n)
        landed(a_all.at[others, rows], a_send.at[u])

        @pl.when(is_lower)
        def _():
            factor_copy(u, n).wait_send()
            for c in range(CHUNKS):
                pass_copy(u, n, c).wait_send()

        @pl.when(jnp.logical_not(is_top))
        def _():
            for c in range(CHUNKS):
                up_copy(u, n, c).wait_send()

    def sent_pair(below, carry):
        sent_unit(2 * below, 2)
        return carry

    def sent_one(u, carry):
        sent_unit(u, 1)
        return carry

    lax.fori_loop(ALONE, jnp.maximum(chip, ALONE), sent_pair, 0)
    lax.fori_loop(0, jnp.minimum(2 * ALONE, 2 * chip), sent_one, 0)

    @pl.when(is_lower)
    def _():
        for c in range(CHUNKS):
            own_copy(c).wait_send()
        hp_pass(layer).wait_send()

    @pl.when(is_lower & (chip > 0))
    def _():
        for c in range(CHUNKS):
            part_copy(c).wait_send()

    @pl.when(is_upper)
    def _():
        landed(a_all.at[others, pl.ds(layer - 1, 1)], a_send.at[layer - 1])

        @pl.when(chip > 0)
        def _():
            landed(k_all.at[others], k_send)

        @pl.when(jnp.logical_not(is_top))
        def _():
            for c in range(CHUNKS):

                @pl.when(pairs_up)
                def _():
                    up_copy(layer - 1, 2, c).wait_send()

                @pl.when(jnp.logical_not(pairs_up))
                def _():
                    up_copy(layer - 1, 1, c).wait_send()
                    up_copy(layer, 1, c).wait_send()

    for target in range(1, n_chip):

        @pl.when(chip < target)
        def _():
            hp_copy(target).wait_send()

        @pl.when(chip >= target)
        def _():
            hp_pass(2 * (target - 1) + core).wait_send()

    for k in range(1, n_pipe):
        s_copy(k).wait_send()
    arrived = s_all.at[pl.ds(0, n_pipe - 1)]
    pltpu.make_async_copy(arrived, arrived, s_recv).wait()
    result = s_all[0]
    for source in range(1, n_pipe):
        result = result + s_all[source]
    result = result[:n_example, :queries] * (ADAPTER_SCALE * SLOT**-0.5)
    example = lane * n_example + lax.broadcasted_iota(jnp.int32, (n_example, queries), 0)
    out_ref[...] = result * jnp.where(example != qe_ref[...], 1.0, 0.0)


def solution(mesh):
    n_dp, n_pipe = mesh.shape["dp"], mesh.shape["pipe"]

    def local(act, cot, down, expand, value, inputs, hidden_cols, inner_cols, lengths, query):
        tokens, width = cot.shape
        rank = down.shape[2]
        queries = hidden_cols.shape[1]
        n_example = tokens // SLOT
        group = 2 * value.shape[1]
        every = group * n_dp
        hbm = pl.BlockSpec(memory_space=pl.ANY)
        vmem = pl.BlockSpec(memory_space=pltpu.VMEM)
        smem = pl.BlockSpec(memory_space=pltpu.SMEM)
        dma = pltpu.SemaphoreType.DMA
        return pl.pallas_call(
            functools.partial(kernel, n_dp, n_pipe),
            out_shape=jax.ShapeDtypeStruct((n_example, queries), F32),
            in_specs=[hbm, hbm, hbm, hbm, vmem, vmem, vmem, vmem, smem, vmem],
            out_specs=vmem,
            scratch_shapes=[
                pltpu.VMEM((PIECES, tokens, width // PIECES), BF16),
                pltpu.VMEM((PIECES, tokens, width // PIECES), BF16),
                pltpu.VMEM((width, rank), BF16),
                pltpu.VMEM((rank, width), BF16),
                pltpu.VMEM((n_pipe, group, width), BF16),
                pltpu.VMEM((n_pipe, group, width), BF16),
                pltpu.VMEM((n_pipe, group, width), BF16),
                pltpu.VMEM((n_dp, n_pipe, group, rank), BF16),
                pltpu.VMEM((n_pipe, group, rank), BF16),
                pltpu.VMEM((rank // n_dp, width), BF16),
                pltpu.VMEM((n_dp, rank // n_dp, rank), BF16),
                pltpu.VMEM((n_pipe, every, tokens), BF16),
                pltpu.VMEM((n_dp, group, width), BF16),
                pltpu.VMEM((rank, tokens), F32),
                pltpu.VMEM((rank, tokens), BF16),
                pltpu.VMEM((every, tokens), F32),
                pltpu.VMEM((every, tokens), F32),
                pltpu.VMEM((every, tokens), F32),
                pltpu.VMEM((n_pipe, 8, 128), F32),
                dma((CHUNKS,)),
                dma((CHUNKS,)),
                dma((PIECES,)),
                dma((PIECES,)),
                dma,
                dma,
                dma((n_pipe, CHUNKS)),
                dma((n_pipe, CHUNKS)),
                dma((n_pipe, CHUNKS)),
                dma((n_pipe, CHUNKS)),
                dma((n_pipe,)),
                dma((n_pipe,)),
                dma((CHUNKS,)),
                dma((CHUNKS,)),
                dma,
                dma,
                dma((n_pipe,)),
                dma((n_pipe,)),
                dma((n_pipe // 2,)),
                dma((n_pipe,)),
                dma((n_pipe,)),
                dma((n_pipe,)),
                dma,
            ],
            compiler_params=pltpu.CompilerParams(
                collective_id=0, has_side_effects=True, vmem_limit_bytes=58 << 20
            ),
            name="influence",
        )(
            act,
            cot,
            down,
            expand,
            value,
            inputs,
            hidden_cols,
            inner_cols,
            lengths,
            query.reshape(1, queries),
        )

    in_specs = (
        P("pipe", "dp", None),
        P("dp", None),
        P("pipe", None, None),
        P("pipe", None, None),
        P("pipe", "dp", None),
        P("pipe", "dp", None),
        P("pipe", None, None),
        P("pipe", None, None),
        P("dp"),
        P(),
    )
    return jax.shard_map(
        local, mesh=mesh, in_specs=in_specs, out_specs=P("dp", None), check_vma=False
    )
```

```python
import functools

import jax
import jax.numpy as jnp
from jax import lax
from jax.experimental import pallas as pl
from jax.experimental.pallas import tpu as pltpu
from jax.sharding import PartitionSpec as P

SLOT = 128
ADAPTER_SCALE = 0.25
MESH = pl.DeviceIdType.MESH
F32 = jnp.float32
BF16 = jnp.bfloat16
CHUNKS = 4
PIECES = 8
ALONE = 1
LOW = 3


def nt(a, b):
    return lax.dot_general(a, b, (((1,), (1,)), ((), ())), preferred_element_type=F32)


def kernel(
    n_dp,
    n_pipe,
    x_hbm,
    cot_hbm,
    d_hbm,
    e_hbm,
    v_hbm,
    i_hbm,
    hc_hbm,
    ic_hbm,
    len_hbm,
    qe_hbm,
    out_ref,
    v_ref,
    i_ref,
    hc_ref,
    ic_ref,
    len_ref,
    qe_ref,
    x_v,
    cot_v,
    d_v,
    e_v,
    z_in,
    y_in,
    sent,
    a_all,
    f_in,
    k_part,
    k_all,
    hp_all,
    rows_all,
    u_acc,
    u_bf,
    own_acc,
    hp_acc,
    total,
    s_all,
    load_small,
    load_e,
    load_d,
    load_cot,
    load_x,
    rows_send,
    rows_recv,
    main_send,
    pass_send,
    z_recv,
    y_recv,
    f_send,
    f_recv,
    part_send,
    part_recv,
    k_send,
    k_recv,
    a_send,
    a_recv,
    hp_send,
    pass_hp,
    hp_recv,
    s_send,
    s_recv,
    go_sem,
):
    lane = lax.axis_index("dp")
    layer = lax.axis_index("pipe")
    core = lax.rem(layer, 2)
    chip = layer // 2
    n_chip = n_pipe // 2
    is_top = chip == n_chip - 1
    width, rank = d_v.shape
    tokens = u_acc.shape[1]
    group = z_in.shape[1]
    half = group // 2
    queries = hc_ref.shape[1]
    every = group * n_dp
    share = rank // n_dp
    wide = width // CHUNKS
    piece = width // PIECES
    n_example = len_ref.shape[1]
    sibling = {"pipe": layer + 1 - 2 * core}
    above = {"pipe": lax.rem(2 * chip + 2, n_pipe)}

    def span(c):
        return slice(c * wide, (c + 1) * wide)

    def remote(src, dst, send_sem, recv_sem, device):
        return pltpu.make_async_remote_copy(
            src_ref=src,
            dst_ref=dst,
            send_sem=send_sem,
            recv_sem=recv_sem,
            device_id=device,
            device_id_type=MESH,
        )

    def landed(ref, sem):
        pltpu.make_async_copy(ref, ref, sem).wait()

    def load_expand(c):
        cols = pl.ds(c * wide, wide)
        return pltpu.make_async_copy(e_hbm.at[0, :, cols], e_v.at[:, cols], load_e.at[c])

    def load_down(c):
        rows = pl.ds(c * wide, wide)
        return pltpu.make_async_copy(d_hbm.at[0, rows, :], d_v.at[rows, :], load_d.at[c])

    def load_cotangent(k):
        cols = pl.ds(pl.multiple_of(k * piece, piece), piece)
        return pltpu.make_async_copy(cot_hbm.at[:, cols], cot_v.at[k], load_cot.at[k])

    def load_activation(k):
        cols = pl.ds(pl.multiple_of(k * piece, piece), piece)
        return pltpu.make_async_copy(x_hbm.at[0, :, cols], x_v.at[k], load_x.at[k])

    small = [
        pltpu.make_async_copy(src, dst, load_small.at[n])
        for n, (src, dst) in enumerate(
            (
                (ic_hbm, ic_ref),
                (v_hbm, v_ref),
                (i_hbm, i_ref),
                (hc_hbm, hc_ref),
                (len_hbm, len_ref),
                (qe_hbm, qe_ref),
            )
        )
    ]
    for copy in small:
        copy.start()
    for c in range(CHUNKS):
        load_expand(c).start()

    barrier = pltpu.get_barrier_semaphore()
    last = n_pipe - 1
    for k in range(1, n_dp):
        pl.semaphore_signal(
            barrier, 1, device_id={"dp": lax.rem(lane + k, n_dp)}, device_id_type=MESH
        )
    pl.semaphore_signal(barrier, 1, device_id=sibling, device_id_type=MESH)

    @pl.when((core == 0) & (chip > 0))
    def _():
        pl.semaphore_signal(
            barrier, 1, device_id={"pipe": jnp.maximum(layer - 1, 0)}, device_id_type=MESH
        )

    @pl.when(layer < last - 1)
    def _():
        pl.semaphore_signal(barrier, 1, device_id={"pipe": last}, device_id_type=MESH)

    waits_above = jnp.where((core == 1) & (layer < last), 1, 0)
    waits_column = jnp.where(layer == last, n_pipe - 2, 0)
    pl.semaphore_wait(barrier, n_dp + waits_above + waits_column)

    @pl.when(layer == last)
    def _():
        for target in range(last):
            pl.semaphore_signal(go_sem, 1, device_id={"pipe": target}, device_id_type=MESH)

    for copy in small:
        copy.wait()

    v_rows = v_ref[0].astype(F32)
    rows_all[lane] = jnp.concatenate([v_rows, i_ref[0].astype(F32)], axis=0).astype(BF16)

    def lane_at(k):
        return {"dp": lax.rem(lane + k, n_dp)}

    def spread_rows():
        for k in range(1, n_dp):
            remote(
                rows_all.at[lane], rows_all.at[lane], rows_send, rows_recv, lane_at(k)
            ).start()

    @pl.when(core == 0)
    def _():
        spread_rows()

    row = lax.broadcasted_iota(jnp.int32, (group, queries), 0)
    col = lax.broadcasted_iota(jnp.int32, (group, queries), 1)
    pick = jnp.where((row >= half) & (lane * half + row - half == col), 1.0, 0.0).astype(BF16)
    ic_lane = jnp.dot(pick, ic_ref[0], preferred_element_type=F32).astype(BF16)
    v_wide = jnp.concatenate([v_rows, jnp.zeros_like(v_rows)], axis=0)

    def own_copy(c):
        return remote(
            sent.at[layer, :, span(c)],
            z_in.at[layer, :, span(c)],
            main_send.at[layer, c],
            z_recv.at[layer, c],
            sibling,
        )

    def up_copy(u, n, c):
        rows = pl.ds(u, n)
        return remote(
            sent.at[rows, :, span(c)],
            z_in.at[rows, :, span(c)],
            main_send.at[u, c],
            z_recv.at[u, c],
            above,
        )

    def over_copy(u, n, c):
        rows = pl.ds(u, n)
        return remote(
            sent.at[rows, :, span(c)],
            y_in.at[rows, :, span(c)],
            main_send.at[u, c],
            y_recv.at[u, c],
            sibling,
        )

    def pass_copy(u, n, c):
        rows = pl.ds(u, n)
        return remote(
            z_in.at[rows, :, span(c)],
            z_in.at[rows, :, span(c)],
            pass_send.at[u, c],
            z_recv.at[u, c],
            sibling,
        )

    def factor_copy(u, n):
        rows = pl.ds(u, n)
        return remote(a_all.at[lane, rows], f_in.at[rows], f_send.at[u], f_recv.at[u], sibling)

    def spread_factors(u, n):
        rows = pl.ds(u, n)
        for k in range(1, n_dp):
            remote(
                a_all.at[lane, rows], a_all.at[lane, rows], a_send.at[u], a_recv.at[u], lane_at(k)
            ).start()

    others = pl.ds(0, n_dp - 1)

    def part_copy(c):
        return remote(
            e_v.at[pl.ds(pl.multiple_of(lane * share, share), share), span(c)],
            k_part.at[:, span(c)],
            part_send.at[c],
            part_recv.at[c],
            sibling,
        )

    is_lower = core == 0
    is_upper = core == 1
    pairs_up = chip >= ALONE

    for c in range(CHUNKS):
        load_expand(c).wait()
        load_down(c).start()
        born = v_wide[:, span(c)] + jnp.dot(ic_lane, e_v[:, span(c)], preferred_element_type=F32)
        sent[layer, :, span(c)] = born.astype(BF16)

        @pl.when(is_lower)
        def _():
            own_copy(c).start()

        @pl.when(is_lower & (chip > 0))
        def _():
            part_copy(c).start()

        @pl.when(is_upper & jnp.logical_not(pairs_up) & jnp.logical_not(is_top))
        def _():
            up_copy(layer, 1, c).start()

    for c in range(CHUNKS):
        load_down(c).wait()
    for k in range(PIECES):
        load_cotangent(k).start()
    for k in range(PIECES):
        load_activation(k).start()

    def take(ref, u, n, c):
        return ref[pl.ds(u, n), :, span(c)].astype(F32).reshape(n * group, wide)

    def down(z, c):
        return jnp.dot(z.astype(BF16), d_v[span(c), :], preferred_element_type=F32)

    def up(factor, c):
        return jnp.dot(factor, e_v[:, span(c)], preferred_element_type=F32)

    def keep(u, n, projected):
        factor = ADAPTER_SCALE * projected
        a_all[lane, pl.ds(u, n)] = factor.reshape(n, group, rank).astype(BF16)
        return factor.astype(BF16)

    def put(u, n, c, moved):
        sent[pl.ds(u, n), :, span(c)] = moved.reshape(n, group, wide).astype(BF16)

    def lower_stage(u, n):
        projected = jnp.zeros((n * group, rank), F32)
        for c in range(CHUNKS):
            up_copy(u, n, c).wait_recv()
            pass_copy(u, n, c).start()
            projected += down(take(z_in, u, n, c), c)
        factor = keep(u, n, projected)
        factor_copy(u, n).start()

        @pl.when(jnp.logical_not(is_top))
        def _():
            for c in range(CHUNKS):
                put(u, n, c, take(z_in, u, n, c) + up(factor, c))
                over_copy(u, n, c).start()

        spread_factors(u, n)

    def upper_stage(u, n):
        projected = jnp.zeros((n * group, rank), F32)
        for c in range(CHUNKS):
            pass_copy(u, n, c).wait_recv()
            projected += down(take(z_in, u, n, c), c)
        factor_copy(u, n).wait_recv()
        below = f_in[pl.ds(u, n)].astype(F32).reshape(n * group, rank).astype(BF16)
        projected += jnp.dot(below, k_all[...].reshape(rank, rank), preferred_element_type=F32)
        factor = keep(u, n, projected)

        @pl.when(jnp.logical_not(is_top))
        def _():
            for c in range(CHUNKS):
                over_copy(u, n, c).wait_recv()
                put(u, n, c, take(y_in, u, n, c) + up(factor, c))
                up_copy(u, n, c).start()

        spread_factors(u, n)

    @pl.when(is_upper)
    def _():
        u = layer - 1
        projected = jnp.zeros((group, rank), F32)
        for c in range(CHUNKS):
            landed(z_in.at[u, :, span(c)], z_recv.at[u, c])
            projected += down(take(z_in, u, 1, c), c)
        factor = keep(u, 1, projected)

        @pl.when(jnp.logical_not(is_top))
        def _():
            for c in range(CHUNKS):
                put(u, 1, c, take(z_in, u, 1, c) + up(factor, c))

                @pl.when(pairs_up)
                def _():
                    up_copy(u, 2, c).start()

                @pl.when(jnp.logical_not(pairs_up))
                def _():
                    up_copy(u, 1, c).start()

        @pl.when(chip > 0)
        def _():
            coupled = jnp.zeros((share, rank), F32)
            for c in range(CHUNKS):
                landed(k_part.at[:, span(c)], part_recv.at[c])
                coupled += jnp.dot(k_part[:, span(c)], d_v[span(c), :], preferred_element_type=F32)
            k_all[lane] = coupled.astype(BF16)
            for k in range(1, n_dp):
                remote(k_all.at[lane], k_all.at[lane], k_send, k_recv, lane_at(k)).start()

        spread_factors(u, 1)
        spread_rows()

    def placed(first):
        row = lax.broadcasted_iota(jnp.int32, (every, queries), 0)
        col = lax.broadcasted_iota(jnp.int32, (every, queries), 1)
        within = lax.rem(row, group) - first
        query = (row // group) * half + within
        hit = (within >= 0) & (within < half) & (query == col)
        return jnp.where(hit, 1.0, 0.0).astype(BF16)

    hc_placed = jnp.dot(placed(0), hc_ref[0], preferred_element_type=F32).astype(BF16)
    ic_placed = jnp.dot(placed(half), ic_ref[0], preferred_element_type=F32).astype(BF16)
    def token_part(k):
        load_cotangent(k).wait()
        cols = pl.ds(pl.multiple_of(k * piece, piece), piece)
        u_acc[...] += nt(e_v[:, cols], cot_v[k])

    def row_part(k):
        load_activation(k).wait()
        cols = pl.ds(pl.multiple_of(k * piece, piece), piece)
        gathered = rows_all[:, :, cols].astype(F32).reshape(every, piece)
        of_value = lax.rem(lax.broadcasted_iota(jnp.int32, (every, piece), 0), group) < half
        value_side = jnp.where(of_value, gathered, 0.0).astype(BF16)
        own_acc[...] += nt(value_side, cot_v[k])
        hidden_side = nt(hc_placed, d_v[cols, :])
        input_side = (hidden_side + jnp.where(of_value, 0.0, gathered)).astype(BF16)
        hp_acc[...] += nt(input_side, x_v[k])

    def hp_copy(target):
        return remote(
            hp_all.at[layer],
            hp_all.at[layer],
            hp_send.at[target],
            hp_recv.at[layer],
            {"pipe": 2 * target + core},
        )

    def hp_pass(source):
        return remote(
            hp_all.at[source], hp_all.at[source], pass_hp.at[source], hp_recv.at[source], sibling
        )

    def settle():
        token = lax.broadcasted_iota(jnp.int32, (every, tokens), 1)
        count = jnp.zeros((every, tokens), jnp.int32)
        for e in range(n_example):
            count = jnp.where(token // SLOT == e, len_ref[:, e : e + 1], count)
        live = jnp.where(lax.rem(token, SLOT) < count, 1.0, 0.0)
        hp_all[layer] = (hp_acc[...] * live).astype(BF16)

        @pl.when(layer < last)
        def _():
            pl.semaphore_wait(go_sem, 1)

        for target in range(1, n_chip):

            @pl.when(chip < target)
            def _():
                hp_copy(target).start()

        @pl.when(is_lower)
        def _():
            hp_pass(layer).start()

        u_bf[...] = u_acc[...].astype(BF16)
        own = own_acc[...] + jnp.dot(ic_placed, u_bf[...], preferred_element_type=F32)
        total[...] = own * hp_all[layer].astype(F32)

    def add(source):
        factors = a_all[:, source].astype(F32).reshape(every, rank).astype(BF16)
        total[...] += jnp.dot(factors, u_bf[...], preferred_element_type=F32) * hp_all[
            source
        ].astype(F32)

    def collect(below):
        mine, other = 2 * below + core, 2 * below + 1 - core
        landed(hp_all.at[mine], hp_recv.at[mine])
        hp_pass(mine).start()
        landed(hp_all.at[other], hp_recv.at[other])

        @pl.when(below >= ALONE)
        def _():
            landed(a_all.at[others, pl.ds(2 * below, 2)], a_recv.at[2 * below])

        @pl.when(below < ALONE)
        def _():
            landed(a_all.at[others, pl.ds(2 * below + 1, 1)], a_recv.at[2 * below + 1])

        add(2 * below + 1)

        @pl.when(below < ALONE)
        def _():
            landed(a_all.at[others, pl.ds(2 * below, 1)], a_recv.at[2 * below])

        add(2 * below)

    u_acc[...] = jnp.zeros_like(u_acc)
    own_acc[...] = jnp.zeros_like(own_acc)
    hp_acc[...] = jnp.zeros_like(hp_acc)
    hc_placed = jnp.dot(placed(0), hc_ref[0], preferred_element_type=F32).astype(BF16)
    ic_placed = jnp.dot(placed(half), ic_ref[0], preferred_element_type=F32).astype(BF16)

    is_low = chip < LOW

    def token_end(step):
        late = jnp.where(step >= chip, PIECES, 0)
        return jnp.where(is_low, late, jnp.clip(4 + 2 * step, 0, PIECES))

    def row_end(step):
        late = jnp.where(step >= chip, PIECES, 0)
        return jnp.where(is_low, late, jnp.clip(2 * step - 2, 0, PIECES))

    def token_side(step, before_token, before_row):
        end_token, end_row = token_end(step), row_end(step)

        def token_step(k, carry):
            token_part(k)
            return carry

        def row_step(k, carry):
            row_part(k)
            return carry

        lax.fori_loop(before_token, end_token, token_step, 0)

        @pl.when((before_row == 0) & (end_row > 0))
        def _():
            landed(rows_all.at[others], rows_recv)

        lax.fori_loop(before_row, end_row, row_step, 0)

        @pl.when((before_row < PIECES) & (end_row == PIECES))
        def _():
            settle()

    def stage(u, n):
        @pl.when(is_lower)
        def _():
            lower_stage(u, n)

        @pl.when(is_upper)
        def _():
            upper_stage(u, n)

    def collect_down(first, last):
        def body(i, carry):
            collect(first - i)
            return carry

        lax.fori_loop(0, jnp.maximum(first - last + 1, 0), body, 0)

    early = 2

    def advance(step, carry):
        @pl.when((step >= 1) & (step <= chip))
        def _():
            below = jnp.maximum(chip - step, 0)

            @pl.when((step == 1) & is_upper)
            def _():
                landed(k_all.at[others], k_recv)

            @pl.when(below >= ALONE)
            def _():
                stage(2 * below, 2)

            @pl.when(below < ALONE)
            def _():
                def one(i, carry):
                    stage(2 * below + 1 - i, 1)
                    return carry

                lax.fori_loop(0, 2, one, 0)

        before_token = jnp.where(step == 0, 0, token_end(step - 1))
        before_row = jnp.where(step == 0, 0, row_end(step - 1))
        token_side(step, before_token, before_row)

        @pl.when((step == n_chip - 2) & is_top)
        def _():
            collect_down(n_chip - 2, early)

        return carry

    lax.fori_loop(0, n_chip, advance, 0)

    @pl.when(is_upper)
    def _():
        own = layer - 1
        landed(hp_all.at[own], hp_recv.at[own])
        landed(a_all.at[others, pl.ds(own, 1)], a_recv.at[own])
        add(own)

    collect_down(jnp.where(is_top, early - 1, chip - 1), 0)

    row = lax.broadcasted_iota(jnp.int32, (8, tokens), 0)
    token = lax.broadcasted_iota(jnp.int32, (8, tokens), 1)
    members = jnp.where(token // SLOT == row, 1.0, 0.0)
    sums = lax.dot_general(
        members,
        total[...],
        (((1,), (1,)), ((), ())),
        precision=lax.Precision.HIGHEST,
        preferred_element_type=F32,
    )
    row = lax.broadcasted_iota(jnp.int32, (every, 128), 0)
    col = lax.broadcasted_iota(jnp.int32, (every, 128), 1)
    joined = jnp.where((row // group) * half + lax.rem(row, half) == col, 1.0, 0.0)
    s_all[layer] = jnp.dot(
        sums, joined, precision=lax.Precision.HIGHEST, preferred_element_type=F32
    )

    def s_copy(k):
        return pltpu.make_async_remote_copy(
            src_ref=s_all.at[layer],
            dst_ref=s_all.at[layer],
            send_sem=s_send.at[k],
            recv_sem=s_recv,
            device_id={"pipe": lax.rem(layer + k, n_pipe)},
            device_id_type=MESH,
        )

    for k in range(1, n_pipe):
        s_copy(k).start()

    landed(rows_all.at[others], rows_send)

    def sent_unit(u, n):
        rows = pl.ds(u, n)
        landed(a_all.at[others, rows], a_send.at[u])

        @pl.when(is_lower)
        def _():
            factor_copy(u, n).wait_send()
            for c in range(CHUNKS):
                pass_copy(u, n, c).wait_send()

        @pl.when(jnp.logical_not(is_top))
        def _():
            for c in range(CHUNKS):
                up_copy(u, n, c).wait_send()

    def sent_pair(below, carry):
        sent_unit(2 * below, 2)
        return carry

    def sent_one(u, carry):
        sent_unit(u, 1)
        return carry

    lax.fori_loop(ALONE, jnp.maximum(chip, ALONE), sent_pair, 0)
    lax.fori_loop(0, jnp.minimum(2 * ALONE, 2 * chip), sent_one, 0)

    @pl.when(is_lower)
    def _():
        for c in range(CHUNKS):
            own_copy(c).wait_send()
        hp_pass(layer).wait_send()

    @pl.when(is_lower & (chip > 0))
    def _():
        for c in range(CHUNKS):
            part_copy(c).wait_send()

    @pl.when(is_upper)
    def _():
        landed(a_all.at[others, pl.ds(layer - 1, 1)], a_send.at[layer - 1])

        @pl.when(chip > 0)
        def _():
            landed(k_all.at[others], k_send)

        @pl.when(jnp.logical_not(is_top))
        def _():
            for c in range(CHUNKS):

                @pl.when(pairs_up)
                def _():
                    up_copy(layer - 1, 2, c).wait_send()

                @pl.when(jnp.logical_not(pairs_up))
                def _():
                    up_copy(layer - 1, 1, c).wait_send()
                    up_copy(layer, 1, c).wait_send()

    for target in range(1, n_chip):

        @pl.when(chip < target)
        def _():
            hp_copy(target).wait_send()

        @pl.when(chip >= target)
        def _():
            hp_pass(2 * (target - 1) + core).wait_send()

    for k in range(1, n_pipe):
        s_copy(k).wait_send()
    arrived = s_all.at[pl.ds(0, n_pipe - 1)]
    pltpu.make_async_copy(arrived, arrived, s_recv).wait()
    result = s_all[0]
    for source in range(1, n_pipe):
        result = result + s_all[source]
    result = result[:n_example, :queries] * (ADAPTER_SCALE * SLOT**-0.5)
    example = lane * n_example + lax.broadcasted_iota(jnp.int32, (n_example, queries), 0)
    out_ref[...] = result * jnp.where(example != qe_ref[...], 1.0, 0.0)


def solution(mesh):
    n_dp, n_pipe = mesh.shape["dp"], mesh.shape["pipe"]

    def local(act, cot, down, expand, value, inputs, hidden_cols, inner_cols, lengths, query):
        tokens, width = cot.shape
        rank = down.shape[2]
        queries = hidden_cols.shape[1]
        n_example = tokens // SLOT
        group = 2 * value.shape[1]
        every = group * n_dp
        hbm = pl.BlockSpec(memory_space=pl.ANY)
        vmem = pl.BlockSpec(memory_space=pltpu.VMEM)
        dma = pltpu.SemaphoreType.DMA
        return pl.pallas_call(
            functools.partial(kernel, n_dp, n_pipe),
            out_shape=jax.ShapeDtypeStruct((n_example, queries), F32),
            in_specs=[hbm] * 10,
            out_specs=vmem,
            scratch_shapes=[
                pltpu.VMEM(value.shape, BF16),
                pltpu.VMEM(inputs.shape, BF16),
                pltpu.VMEM(hidden_cols.shape, BF16),
                pltpu.VMEM(inner_cols.shape, BF16),
                pltpu.VMEM((1, n_example), jnp.int32),
                pltpu.VMEM((1, queries), jnp.int32),
                pltpu.VMEM((PIECES, tokens, width // PIECES), BF16),
                pltpu.VMEM((PIECES, tokens, width // PIECES), BF16),
                pltpu.VMEM((width, rank), BF16),
                pltpu.VMEM((rank, width), BF16),
                pltpu.VMEM((n_pipe, group, width), BF16),
                pltpu.VMEM((n_pipe, group, width), BF16),
                pltpu.VMEM((n_pipe, group, width), BF16),
                pltpu.VMEM((n_dp, n_pipe, group, rank), BF16),
                pltpu.VMEM((n_pipe, group, rank), BF16),
                pltpu.VMEM((rank // n_dp, width), BF16),
                pltpu.VMEM((n_dp, rank // n_dp, rank), BF16),
                pltpu.VMEM((n_pipe, every, tokens), BF16),
                pltpu.VMEM((n_dp, group, width), BF16),
                pltpu.VMEM((rank, tokens), F32),
                pltpu.VMEM((rank, tokens), BF16),
                pltpu.VMEM((every, tokens), F32),
                pltpu.VMEM((every, tokens), F32),
                pltpu.VMEM((every, tokens), F32),
                pltpu.VMEM((n_pipe, 8, 128), F32),
                dma((6,)),
                dma((CHUNKS,)),
                dma((CHUNKS,)),
                dma((PIECES,)),
                dma((PIECES,)),
                dma,
                dma,
                dma((n_pipe, CHUNKS)),
                dma((n_pipe, CHUNKS)),
                dma((n_pipe, CHUNKS)),
                dma((n_pipe, CHUNKS)),
                dma((n_pipe,)),
                dma((n_pipe,)),
                dma((CHUNKS,)),
                dma((CHUNKS,)),
                dma,
                dma,
                dma((n_pipe,)),
                dma((n_pipe,)),
                dma((n_pipe // 2,)),
                dma((n_pipe,)),
                dma((n_pipe,)),
                dma((n_pipe,)),
                dma,
                pltpu.SemaphoreType.REGULAR,
            ],
            compiler_params=pltpu.CompilerParams(
                collective_id=0, has_side_effects=True, vmem_limit_bytes=58 << 20
            ),
            name="influence",
        )(
            act,
            cot,
            down,
            expand,
            value,
            inputs,
            hidden_cols,
            inner_cols,
            lengths.reshape(1, n_example),
            query.reshape(1, queries),
        )

    in_specs = (
        P("pipe", "dp", None),
        P("dp", None),
        P("pipe", None, None),
        P("pipe", None, None),
        P("pipe", "dp", None),
        P("pipe", "dp", None),
        P("pipe", None, None),
        P("pipe", None, None),
        P("dp"),
        P(),
    )
    return jax.shard_map(
        local, mesh=mesh, in_specs=in_specs, out_specs=P("dp", None), check_vma=False
    )
```

```python
import functools

import jax
import jax.numpy as jnp
from jax import lax
from jax.experimental import pallas as pl
from jax.experimental.pallas import tpu as pltpu
from jax.sharding import PartitionSpec as P

SLOT = 128
ADAPTER_SCALE = 0.25
MESH = pl.DeviceIdType.MESH
F32 = jnp.float32
BF16 = jnp.bfloat16
CHUNKS = 4
PIECES = 8
ALONE = 1
AHEAD = 3
LOW = 3


def nt(a, b):
    return lax.dot_general(a, b, (((1,), (1,)), ((), ())), preferred_element_type=F32)


def kernel(
    n_dp,
    n_pipe,
    x_hbm,
    cot_hbm,
    d_hbm,
    e_hbm,
    v_hbm,
    i_hbm,
    hc_hbm,
    ic_hbm,
    len_hbm,
    qe_hbm,
    out_ref,
    v_ref,
    i_ref,
    hc_ref,
    ic_ref,
    len_ref,
    qe_ref,
    x_v,
    cot_v,
    d_v,
    e_v,
    z_in,
    y_in,
    sent,
    a_all,
    f_in,
    k_part,
    k_all,
    hp_all,
    rows_all,
    u_acc,
    u_bf,
    own_acc,
    hp_acc,
    total,
    s_all,
    load_small,
    load_e,
    load_d,
    load_cot,
    load_x,
    rows_send,
    rows_recv,
    main_send,
    pass_send,
    z_recv,
    y_recv,
    f_send,
    f_recv,
    part_send,
    part_recv,
    k_send,
    k_recv,
    a_send,
    a_recv,
    hp_send,
    pass_hp,
    hp_recv,
    s_send,
    s_recv,
    go_sem,
):
    lane = lax.axis_index("dp")
    layer = lax.axis_index("pipe")
    core = lax.rem(layer, 2)
    chip = layer // 2
    n_chip = n_pipe // 2
    is_top = chip == n_chip - 1
    width, rank = d_v.shape
    tokens = u_acc.shape[1]
    group = z_in.shape[1]
    half = group // 2
    queries = hc_ref.shape[1]
    every = group * n_dp
    share = rank // n_dp
    wide = width // CHUNKS
    piece = width // PIECES
    n_example = len_ref.shape[1]
    sibling = {"pipe": layer + 1 - 2 * core}
    above = {"pipe": lax.rem(2 * chip + 2, n_pipe)}

    def span(c):
        return slice(c * wide, (c + 1) * wide)

    def remote(src, dst, send_sem, recv_sem, device):
        return pltpu.make_async_remote_copy(
            src_ref=src,
            dst_ref=dst,
            send_sem=send_sem,
            recv_sem=recv_sem,
            device_id=device,
            device_id_type=MESH,
        )

    def landed(ref, sem):
        pltpu.make_async_copy(ref, ref, sem).wait()

    def load_expand(c):
        cols = pl.ds(c * wide, wide)
        return pltpu.make_async_copy(e_hbm.at[0, :, cols], e_v.at[:, cols], load_e.at[c])

    def load_down(c):
        rows = pl.ds(c * wide, wide)
        return pltpu.make_async_copy(d_hbm.at[0, rows, :], d_v.at[rows, :], load_d.at[c])

    def load_cotangent(k):
        cols = pl.ds(pl.multiple_of(k * piece, piece), piece)
        return pltpu.make_async_copy(cot_hbm.at[:, cols], cot_v.at[k], load_cot.at[k])

    def load_activation(k):
        cols = pl.ds(pl.multiple_of(k * piece, piece), piece)
        return pltpu.make_async_copy(x_hbm.at[0, :, cols], x_v.at[k], load_x.at[k])

    small = [
        pltpu.make_async_copy(src, dst, load_small.at[n])
        for n, (src, dst) in enumerate(
            (
                (ic_hbm, ic_ref),
                (v_hbm, v_ref),
                (i_hbm, i_ref),
                (hc_hbm, hc_ref),
                (len_hbm, len_ref),
                (qe_hbm, qe_ref),
            )
        )
    ]
    for copy in small:
        copy.start()
    for c in range(CHUNKS):
        load_expand(c).start()

    barrier = pltpu.get_barrier_semaphore()
    last = n_pipe - 1
    for k in range(1, n_dp):
        pl.semaphore_signal(
            barrier, 1, device_id={"dp": lax.rem(lane + k, n_dp)}, device_id_type=MESH
        )
    pl.semaphore_signal(barrier, 1, device_id=sibling, device_id_type=MESH)

    @pl.when((core == 0) & (chip > 0))
    def _():
        pl.semaphore_signal(
            barrier, 1, device_id={"pipe": jnp.maximum(layer - 1, 0)}, device_id_type=MESH
        )

    @pl.when(layer < last - 1)
    def _():
        pl.semaphore_signal(barrier, 1, device_id={"pipe": last}, device_id_type=MESH)

    waits_above = jnp.where((core == 1) & (layer < last), 1, 0)
    waits_column = jnp.where(layer == last, n_pipe - 2, 0)
    pl.semaphore_wait(barrier, n_dp + waits_above + waits_column)

    @pl.when(layer == last)
    def _():
        for target in range(last):
            pl.semaphore_signal(go_sem, 1, device_id={"pipe": target}, device_id_type=MESH)

    for copy in small:
        copy.wait()

    v_rows = v_ref[0].astype(F32)
    rows_all[lane] = jnp.concatenate([v_rows, i_ref[0].astype(F32)], axis=0).astype(BF16)

    def lane_at(k):
        return {"dp": lax.rem(lane + k, n_dp)}

    def spread_rows():
        for k in range(1, n_dp):
            remote(
                rows_all.at[lane], rows_all.at[lane], rows_send, rows_recv, lane_at(k)
            ).start()

    is_low = chip < LOW

    @pl.when((core == 0) & jnp.logical_not(is_low))
    def _():
        spread_rows()

    row = lax.broadcasted_iota(jnp.int32, (group, queries), 0)
    col = lax.broadcasted_iota(jnp.int32, (group, queries), 1)
    pick = jnp.where((row >= half) & (lane * half + row - half == col), 1.0, 0.0).astype(BF16)
    ic_lane = jnp.dot(pick, ic_ref[0], preferred_element_type=F32).astype(BF16)
    v_wide = jnp.concatenate([v_rows, jnp.zeros_like(v_rows)], axis=0)

    def own_copy(c):
        return remote(
            sent.at[layer, :, span(c)],
            z_in.at[layer, :, span(c)],
            main_send.at[layer, c],
            z_recv.at[layer, c],
            sibling,
        )

    def up_copy(u, n, c):
        rows = pl.ds(u, n)
        return remote(
            sent.at[rows, :, span(c)],
            z_in.at[rows, :, span(c)],
            main_send.at[u, c],
            z_recv.at[u, c],
            above,
        )

    def over_copy(u, n, c):
        rows = pl.ds(u, n)
        return remote(
            sent.at[rows, :, span(c)],
            y_in.at[rows, :, span(c)],
            main_send.at[u, c],
            y_recv.at[u, c],
            sibling,
        )

    def pass_copy(u, n, c):
        rows = pl.ds(u, n)
        return remote(
            z_in.at[rows, :, span(c)],
            z_in.at[rows, :, span(c)],
            pass_send.at[u, c],
            z_recv.at[u, c],
            sibling,
        )

    def factor_copy(u, n):
        rows = pl.ds(u, n)
        return remote(a_all.at[lane, rows], f_in.at[rows], f_send.at[u], f_recv.at[u], sibling)

    def spread_factors(u, n):
        rows = pl.ds(u, n)
        for k in range(1, n_dp):
            remote(
                a_all.at[lane, rows], a_all.at[lane, rows], a_send.at[u], a_recv.at[u], lane_at(k)
            ).start()

    others = pl.ds(0, n_dp - 1)

    def part_copy(c):
        return remote(
            e_v.at[pl.ds(pl.multiple_of(lane * share, share), share), span(c)],
            k_part.at[:, span(c)],
            part_send.at[c],
            part_recv.at[c],
            sibling,
        )

    is_lower = core == 0
    is_upper = core == 1
    pairs_up = chip >= ALONE

    for c in range(CHUNKS):
        load_expand(c).wait()
        load_down(c).start()
        born = v_wide[:, span(c)] + jnp.dot(ic_lane, e_v[:, span(c)], preferred_element_type=F32)
        sent[layer, :, span(c)] = born.astype(BF16)

        @pl.when(is_lower)
        def _():
            own_copy(c).start()

        @pl.when(is_lower & (chip > 0))
        def _():
            part_copy(c).start()

        @pl.when(is_upper & jnp.logical_not(pairs_up) & jnp.logical_not(is_top))
        def _():
            up_copy(layer, 1, c).start()

    for c in range(CHUNKS):
        load_down(c).wait()

    def first_loads():
        for k in range(AHEAD):
            load_cotangent(k).start()
        for k in range(AHEAD):
            load_activation(k).start()

    @pl.when(jnp.logical_not(is_low))
    def _():
        first_loads()

    def take(ref, u, n, c):
        return ref[pl.ds(u, n), :, span(c)].astype(F32).reshape(n * group, wide)

    def down(z, c):
        return jnp.dot(z.astype(BF16), d_v[span(c), :], preferred_element_type=F32)

    def up(factor, c):
        return jnp.dot(factor, e_v[:, span(c)], preferred_element_type=F32)

    def keep(u, n, projected):
        factor = ADAPTER_SCALE * projected
        a_all[lane, pl.ds(u, n)] = factor.reshape(n, group, rank).astype(BF16)
        return factor.astype(BF16)

    def put(u, n, c, moved):
        sent[pl.ds(u, n), :, span(c)] = moved.reshape(n, group, wide).astype(BF16)

    def lower_stage(u, n):
        projected = jnp.zeros((n * group, rank), F32)
        for c in range(CHUNKS):
            up_copy(u, n, c).wait_recv()
            pass_copy(u, n, c).start()
            projected += down(take(z_in, u, n, c), c)
        factor = keep(u, n, projected)
        factor_copy(u, n).start()

        @pl.when(jnp.logical_not(is_top))
        def _():
            for c in range(CHUNKS):
                put(u, n, c, take(z_in, u, n, c) + up(factor, c))
                over_copy(u, n, c).start()

        spread_factors(u, n)

    def upper_stage(u, n):
        projected = jnp.zeros((n * group, rank), F32)
        for c in range(CHUNKS):
            pass_copy(u, n, c).wait_recv()
            projected += down(take(z_in, u, n, c), c)
        factor_copy(u, n).wait_recv()
        below = f_in[pl.ds(u, n)].astype(F32).reshape(n * group, rank).astype(BF16)
        projected += jnp.dot(below, k_all[...].reshape(rank, rank), preferred_element_type=F32)
        factor = keep(u, n, projected)

        @pl.when(jnp.logical_not(is_top))
        def _():
            for c in range(CHUNKS):
                over_copy(u, n, c).wait_recv()
                put(u, n, c, take(y_in, u, n, c) + up(factor, c))
                up_copy(u, n, c).start()

        spread_factors(u, n)

    @pl.when(is_upper)
    def _():
        u = layer - 1
        projected = jnp.zeros((group, rank), F32)
        for c in range(CHUNKS):
            landed(z_in.at[u, :, span(c)], z_recv.at[u, c])
            projected += down(take(z_in, u, 1, c), c)
        factor = keep(u, 1, projected)

        @pl.when(jnp.logical_not(is_top))
        def _():
            for c in range(CHUNKS):
                put(u, 1, c, take(z_in, u, 1, c) + up(factor, c))

                @pl.when(pairs_up)
                def _():
                    up_copy(u, 2, c).start()

                @pl.when(jnp.logical_not(pairs_up))
                def _():
                    up_copy(u, 1, c).start()

        @pl.when(chip > 0)
        def _():
            coupled = jnp.zeros((share, rank), F32)
            for c in range(CHUNKS):
                landed(k_part.at[:, span(c)], part_recv.at[c])
                coupled += jnp.dot(k_part[:, span(c)], d_v[span(c), :], preferred_element_type=F32)
            k_all[lane] = coupled.astype(BF16)
            for k in range(1, n_dp):
                remote(k_all.at[lane], k_all.at[lane], k_send, k_recv, lane_at(k)).start()

        spread_factors(u, 1)

        @pl.when(jnp.logical_not(is_low))
        def _():
            spread_rows()

    def placed(first):
        row = lax.broadcasted_iota(jnp.int32, (every, queries), 0)
        col = lax.broadcasted_iota(jnp.int32, (every, queries), 1)
        within = lax.rem(row, group) - first
        query = (row // group) * half + within
        hit = (within >= 0) & (within < half) & (query == col)
        return jnp.where(hit, 1.0, 0.0).astype(BF16)

    hc_placed = jnp.dot(placed(0), hc_ref[0], preferred_element_type=F32).astype(BF16)
    ic_placed = jnp.dot(placed(half), ic_ref[0], preferred_element_type=F32).astype(BF16)
    def token_part(k):
        load_cotangent(k).wait()

        @pl.when(k + AHEAD < PIECES)
        def _():
            load_cotangent(jnp.minimum(k + AHEAD, PIECES - 1)).start()

        cols = pl.ds(pl.multiple_of(k * piece, piece), piece)
        u_acc[...] += nt(e_v[:, cols], cot_v[k])

    def row_part(k):
        load_activation(k).wait()

        @pl.when(k + AHEAD < PIECES)
        def _():
            load_activation(jnp.minimum(k + AHEAD, PIECES - 1)).start()

        cols = pl.ds(pl.multiple_of(k * piece, piece), piece)
        gathered = rows_all[:, :, cols].astype(F32).reshape(every, piece)
        of_value = lax.rem(lax.broadcasted_iota(jnp.int32, (every, piece), 0), group) < half
        value_side = jnp.where(of_value, gathered, 0.0).astype(BF16)
        own_acc[...] += nt(value_side, cot_v[k])
        hidden_side = nt(hc_placed, d_v[cols, :])
        input_side = (hidden_side + jnp.where(of_value, 0.0, gathered)).astype(BF16)
        hp_acc[...] += nt(input_side, x_v[k])

    def hp_copy(target):
        return remote(
            hp_all.at[layer],
            hp_all.at[layer],
            hp_send.at[target],
            hp_recv.at[layer],
            {"pipe": 2 * target + core},
        )

    def hp_pass(source):
        return remote(
            hp_all.at[source], hp_all.at[source], pass_hp.at[source], hp_recv.at[source], sibling
        )

    def settle():
        token = lax.broadcasted_iota(jnp.int32, (every, tokens), 1)
        count = jnp.zeros((every, tokens), jnp.int32)
        for e in range(n_example):
            count = jnp.where(token // SLOT == e, len_ref[:, e : e + 1], count)
        live = jnp.where(lax.rem(token, SLOT) < count, 1.0, 0.0)
        hp_all[layer] = (hp_acc[...] * live).astype(BF16)

        @pl.when(layer < last)
        def _():
            pl.semaphore_wait(go_sem, 1)

        for target in range(1, n_chip):

            @pl.when(chip < target)
            def _():
                hp_copy(target).start()

        @pl.when(is_lower)
        def _():
            hp_pass(layer).start()

        u_bf[...] = u_acc[...].astype(BF16)
        own = own_acc[...] + jnp.dot(ic_placed, u_bf[...], preferred_element_type=F32)
        total[...] = own * hp_all[layer].astype(F32)

    def add(source):
        factors = a_all[:, source].astype(F32).reshape(every, rank).astype(BF16)
        total[...] += jnp.dot(factors, u_bf[...], preferred_element_type=F32) * hp_all[
            source
        ].astype(F32)

    def collect(below):
        mine, other = 2 * below + core, 2 * below + 1 - core
        landed(hp_all.at[mine], hp_recv.at[mine])
        hp_pass(mine).start()
        landed(hp_all.at[other], hp_recv.at[other])

        @pl.when(below >= ALONE)
        def _():
            landed(a_all.at[others, pl.ds(2 * below, 2)], a_recv.at[2 * below])

        @pl.when(below < ALONE)
        def _():
            landed(a_all.at[others, pl.ds(2 * below + 1, 1)], a_recv.at[2 * below + 1])

        add(2 * below + 1)

        @pl.when(below < ALONE)
        def _():
            landed(a_all.at[others, pl.ds(2 * below, 1)], a_recv.at[2 * below])

        add(2 * below)

    u_acc[...] = jnp.zeros_like(u_acc)
    own_acc[...] = jnp.zeros_like(own_acc)
    hp_acc[...] = jnp.zeros_like(hp_acc)
    hc_placed = jnp.dot(placed(0), hc_ref[0], preferred_element_type=F32).astype(BF16)
    ic_placed = jnp.dot(placed(half), ic_ref[0], preferred_element_type=F32).astype(BF16)

    def token_end(step):
        late = jnp.where(step >= chip, PIECES, 0)
        return jnp.where(is_low, late, jnp.clip(4 + 2 * step, 0, PIECES))

    def row_end(step):
        late = jnp.where(step >= chip, PIECES, 0)
        return jnp.where(is_low, late, jnp.clip(2 * step - 2, 0, PIECES))

    def token_side(step, before_token, before_row):
        end_token, end_row = token_end(step), row_end(step)

        @pl.when(is_low & (before_token == 0) & (end_token > 0))
        def _():
            first_loads()
            spread_rows()

        def token_step(k, carry):
            token_part(k)
            return carry

        def row_step(k, carry):
            row_part(k)
            return carry

        lax.fori_loop(before_token, end_token, token_step, 0)

        @pl.when((before_row == 0) & (end_row > 0))
        def _():
            landed(rows_all.at[others], rows_recv)

        lax.fori_loop(before_row, end_row, row_step, 0)

        @pl.when((before_row < PIECES) & (end_row == PIECES))
        def _():
            settle()

    def stage(u, n):
        @pl.when(is_lower)
        def _():
            lower_stage(u, n)

        @pl.when(is_upper)
        def _():
            upper_stage(u, n)

    def collect_down(first, last):
        def body(i, carry):
            collect(first - i)
            return carry

        lax.fori_loop(0, jnp.maximum(first - last + 1, 0), body, 0)

    early = 2

    def advance(step, carry):
        @pl.when((step >= 1) & (step <= chip))
        def _():
            below = jnp.maximum(chip - step, 0)

            @pl.when((step == 1) & is_upper)
            def _():
                landed(k_all.at[others], k_recv)

            @pl.when(below >= ALONE)
            def _():
                stage(2 * below, 2)

            @pl.when(below < ALONE)
            def _():
                def one(i, carry):
                    stage(2 * below + 1 - i, 1)
                    return carry

                lax.fori_loop(0, 2, one, 0)

        before_token = jnp.where(step == 0, 0, token_end(step - 1))
        before_row = jnp.where(step == 0, 0, row_end(step - 1))
        token_side(step, before_token, before_row)

        @pl.when((step == n_chip - 2) & is_top)
        def _():
            collect_down(n_chip - 2, early)

        return carry

    lax.fori_loop(0, n_chip, advance, 0)

    @pl.when(is_upper)
    def _():
        own = layer - 1
        landed(hp_all.at[own], hp_recv.at[own])
        landed(a_all.at[others, pl.ds(own, 1)], a_recv.at[own])
        add(own)

    collect_down(jnp.where(is_top, early - 1, chip - 1), 0)

    row = lax.broadcasted_iota(jnp.int32, (8, tokens), 0)
    token = lax.broadcasted_iota(jnp.int32, (8, tokens), 1)
    members = jnp.where(token // SLOT == row, 1.0, 0.0)
    sums = lax.dot_general(
        members,
        total[...],
        (((1,), (1,)), ((), ())),
        precision=lax.Precision.HIGHEST,
        preferred_element_type=F32,
    )
    row = lax.broadcasted_iota(jnp.int32, (every, 128), 0)
    col = lax.broadcasted_iota(jnp.int32, (every, 128), 1)
    joined = jnp.where((row // group) * half + lax.rem(row, half) == col, 1.0, 0.0)
    s_all[layer] = jnp.dot(
        sums, joined, precision=lax.Precision.HIGHEST, preferred_element_type=F32
    )

    def s_copy(k):
        return pltpu.make_async_remote_copy(
            src_ref=s_all.at[layer],
            dst_ref=s_all.at[layer],
            send_sem=s_send.at[k],
            recv_sem=s_recv,
            device_id={"pipe": lax.rem(layer + k, n_pipe)},
            device_id_type=MESH,
        )

    for k in range(1, n_pipe):
        s_copy(k).start()

    landed(rows_all.at[others], rows_send)

    def sent_unit(u, n):
        rows = pl.ds(u, n)
        landed(a_all.at[others, rows], a_send.at[u])

        @pl.when(is_lower)
        def _():
            factor_copy(u, n).wait_send()
            for c in range(CHUNKS):
                pass_copy(u, n, c).wait_send()

        @pl.when(jnp.logical_not(is_top))
        def _():
            for c in range(CHUNKS):
                up_copy(u, n, c).wait_send()

    def sent_pair(below, carry):
        sent_unit(2 * below, 2)
        return carry

    def sent_one(u, carry):
        sent_unit(u, 1)
        return carry

    lax.fori_loop(ALONE, jnp.maximum(chip, ALONE), sent_pair, 0)
    lax.fori_loop(0, jnp.minimum(2 * ALONE, 2 * chip), sent_one, 0)

    @pl.when(is_lower)
    def _():
        for c in range(CHUNKS):
            own_copy(c).wait_send()
        hp_pass(layer).wait_send()

    @pl.when(is_lower & (chip > 0))
    def _():
        for c in range(CHUNKS):
            part_copy(c).wait_send()

    @pl.when(is_upper)
    def _():
        landed(a_all.at[others, pl.ds(layer - 1, 1)], a_send.at[layer - 1])

        @pl.when(chip > 0)
        def _():
            landed(k_all.at[others], k_send)

        @pl.when(jnp.logical_not(is_top))
        def _():
            for c in range(CHUNKS):

                @pl.when(pairs_up)
                def _():
                    up_copy(layer - 1, 2, c).wait_send()

                @pl.when(jnp.logical_not(pairs_up))
                def _():
                    up_copy(layer - 1, 1, c).wait_send()
                    up_copy(layer, 1, c).wait_send()

    for target in range(1, n_chip):

        @pl.when(chip < target)
        def _():
            hp_copy(target).wait_send()

        @pl.when(chip >= target)
        def _():
            hp_pass(2 * (target - 1) + core).wait_send()

    for k in range(1, n_pipe):
        s_copy(k).wait_send()
    arrived = s_all.at[pl.ds(0, n_pipe - 1)]
    pltpu.make_async_copy(arrived, arrived, s_recv).wait()
    result = s_all[0]
    for source in range(1, n_pipe):
        result = result + s_all[source]
    result = result[:n_example, :queries] * (ADAPTER_SCALE * SLOT**-0.5)
    example = lane * n_example + lax.broadcasted_iota(jnp.int32, (n_example, queries), 0)
    out_ref[...] = result * jnp.where(example != qe_ref[...], 1.0, 0.0)


def solution(mesh):
    n_dp, n_pipe = mesh.shape["dp"], mesh.shape["pipe"]

    def local(act, cot, down, expand, value, inputs, hidden_cols, inner_cols, lengths, query):
        tokens, width = cot.shape
        rank = down.shape[2]
        queries = hidden_cols.shape[1]
        n_example = tokens // SLOT
        group = 2 * value.shape[1]
        every = group * n_dp
        hbm = pl.BlockSpec(memory_space=pl.ANY)
        vmem = pl.BlockSpec(memory_space=pltpu.VMEM)
        dma = pltpu.SemaphoreType.DMA
        return pl.pallas_call(
            functools.partial(kernel, n_dp, n_pipe),
            out_shape=jax.ShapeDtypeStruct((n_example, queries), F32),
            in_specs=[hbm] * 10,
            out_specs=vmem,
            scratch_shapes=[
                pltpu.VMEM(value.shape, BF16),
                pltpu.VMEM(inputs.shape, BF16),
                pltpu.VMEM(hidden_cols.shape, BF16),
                pltpu.VMEM(inner_cols.shape, BF16),
                pltpu.VMEM((1, n_example), jnp.int32),
                pltpu.VMEM((1, queries), jnp.int32),
                pltpu.VMEM((PIECES, tokens, width // PIECES), BF16),
                pltpu.VMEM((PIECES, tokens, width // PIECES), BF16),
                pltpu.VMEM((width, rank), BF16),
                pltpu.VMEM((rank, width), BF16),
                pltpu.VMEM((n_pipe, group, width), BF16),
                pltpu.VMEM((n_pipe, group, width), BF16),
                pltpu.VMEM((n_pipe, group, width), BF16),
                pltpu.VMEM((n_dp, n_pipe, group, rank), BF16),
                pltpu.VMEM((n_pipe, group, rank), BF16),
                pltpu.VMEM((rank // n_dp, width), BF16),
                pltpu.VMEM((n_dp, rank // n_dp, rank), BF16),
                pltpu.VMEM((n_pipe, every, tokens), BF16),
                pltpu.VMEM((n_dp, group, width), BF16),
                pltpu.VMEM((rank, tokens), F32),
                pltpu.VMEM((rank, tokens), BF16),
                pltpu.VMEM((every, tokens), F32),
                pltpu.VMEM((every, tokens), F32),
                pltpu.VMEM((every, tokens), F32),
                pltpu.VMEM((n_pipe, 8, 128), F32),
                dma((6,)),
                dma((CHUNKS,)),
                dma((CHUNKS,)),
                dma((PIECES,)),
                dma((PIECES,)),
                dma,
                dma,
                dma((n_pipe, CHUNKS)),
                dma((n_pipe, CHUNKS)),
                dma((n_pipe, CHUNKS)),
                dma((n_pipe, CHUNKS)),
                dma((n_pipe,)),
                dma((n_pipe,)),
                dma((CHUNKS,)),
                dma((CHUNKS,)),
                dma,
                dma,
                dma((n_pipe,)),
                dma((n_pipe,)),
                dma((n_pipe // 2,)),
                dma((n_pipe,)),
                dma((n_pipe,)),
                dma((n_pipe,)),
                dma,
                pltpu.SemaphoreType.REGULAR,
            ],
            compiler_params=pltpu.CompilerParams(
                collective_id=0, has_side_effects=True, vmem_limit_bytes=58 << 20
            ),
            name="influence",
        )(
            act,
            cot,
            down,
            expand,
            value,
            inputs,
            hidden_cols,
            inner_cols,
            lengths.reshape(1, n_example),
            query.reshape(1, queries),
        )

    in_specs = (
        P("pipe", "dp", None),
        P("dp", None),
        P("pipe", None, None),
        P("pipe", None, None),
        P("pipe", "dp", None),
        P("pipe", "dp", None),
        P("pipe", None, None),
        P("pipe", None, None),
        P("dp"),
        P(),
    )
    return jax.shard_map(
        local, mesh=mesh, in_specs=in_specs, out_specs=P("dp", None), check_vma=False
    )
```

```python
import functools

import jax
import jax.numpy as jnp
from jax import lax
from jax.experimental import pallas as pl
from jax.experimental.pallas import tpu as pltpu
from jax.sharding import PartitionSpec as P

SLOT = 128
ADAPTER_SCALE = 0.25
MESH = pl.DeviceIdType.MESH
F32 = jnp.float32
BF16 = jnp.bfloat16
CHUNKS = 4
PIECES = 8
ALONE = 1
LOW = 3


def nt(a, b):
    return lax.dot_general(a, b, (((1,), (1,)), ((), ())), preferred_element_type=F32)


def kernel(
    n_dp,
    n_pipe,
    x_hbm,
    cot_hbm,
    d_hbm,
    e_hbm,
    v_hbm,
    i_hbm,
    hc_hbm,
    ic_hbm,
    len_hbm,
    qe_hbm,
    out_ref,
    v_ref,
    i_ref,
    hc_ref,
    ic_ref,
    len_ref,
    qe_ref,
    x_v,
    cot_v,
    d_v,
    e_v,
    z_in,
    y_in,
    sent,
    a_all,
    f_in,
    k_part,
    k_all,
    hp_all,
    rows_all,
    u_acc,
    u_bf,
    own_acc,
    hp_acc,
    total,
    s_all,
    load_small,
    load_e,
    load_d,
    load_cot,
    load_x,
    rows_send,
    rows_recv,
    main_send,
    pass_send,
    z_recv,
    y_recv,
    f_send,
    f_recv,
    part_send,
    part_recv,
    k_send,
    k_recv,
    a_send,
    a_recv,
    hp_send,
    pass_hp,
    hp_recv,
    s_send,
    s_recv,
    go_sem,
):
    lane = lax.axis_index("dp")
    layer = lax.axis_index("pipe")
    core = lax.rem(layer, 2)
    chip = layer // 2
    n_chip = n_pipe // 2
    is_top = chip == n_chip - 1
    width, rank = d_v.shape
    tokens = u_acc.shape[1]
    group = z_in.shape[1]
    half = group // 2
    queries = hc_ref.shape[1]
    every = group * n_dp
    share = rank // n_dp
    wide = width // CHUNKS
    piece = width // PIECES
    n_example = len_ref.shape[1]
    sibling = {"pipe": layer + 1 - 2 * core}
    above = {"pipe": lax.rem(2 * chip + 2, n_pipe)}

    def span(c):
        return slice(c * wide, (c + 1) * wide)

    def remote(src, dst, send_sem, recv_sem, device):
        return pltpu.make_async_remote_copy(
            src_ref=src,
            dst_ref=dst,
            send_sem=send_sem,
            recv_sem=recv_sem,
            device_id=device,
            device_id_type=MESH,
        )

    def landed(ref, sem):
        pltpu.make_async_copy(ref, ref, sem).wait()

    def load_expand(c):
        cols = pl.ds(c * wide, wide)
        return pltpu.make_async_copy(e_hbm.at[0, :, cols], e_v.at[:, cols], load_e.at[c])

    def load_down(c):
        rows = pl.ds(c * wide, wide)
        return pltpu.make_async_copy(d_hbm.at[0, rows, :], d_v.at[rows, :], load_d.at[c])

    def load_cotangent(k):
        cols = pl.ds(pl.multiple_of(k * piece, piece), piece)
        return pltpu.make_async_copy(cot_hbm.at[:, cols], cot_v.at[k], load_cot.at[k])

    def load_activation(k):
        cols = pl.ds(pl.multiple_of(k * piece, piece), piece)
        return pltpu.make_async_copy(x_hbm.at[0, :, cols], x_v.at[k], load_x.at[k])

    small = [
        pltpu.make_async_copy(src, dst, load_small.at[n])
        for n, (src, dst) in enumerate(
            (
                (ic_hbm, ic_ref),
                (v_hbm, v_ref),
                (i_hbm, i_ref),
                (hc_hbm, hc_ref),
                (len_hbm, len_ref),
                (qe_hbm, qe_ref),
            )
        )
    ]
    for copy in small:
        copy.start()
    is_lower = core == 0
    is_upper = core == 1

    @pl.when(is_lower)
    def _():
        for c in range(CHUNKS):
            load_expand(c).start()

    @pl.when(is_upper)
    def _():
        for c in range(CHUNKS):
            load_down(c).start()

    barrier = pltpu.get_barrier_semaphore()
    last = n_pipe - 1
    for k in range(1, n_dp):
        pl.semaphore_signal(
            barrier, 1, device_id={"dp": lax.rem(lane + k, n_dp)}, device_id_type=MESH
        )
    pl.semaphore_signal(barrier, 1, device_id=sibling, device_id_type=MESH)

    @pl.when((core == 0) & (chip > 0))
    def _():
        pl.semaphore_signal(
            barrier, 1, device_id={"pipe": jnp.maximum(layer - 1, 0)}, device_id_type=MESH
        )

    @pl.when(layer < last - 1)
    def _():
        pl.semaphore_signal(barrier, 1, device_id={"pipe": last}, device_id_type=MESH)

    waits_above = jnp.where((core == 1) & (layer < last), 1, 0)
    waits_column = jnp.where(layer == last, n_pipe - 2, 0)
    pl.semaphore_wait(barrier, n_dp + waits_above + waits_column)

    @pl.when(layer == last)
    def _():
        for target in range(last):
            pl.semaphore_signal(go_sem, 1, device_id={"pipe": target}, device_id_type=MESH)

    for copy in small:
        copy.wait()

    v_rows = v_ref[0].astype(F32)
    rows_all[lane] = jnp.concatenate([v_rows, i_ref[0].astype(F32)], axis=0).astype(BF16)

    def lane_at(k):
        return {"dp": lax.rem(lane + k, n_dp)}

    def spread_rows():
        for k in range(1, n_dp):
            remote(
                rows_all.at[lane], rows_all.at[lane], rows_send, rows_recv, lane_at(k)
            ).start()

    row = lax.broadcasted_iota(jnp.int32, (group, queries), 0)
    col = lax.broadcasted_iota(jnp.int32, (group, queries), 1)
    pick = jnp.where((row >= half) & (lane * half + row - half == col), 1.0, 0.0).astype(BF16)
    ic_lane = jnp.dot(pick, ic_ref[0], preferred_element_type=F32).astype(BF16)
    v_wide = jnp.concatenate([v_rows, jnp.zeros_like(v_rows)], axis=0)

    def own_copy(c):
        return remote(
            sent.at[layer, :, span(c)],
            z_in.at[layer, :, span(c)],
            main_send.at[layer, c],
            z_recv.at[layer, c],
            sibling,
        )

    def up_copy(u, n, c):
        rows = pl.ds(u, n)
        return remote(
            sent.at[rows, :, span(c)],
            z_in.at[rows, :, span(c)],
            main_send.at[u, c],
            z_recv.at[u, c],
            above,
        )

    def over_copy(u, n, c):
        rows = pl.ds(u, n)
        return remote(
            sent.at[rows, :, span(c)],
            y_in.at[rows, :, span(c)],
            main_send.at[u, c],
            y_recv.at[u, c],
            sibling,
        )

    def pass_copy(u, n, c):
        rows = pl.ds(u, n)
        return remote(
            z_in.at[rows, :, span(c)],
            z_in.at[rows, :, span(c)],
            pass_send.at[u, c],
            z_recv.at[u, c],
            sibling,
        )

    def factor_copy(u, n):
        rows = pl.ds(u, n)
        return remote(a_all.at[lane, rows], f_in.at[rows], f_send.at[u], f_recv.at[u], sibling)

    def spread_factors(u, n):
        rows = pl.ds(u, n)
        for k in range(1, n_dp):
            remote(
                a_all.at[lane, rows], a_all.at[lane, rows], a_send.at[u], a_recv.at[u], lane_at(k)
            ).start()

    others = pl.ds(0, n_dp - 1)

    def part_copy():
        return remote(
            e_hbm.at[0, pl.ds(pl.multiple_of(lane * share, share), share), :],
            k_part,
            part_send,
            part_recv,
            sibling,
        )

    pairs_up = chip >= ALONE

    @pl.when(is_lower & (chip > 0))
    def _():
        part_copy().start()

    @pl.when(is_lower)
    def _():
        spread_rows()

    def born(c):
        own = v_wide[:, span(c)] + jnp.dot(ic_lane, e_v[:, span(c)], preferred_element_type=F32)
        sent[layer, :, span(c)] = own.astype(BF16)

    @pl.when(is_lower)
    def _():
        for c in range(CHUNKS):
            load_expand(c).wait()
            load_down(c).start()
            born(c)
            own_copy(c).start()
        for c in range(CHUNKS):
            load_down(c).wait()

    def take(ref, u, n, c):
        return ref[pl.ds(u, n), :, span(c)].astype(F32).reshape(n * group, wide)

    def down(z, c):
        return jnp.dot(z.astype(BF16), d_v[span(c), :], preferred_element_type=F32)

    def up(factor, c):
        return jnp.dot(factor, e_v[:, span(c)], preferred_element_type=F32)

    def keep(u, n, projected):
        factor = ADAPTER_SCALE * projected
        a_all[lane, pl.ds(u, n)] = factor.reshape(n, group, rank).astype(BF16)
        return factor.astype(BF16)

    def put(u, n, c, moved):
        sent[pl.ds(u, n), :, span(c)] = moved.reshape(n, group, wide).astype(BF16)

    def lower_stage(u, n):
        projected = jnp.zeros((n * group, rank), F32)
        for c in range(CHUNKS):
            up_copy(u, n, c).wait_recv()
            pass_copy(u, n, c).start()
            projected += down(take(z_in, u, n, c), c)
        factor = keep(u, n, projected)
        factor_copy(u, n).start()

        @pl.when(jnp.logical_not(is_top))
        def _():
            for c in range(CHUNKS):
                put(u, n, c, take(z_in, u, n, c) + up(factor, c))
                over_copy(u, n, c).start()

        spread_factors(u, n)

    def upper_stage(u, n, first):
        projected = jnp.zeros((n * group, rank), F32)
        for c in range(CHUNKS):
            pass_copy(u, n, c).wait_recv()
            projected += down(take(z_in, u, n, c), c)
        factor_copy(u, n).wait_recv()

        @pl.when(first)
        def _():
            landed(k_all.at[others], k_recv)

        below = f_in[pl.ds(u, n)].astype(F32).reshape(n * group, rank).astype(BF16)
        projected += jnp.dot(below, k_all[...].reshape(rank, rank), preferred_element_type=F32)
        factor = keep(u, n, projected)

        @pl.when(jnp.logical_not(is_top))
        def _():
            for c in range(CHUNKS):
                over_copy(u, n, c).wait_recv()
                put(u, n, c, take(y_in, u, n, c) + up(factor, c))
                up_copy(u, n, c).start()

        spread_factors(u, n)

    @pl.when(is_upper)
    def _():
        u = layer - 1

        @pl.when(chip > 0)
        def _():
            landed(k_part, part_recv)
            coupled = jnp.zeros((share, rank), F32)
            for c in range(CHUNKS):
                load_down(c).wait()
                load_expand(c).start()
                coupled += jnp.dot(k_part[:, span(c)], d_v[span(c), :], preferred_element_type=F32)
            k_all[lane] = coupled.astype(BF16)
            for k in range(1, n_dp):
                remote(k_all.at[lane], k_all.at[lane], k_send, k_recv, lane_at(k)).start()

        @pl.when(chip == 0)
        def _():
            for c in range(CHUNKS):
                load_down(c).wait()
                load_expand(c).start()

        projected = jnp.zeros((group, rank), F32)
        for c in range(CHUNKS):
            landed(z_in.at[u, :, span(c)], z_recv.at[u, c])
            projected += down(take(z_in, u, 1, c), c)
        factor = keep(u, 1, projected)
        for c in range(CHUNKS):
            load_expand(c).wait()

            @pl.when(jnp.logical_not(is_top))
            def _():
                born(c)
                put(u, 1, c, take(z_in, u, 1, c) + up(factor, c))

                @pl.when(pairs_up)
                def _():
                    up_copy(u, 2, c).start()

                @pl.when(jnp.logical_not(pairs_up))
                def _():
                    up_copy(layer, 1, c).start()
                    up_copy(u, 1, c).start()

        spread_factors(u, 1)
        spread_rows()

    for k in range(PIECES):
        load_cotangent(k).start()
    for k in range(PIECES):
        load_activation(k).start()

    def placed(first):
        row = lax.broadcasted_iota(jnp.int32, (every, queries), 0)
        col = lax.broadcasted_iota(jnp.int32, (every, queries), 1)
        within = lax.rem(row, group) - first
        query = (row // group) * half + within
        hit = (within >= 0) & (within < half) & (query == col)
        return jnp.where(hit, 1.0, 0.0).astype(BF16)

    hc_placed = jnp.dot(placed(0), hc_ref[0], preferred_element_type=F32).astype(BF16)
    ic_placed = jnp.dot(placed(half), ic_ref[0], preferred_element_type=F32).astype(BF16)
    def token_part(k):
        load_cotangent(k).wait()
        cols = pl.ds(pl.multiple_of(k * piece, piece), piece)
        u_acc[...] += nt(e_v[:, cols], cot_v[k])

    def row_part(k):
        load_activation(k).wait()
        cols = pl.ds(pl.multiple_of(k * piece, piece), piece)
        gathered = rows_all[:, :, cols].astype(F32).reshape(every, piece)
        of_value = lax.rem(lax.broadcasted_iota(jnp.int32, (every, piece), 0), group) < half
        value_side = jnp.where(of_value, gathered, 0.0).astype(BF16)
        own_acc[...] += nt(value_side, cot_v[k])
        hidden_side = nt(hc_placed, d_v[cols, :])
        input_side = (hidden_side + jnp.where(of_value, 0.0, gathered)).astype(BF16)
        hp_acc[...] += nt(input_side, x_v[k])

    def hp_copy(target):
        return remote(
            hp_all.at[layer],
            hp_all.at[layer],
            hp_send.at[target],
            hp_recv.at[layer],
            {"pipe": 2 * target + core},
        )

    def hp_pass(source):
        return remote(
            hp_all.at[source], hp_all.at[source], pass_hp.at[source], hp_recv.at[source], sibling
        )

    def settle():
        token = lax.broadcasted_iota(jnp.int32, (every, tokens), 1)
        count = jnp.zeros((every, tokens), jnp.int32)
        for e in range(n_example):
            count = jnp.where(token // SLOT == e, len_ref[:, e : e + 1], count)
        live = jnp.where(lax.rem(token, SLOT) < count, 1.0, 0.0)
        hp_all[layer] = (hp_acc[...] * live).astype(BF16)

        @pl.when(layer < last)
        def _():
            pl.semaphore_wait(go_sem, 1)

        for target in range(1, n_chip):

            @pl.when(chip < target)
            def _():
                hp_copy(target).start()

        @pl.when(is_lower)
        def _():
            hp_pass(layer).start()

        u_bf[...] = u_acc[...].astype(BF16)
        own = own_acc[...] + jnp.dot(ic_placed, u_bf[...], preferred_element_type=F32)
        total[...] = own * hp_all[layer].astype(F32)

    def add(source):
        factors = a_all[:, source].astype(F32).reshape(every, rank).astype(BF16)
        total[...] += jnp.dot(factors, u_bf[...], preferred_element_type=F32) * hp_all[
            source
        ].astype(F32)

    def collect(below):
        mine, other = 2 * below + core, 2 * below + 1 - core
        landed(hp_all.at[mine], hp_recv.at[mine])
        hp_pass(mine).start()
        landed(hp_all.at[other], hp_recv.at[other])

        @pl.when(below >= ALONE)
        def _():
            landed(a_all.at[others, pl.ds(2 * below, 2)], a_recv.at[2 * below])

        @pl.when(below < ALONE)
        def _():
            landed(a_all.at[others, pl.ds(2 * below + 1, 1)], a_recv.at[2 * below + 1])

        add(2 * below + 1)

        @pl.when(below < ALONE)
        def _():
            landed(a_all.at[others, pl.ds(2 * below, 1)], a_recv.at[2 * below])

        add(2 * below)

    u_acc[...] = jnp.zeros_like(u_acc)
    own_acc[...] = jnp.zeros_like(own_acc)
    hp_acc[...] = jnp.zeros_like(hp_acc)
    hc_placed = jnp.dot(placed(0), hc_ref[0], preferred_element_type=F32).astype(BF16)
    ic_placed = jnp.dot(placed(half), ic_ref[0], preferred_element_type=F32).astype(BF16)

    is_low = chip < LOW

    def token_end(step):
        late = jnp.where(step >= chip, PIECES, 0)
        return jnp.where(is_low, late, jnp.clip(4 + 2 * step, 0, PIECES))

    def row_end(step):
        late = jnp.where(step >= chip, PIECES, 0)
        return jnp.where(is_low, late, jnp.clip(2 * step - 2, 0, PIECES))

    def token_side(step, before_token, before_row):
        end_token, end_row = token_end(step), row_end(step)

        def token_step(k, carry):
            token_part(k)
            return carry

        def row_step(k, carry):
            row_part(k)
            return carry

        lax.fori_loop(before_token, end_token, token_step, 0)

        @pl.when((before_row == 0) & (end_row > 0))
        def _():
            landed(rows_all.at[others], rows_recv)

        lax.fori_loop(before_row, end_row, row_step, 0)

        @pl.when((before_row < PIECES) & (end_row == PIECES))
        def _():
            settle()

    def stage(u, n, first):
        @pl.when(is_lower)
        def _():
            lower_stage(u, n)

        @pl.when(is_upper)
        def _():
            upper_stage(u, n, first)

    def collect_down(first, last):
        def body(i, carry):
            collect(first - i)
            return carry

        lax.fori_loop(0, jnp.maximum(first - last + 1, 0), body, 0)

    early = 2

    def advance(step, carry):
        @pl.when((step >= 1) & (step <= chip))
        def _():
            below = jnp.maximum(chip - step, 0)

            @pl.when(below >= ALONE)
            def _():
                stage(2 * below, 2, step == 1)

            @pl.when(below < ALONE)
            def _():
                def one(i, carry):
                    stage(2 * below + 1 - i, 1, (step == 1) & (i == 0))
                    return carry

                lax.fori_loop(0, 2, one, 0)

        before_token = jnp.where(step == 0, 0, token_end(step - 1))
        before_row = jnp.where(step == 0, 0, row_end(step - 1))
        token_side(step, before_token, before_row)

        @pl.when((step == n_chip - 2) & is_top)
        def _():
            collect_down(n_chip - 2, early)

        return carry

    lax.fori_loop(0, n_chip, advance, 0)

    @pl.when(is_upper)
    def _():
        own = layer - 1
        landed(hp_all.at[own], hp_recv.at[own])
        landed(a_all.at[others, pl.ds(own, 1)], a_recv.at[own])
        add(own)

    collect_down(jnp.where(is_top, early - 1, chip - 1), 0)

    row = lax.broadcasted_iota(jnp.int32, (8, tokens), 0)
    token = lax.broadcasted_iota(jnp.int32, (8, tokens), 1)
    members = jnp.where(token // SLOT == row, 1.0, 0.0)
    sums = lax.dot_general(
        members,
        total[...],
        (((1,), (1,)), ((), ())),
        precision=lax.Precision.HIGHEST,
        preferred_element_type=F32,
    )
    row = lax.broadcasted_iota(jnp.int32, (every, 128), 0)
    col = lax.broadcasted_iota(jnp.int32, (every, 128), 1)
    joined = jnp.where((row // group) * half + lax.rem(row, half) == col, 1.0, 0.0)
    s_all[layer] = jnp.dot(
        sums, joined, precision=lax.Precision.HIGHEST, preferred_element_type=F32
    )

    def s_copy(k):
        return pltpu.make_async_remote_copy(
            src_ref=s_all.at[layer],
            dst_ref=s_all.at[layer],
            send_sem=s_send.at[k],
            recv_sem=s_recv,
            device_id={"pipe": lax.rem(layer + k, n_pipe)},
            device_id_type=MESH,
        )

    for k in range(1, n_pipe):
        s_copy(k).start()

    landed(rows_all.at[others], rows_send)

    def sent_unit(u, n):
        rows = pl.ds(u, n)
        landed(a_all.at[others, rows], a_send.at[u])

        @pl.when(is_lower)
        def _():
            factor_copy(u, n).wait_send()
            for c in range(CHUNKS):
                pass_copy(u, n, c).wait_send()

        @pl.when(jnp.logical_not(is_top))
        def _():
            for c in range(CHUNKS):
                up_copy(u, n, c).wait_send()

    def sent_pair(below, carry):
        sent_unit(2 * below, 2)
        return carry

    def sent_one(u, carry):
        sent_unit(u, 1)
        return carry

    lax.fori_loop(ALONE, jnp.maximum(chip, ALONE), sent_pair, 0)
    lax.fori_loop(0, jnp.minimum(2 * ALONE, 2 * chip), sent_one, 0)

    @pl.when(is_lower)
    def _():
        for c in range(CHUNKS):
            own_copy(c).wait_send()
        hp_pass(layer).wait_send()

    @pl.when(is_lower & (chip > 0))
    def _():
        part_copy().wait_send()

    @pl.when(is_upper)
    def _():
        landed(a_all.at[others, pl.ds(layer - 1, 1)], a_send.at[layer - 1])

        @pl.when(chip > 0)
        def _():
            landed(k_all.at[others], k_send)

        @pl.when(jnp.logical_not(is_top))
        def _():
            for c in range(CHUNKS):

                @pl.when(pairs_up)
                def _():
                    up_copy(layer - 1, 2, c).wait_send()

                @pl.when(jnp.logical_not(pairs_up))
                def _():
                    up_copy(layer - 1, 1, c).wait_send()
                    up_copy(layer, 1, c).wait_send()

    for target in range(1, n_chip):

        @pl.when(chip < target)
        def _():
            hp_copy(target).wait_send()

        @pl.when(chip >= target)
        def _():
            hp_pass(2 * (target - 1) + core).wait_send()

    for k in range(1, n_pipe):
        s_copy(k).wait_send()
    arrived = s_all.at[pl.ds(0, n_pipe - 1)]
    pltpu.make_async_copy(arrived, arrived, s_recv).wait()
    result = s_all[0]
    for source in range(1, n_pipe):
        result = result + s_all[source]
    result = result[:n_example, :queries] * (ADAPTER_SCALE * SLOT**-0.5)
    example = lane * n_example + lax.broadcasted_iota(jnp.int32, (n_example, queries), 0)
    out_ref[...] = result * jnp.where(example != qe_ref[...], 1.0, 0.0)


def solution(mesh):
    n_dp, n_pipe = mesh.shape["dp"], mesh.shape["pipe"]

    def local(act, cot, down, expand, value, inputs, hidden_cols, inner_cols, lengths, query):
        tokens, width = cot.shape
        rank = down.shape[2]
        queries = hidden_cols.shape[1]
        n_example = tokens // SLOT
        group = 2 * value.shape[1]
        every = group * n_dp
        hbm = pl.BlockSpec(memory_space=pl.ANY)
        vmem = pl.BlockSpec(memory_space=pltpu.VMEM)
        dma = pltpu.SemaphoreType.DMA
        return pl.pallas_call(
            functools.partial(kernel, n_dp, n_pipe),
            out_shape=jax.ShapeDtypeStruct((n_example, queries), F32),
            in_specs=[hbm] * 10,
            out_specs=vmem,
            scratch_shapes=[
                pltpu.VMEM(value.shape, BF16),
                pltpu.VMEM(inputs.shape, BF16),
                pltpu.VMEM(hidden_cols.shape, BF16),
                pltpu.VMEM(inner_cols.shape, BF16),
                pltpu.VMEM((1, n_example), jnp.int32),
                pltpu.VMEM((1, queries), jnp.int32),
                pltpu.VMEM((PIECES, tokens, width // PIECES), BF16),
                pltpu.VMEM((PIECES, tokens, width // PIECES), BF16),
                pltpu.VMEM((width, rank), BF16),
                pltpu.VMEM((rank, width), BF16),
                pltpu.VMEM((n_pipe, group, width), BF16),
                pltpu.VMEM((n_pipe, group, width), BF16),
                pltpu.VMEM((n_pipe, group, width), BF16),
                pltpu.VMEM((n_dp, n_pipe, group, rank), BF16),
                pltpu.VMEM((n_pipe, group, rank), BF16),
                pltpu.VMEM((rank // n_dp, width), BF16),
                pltpu.VMEM((n_dp, rank // n_dp, rank), BF16),
                pltpu.VMEM((n_pipe, every, tokens), BF16),
                pltpu.VMEM((n_dp, group, width), BF16),
                pltpu.VMEM((rank, tokens), F32),
                pltpu.VMEM((rank, tokens), BF16),
                pltpu.VMEM((every, tokens), F32),
                pltpu.VMEM((every, tokens), F32),
                pltpu.VMEM((every, tokens), F32),
                pltpu.VMEM((n_pipe, 8, 128), F32),
                dma((6,)),
                dma((CHUNKS,)),
                dma((CHUNKS,)),
                dma((PIECES,)),
                dma((PIECES,)),
                dma,
                dma,
                dma((n_pipe, CHUNKS)),
                dma((n_pipe, CHUNKS)),
                dma((n_pipe, CHUNKS)),
                dma((n_pipe, CHUNKS)),
                dma((n_pipe,)),
                dma((n_pipe,)),
                dma,
                dma,
                dma,
                dma,
                dma((n_pipe,)),
                dma((n_pipe,)),
                dma((n_pipe // 2,)),
                dma((n_pipe,)),
                dma((n_pipe,)),
                dma((n_pipe,)),
                dma,
                pltpu.SemaphoreType.REGULAR,
            ],
            compiler_params=pltpu.CompilerParams(
                collective_id=0, has_side_effects=True, vmem_limit_bytes=58 << 20
            ),
            name="influence",
        )(
            act,
            cot,
            down,
            expand,
            value,
            inputs,
            hidden_cols,
            inner_cols,
            lengths.reshape(1, n_example),
            query.reshape(1, queries),
        )

    in_specs = (
        P("pipe", "dp", None),
        P("dp", None),
        P("pipe", None, None),
        P("pipe", None, None),
        P("pipe", "dp", None),
        P("pipe", "dp", None),
        P("pipe", None, None),
        P("pipe", None, None),
        P("dp"),
        P(),
    )
    return jax.shard_map(
        local, mesh=mesh, in_specs=in_specs, out_specs=P("dp", None), check_vma=False
    )
```

```python
import functools

import jax
import jax.numpy as jnp
from jax import lax
from jax.experimental import pallas as pl
from jax.experimental.pallas import tpu as pltpu
from jax.sharding import PartitionSpec as P

SLOT = 128
ADAPTER_SCALE = 0.25
MESH = pl.DeviceIdType.MESH
F32 = jnp.float32
BF16 = jnp.bfloat16
CHUNKS = 4
PIECES = 8
ALONE = 1
LOW = 3


def nt(a, b):
    return lax.dot_general(a, b, (((1,), (1,)), ((), ())), preferred_element_type=F32)


def kernel(
    n_dp,
    n_pipe,
    x_hbm,
    cot_hbm,
    d_hbm,
    e_hbm,
    v_hbm,
    i_hbm,
    hc_hbm,
    ic_hbm,
    len_hbm,
    qe_hbm,
    out_ref,
    v_ref,
    i_ref,
    hc_ref,
    ic_ref,
    len_ref,
    qe_ref,
    x_v,
    cot_v,
    d_v,
    e_v,
    z_in,
    y_in,
    sent,
    a_all,
    f_in,
    k_part,
    k_all,
    hp_all,
    rows_all,
    u_acc,
    u_bf,
    own_acc,
    hp_acc,
    total,
    s_all,
    load_small,
    load_e,
    load_d,
    load_cot,
    load_x,
    rows_send,
    rows_recv,
    main_send,
    pass_send,
    z_recv,
    y_recv,
    f_send,
    f_recv,
    part_send,
    part_recv,
    k_send,
    k_recv,
    a_send,
    a_recv,
    hp_send,
    pass_hp,
    hp_recv,
    s_send,
    s_recv,
    go_sem,
):
    lane = lax.axis_index("dp")
    layer = lax.axis_index("pipe")
    core = lax.rem(layer, 2)
    chip = layer // 2
    n_chip = n_pipe // 2
    is_top = chip == n_chip - 1
    width, rank = d_v.shape
    tokens = u_acc.shape[1]
    group = z_in.shape[1]
    half = group // 2
    queries = hc_ref.shape[1]
    every = group * n_dp
    share = rank // n_dp
    wide = width // CHUNKS
    piece = width // PIECES
    n_example = len_ref.shape[1]
    sibling = {"pipe": layer + 1 - 2 * core}
    above = {"pipe": lax.rem(2 * chip + 2, n_pipe)}

    def span(c):
        return slice(c * wide, (c + 1) * wide)

    def remote(src, dst, send_sem, recv_sem, device):
        return pltpu.make_async_remote_copy(
            src_ref=src,
            dst_ref=dst,
            send_sem=send_sem,
            recv_sem=recv_sem,
            device_id=device,
            device_id_type=MESH,
        )

    def landed(ref, sem):
        pltpu.make_async_copy(ref, ref, sem).wait()

    def load_expand(c):
        cols = pl.ds(c * wide, wide)
        return pltpu.make_async_copy(e_hbm.at[0, :, cols], e_v.at[:, cols], load_e.at[c])

    def load_down(c):
        rows = pl.ds(c * wide, wide)
        return pltpu.make_async_copy(d_hbm.at[0, rows, :], d_v.at[rows, :], load_d.at[c])

    def load_cotangent(k):
        cols = pl.ds(pl.multiple_of(k * piece, piece), piece)
        return pltpu.make_async_copy(cot_hbm.at[:, cols], cot_v.at[k], load_cot.at[k])

    def load_activation(k):
        cols = pl.ds(pl.multiple_of(k * piece, piece), piece)
        return pltpu.make_async_copy(x_hbm.at[0, :, cols], x_v.at[k], load_x.at[k])

    small = [
        pltpu.make_async_copy(src, dst, load_small.at[n])
        for n, (src, dst) in enumerate(
            (
                (ic_hbm, ic_ref),
                (v_hbm, v_ref),
                (i_hbm, i_ref),
                (hc_hbm, hc_ref),
                (len_hbm, len_ref),
                (qe_hbm, qe_ref),
            )
        )
    ]
    for copy in small:
        copy.start()
    is_lower = core == 0
    is_upper = core == 1

    @pl.when(is_lower)
    def _():
        for c in range(CHUNKS):
            load_expand(c).start()

    @pl.when(is_upper)
    def _():
        for c in range(CHUNKS):
            load_down(c).start()

    barrier = pltpu.get_barrier_semaphore()
    last = n_pipe - 1
    for k in range(1, n_dp):
        pl.semaphore_signal(
            barrier, 1, device_id={"dp": lax.rem(lane + k, n_dp)}, device_id_type=MESH
        )
    pl.semaphore_signal(barrier, 1, device_id=sibling, device_id_type=MESH)

    @pl.when((core == 0) & (chip > 0))
    def _():
        pl.semaphore_signal(
            barrier, 1, device_id={"pipe": jnp.maximum(layer - 1, 0)}, device_id_type=MESH
        )

    @pl.when(layer < last - 1)
    def _():
        pl.semaphore_signal(barrier, 1, device_id={"pipe": last}, device_id_type=MESH)

    waits_above = jnp.where((core == 1) & (layer < last), 1, 0)
    waits_column = jnp.where(layer == last, n_pipe - 2, 0)
    pl.semaphore_wait(barrier, n_dp + waits_above + waits_column)

    @pl.when(layer == last)
    def _():
        for target in range(last):
            pl.semaphore_signal(go_sem, 1, device_id={"pipe": target}, device_id_type=MESH)

    for copy in small:
        copy.wait()

    v_rows = v_ref[0].astype(F32)
    rows_all[lane] = jnp.concatenate([v_rows, i_ref[0].astype(F32)], axis=0).astype(BF16)

    def lane_at(k):
        return {"dp": lax.rem(lane + k, n_dp)}

    def spread_rows():
        for k in range(1, n_dp):
            remote(
                rows_all.at[lane], rows_all.at[lane], rows_send, rows_recv, lane_at(k)
            ).start()

    row = lax.broadcasted_iota(jnp.int32, (group, queries), 0)
    col = lax.broadcasted_iota(jnp.int32, (group, queries), 1)
    pick = jnp.where((row >= half) & (lane * half + row - half == col), 1.0, 0.0).astype(BF16)
    ic_lane = jnp.dot(pick, ic_ref[0], preferred_element_type=F32).astype(BF16)
    v_wide = jnp.concatenate([v_rows, jnp.zeros_like(v_rows)], axis=0)

    def own_copy(c):
        return remote(
            sent.at[layer, :, span(c)],
            z_in.at[layer, :, span(c)],
            main_send.at[layer, c],
            z_recv.at[layer, c],
            sibling,
        )

    def up_copy(u, n, c):
        rows = pl.ds(u, n)
        return remote(
            sent.at[rows, :, span(c)],
            z_in.at[rows, :, span(c)],
            main_send.at[u, c],
            z_recv.at[u, c],
            above,
        )

    def over_copy(u, n, c):
        rows = pl.ds(u, n)
        return remote(
            sent.at[rows, :, span(c)],
            y_in.at[rows, :, span(c)],
            main_send.at[u, c],
            y_recv.at[u, c],
            sibling,
        )

    def pass_copy(u, n, c):
        rows = pl.ds(u, n)
        return remote(
            z_in.at[rows, :, span(c)],
            z_in.at[rows, :, span(c)],
            pass_send.at[u, c],
            z_recv.at[u, c],
            sibling,
        )

    def factor_copy(u, n):
        rows = pl.ds(u, n)
        return remote(a_all.at[lane, rows], f_in.at[rows], f_send.at[u], f_recv.at[u], sibling)

    def spread_factors(u, n):
        rows = pl.ds(u, n)
        for k in range(1, n_dp):
            remote(
                a_all.at[lane, rows], a_all.at[lane, rows], a_send.at[u], a_recv.at[u], lane_at(k)
            ).start()

    others = pl.ds(0, n_dp - 1)

    def part_copy():
        return remote(
            e_hbm.at[0, pl.ds(pl.multiple_of(lane * share, share), share), :],
            k_part,
            part_send,
            part_recv,
            sibling,
        )

    pairs_up = chip >= ALONE

    @pl.when(is_lower & (chip > 0))
    def _():
        part_copy().start()

    @pl.when(is_lower)
    def _():
        spread_rows()

    def born(c):
        own = v_wide[:, span(c)] + jnp.dot(ic_lane, e_v[:, span(c)], preferred_element_type=F32)
        sent[layer, :, span(c)] = own.astype(BF16)

    @pl.when(is_lower)
    def _():
        for c in range(CHUNKS):
            load_expand(c).wait()
            load_down(c).start()
            born(c)
            own_copy(c).start()
        for c in range(CHUNKS):
            load_down(c).wait()

    def take(ref, u, n, c):
        return ref[pl.ds(u, n), :, span(c)].astype(F32).reshape(n * group, wide)

    def down(z, c):
        return jnp.dot(z.astype(BF16), d_v[span(c), :], preferred_element_type=F32)

    def up(factor, c):
        return jnp.dot(factor, e_v[:, span(c)], preferred_element_type=F32)

    def keep(u, n, projected):
        factor = ADAPTER_SCALE * projected
        a_all[lane, pl.ds(u, n)] = factor.reshape(n, group, rank).astype(BF16)
        return factor.astype(BF16)

    def put(u, n, c, moved):
        sent[pl.ds(u, n), :, span(c)] = moved.reshape(n, group, wide).astype(BF16)

    def lower_stage(u, n):
        projected = jnp.zeros((n * group, rank), F32)
        for c in range(CHUNKS):
            up_copy(u, n, c).wait_recv()
            pass_copy(u, n, c).start()
            projected += down(take(z_in, u, n, c), c)
        factor = keep(u, n, projected)
        factor_copy(u, n).start()

        @pl.when(jnp.logical_not(is_top))
        def _():
            for c in range(CHUNKS):
                put(u, n, c, take(z_in, u, n, c) + up(factor, c))
                over_copy(u, n, c).start()

        spread_factors(u, n)

    def upper_stage(u, n, first):
        projected = jnp.zeros((n * group, rank), F32)
        for c in range(CHUNKS):
            pass_copy(u, n, c).wait_recv()
            projected += down(take(z_in, u, n, c), c)
        factor_copy(u, n).wait_recv()

        @pl.when(first)
        def _():
            landed(k_all.at[others], k_recv)

        below = f_in[pl.ds(u, n)].astype(F32).reshape(n * group, rank).astype(BF16)
        projected += jnp.dot(below, k_all[...].reshape(rank, rank), preferred_element_type=F32)
        factor = keep(u, n, projected)

        @pl.when(jnp.logical_not(is_top))
        def _():
            for c in range(CHUNKS):
                over_copy(u, n, c).wait_recv()
                put(u, n, c, take(y_in, u, n, c) + up(factor, c))
                up_copy(u, n, c).start()

        spread_factors(u, n)

    @pl.when(is_upper)
    def _():
        u = layer - 1

        @pl.when(chip > 0)
        def _():
            landed(k_part, part_recv)
            coupled = jnp.zeros((share, rank), F32)
            for c in range(CHUNKS):
                load_down(c).wait()
                load_expand(c).start()
                coupled += jnp.dot(k_part[:, span(c)], d_v[span(c), :], preferred_element_type=F32)
            k_all[lane] = coupled.astype(BF16)
            for k in range(1, n_dp):
                remote(k_all.at[lane], k_all.at[lane], k_send, k_recv, lane_at(k)).start()

        @pl.when(chip == 0)
        def _():
            for c in range(CHUNKS):
                load_down(c).wait()
                load_expand(c).start()

        projected = jnp.zeros((group, rank), F32)
        for c in range(CHUNKS):
            landed(z_in.at[u, :, span(c)], z_recv.at[u, c])
            projected += down(take(z_in, u, 1, c), c)
        factor = keep(u, 1, projected)
        for c in range(CHUNKS):
            load_expand(c).wait()

            @pl.when(jnp.logical_not(is_top))
            def _():
                born(c)
                put(u, 1, c, take(z_in, u, 1, c) + up(factor, c))

                @pl.when(pairs_up)
                def _():
                    up_copy(u, 2, c).start()

                @pl.when(jnp.logical_not(pairs_up))
                def _():
                    up_copy(layer, 1, c).start()
                    up_copy(u, 1, c).start()

        spread_factors(u, 1)
        spread_rows()

    for k in range(PIECES):
        load_cotangent(k).start()
    for k in range(PIECES):
        load_activation(k).start()

    def placed(first):
        row = lax.broadcasted_iota(jnp.int32, (every, queries), 0)
        col = lax.broadcasted_iota(jnp.int32, (every, queries), 1)
        within = lax.rem(row, group) - first
        query = (row // group) * half + within
        hit = (within >= 0) & (within < half) & (query == col)
        return jnp.where(hit, 1.0, 0.0).astype(BF16)

    hc_placed = jnp.dot(placed(0), hc_ref[0], preferred_element_type=F32).astype(BF16)
    ic_placed = jnp.dot(placed(half), ic_ref[0], preferred_element_type=F32).astype(BF16)
    def token_part(k):
        load_cotangent(k).wait()
        cols = pl.ds(pl.multiple_of(k * piece, piece), piece)
        u_acc[...] += nt(e_v[:, cols], cot_v[k])

    def row_part(k):
        load_activation(k).wait()
        cols = pl.ds(pl.multiple_of(k * piece, piece), piece)
        gathered = rows_all[:, :, cols].astype(F32).reshape(every, piece)
        of_value = lax.rem(lax.broadcasted_iota(jnp.int32, (every, piece), 0), group) < half
        value_side = jnp.where(of_value, gathered, 0.0).astype(BF16)
        own_acc[...] += nt(value_side, cot_v[k])
        hidden_side = nt(hc_placed, d_v[cols, :])
        input_side = (hidden_side + jnp.where(of_value, 0.0, gathered)).astype(BF16)
        hp_acc[...] += nt(input_side, x_v[k])

    def hp_copy(target):
        return remote(
            hp_all.at[layer],
            hp_all.at[layer],
            hp_send.at[target],
            hp_recv.at[layer],
            {"pipe": 2 * target + core},
        )

    def hp_pass(source):
        return remote(
            hp_all.at[source], hp_all.at[source], pass_hp.at[source], hp_recv.at[source], sibling
        )

    def settle():
        token = lax.broadcasted_iota(jnp.int32, (every, tokens), 1)
        count = jnp.zeros((every, tokens), jnp.int32)
        for e in range(n_example):
            count = jnp.where(token // SLOT == e, len_ref[:, e : e + 1], count)
        live = jnp.where(lax.rem(token, SLOT) < count, 1.0, 0.0)
        hp_all[layer] = (hp_acc[...] * live).astype(BF16)

        @pl.when(layer < last)
        def _():
            pl.semaphore_wait(go_sem, 1)

        for target in range(1, n_chip):

            @pl.when(chip < target)
            def _():
                hp_copy(target).start()

        @pl.when(is_lower)
        def _():
            hp_pass(layer).start()

        u_bf[...] = u_acc[...].astype(BF16)
        own = own_acc[...] + jnp.dot(ic_placed, u_bf[...], preferred_element_type=F32)
        total[...] = own * hp_all[layer].astype(F32)

    def add(source):
        factors = a_all[:, source].astype(F32).reshape(every, rank).astype(BF16)
        total[...] += jnp.dot(factors, u_bf[...], preferred_element_type=F32) * hp_all[
            source
        ].astype(F32)

    def collect(below):
        mine, other = 2 * below + core, 2 * below + 1 - core
        landed(hp_all.at[mine], hp_recv.at[mine])
        hp_pass(mine).start()
        landed(hp_all.at[other], hp_recv.at[other])

        @pl.when(below >= ALONE)
        def _():
            landed(a_all.at[others, pl.ds(2 * below, 2)], a_recv.at[2 * below])

        @pl.when(below < ALONE)
        def _():
            landed(a_all.at[others, pl.ds(2 * below + 1, 1)], a_recv.at[2 * below + 1])

        add(2 * below + 1)

        @pl.when(below < ALONE)
        def _():
            landed(a_all.at[others, pl.ds(2 * below, 1)], a_recv.at[2 * below])

        add(2 * below)

    u_acc[...] = jnp.zeros_like(u_acc)
    own_acc[...] = jnp.zeros_like(own_acc)
    hp_acc[...] = jnp.zeros_like(hp_acc)
    hc_placed = jnp.dot(placed(0), hc_ref[0], preferred_element_type=F32).astype(BF16)
    ic_placed = jnp.dot(placed(half), ic_ref[0], preferred_element_type=F32).astype(BF16)

    is_low = chip < LOW

    def token_end(step):
        late = jnp.where(step >= chip, PIECES, 0)
        return jnp.where(is_low, late, jnp.clip(4 + 4 * step, 0, PIECES))

    def row_end(step):
        late = jnp.where(step >= chip, PIECES, 0)
        return jnp.where(is_low, late, jnp.clip(3 * step - 3, 0, PIECES))

    def token_side(step, before_token, before_row):
        end_token, end_row = token_end(step), row_end(step)

        def token_step(k, carry):
            token_part(k)
            return carry

        def row_step(k, carry):
            row_part(k)
            return carry

        lax.fori_loop(before_token, end_token, token_step, 0)

        @pl.when((before_row == 0) & (end_row > 0))
        def _():
            landed(rows_all.at[others], rows_recv)

        lax.fori_loop(before_row, end_row, row_step, 0)

        @pl.when((before_row < PIECES) & (end_row == PIECES))
        def _():
            settle()

    def stage(u, n, first):
        @pl.when(is_lower)
        def _():
            lower_stage(u, n)

        @pl.when(is_upper)
        def _():
            upper_stage(u, n, first)

    def collect_down(first, last):
        def body(i, carry):
            collect(first - i)
            return carry

        lax.fori_loop(0, jnp.maximum(first - last + 1, 0), body, 0)

    early = 4

    def advance(step, carry):
        @pl.when((step >= 1) & (step <= chip))
        def _():
            below = jnp.maximum(chip - step, 0)

            @pl.when(below >= ALONE)
            def _():
                stage(2 * below, 2, step == 1)

            @pl.when(below < ALONE)
            def _():
                def one(i, carry):
                    stage(2 * below + 1 - i, 1, (step == 1) & (i == 0))
                    return carry

                lax.fori_loop(0, 2, one, 0)

        before_token = jnp.where(step == 0, 0, token_end(step - 1))
        before_row = jnp.where(step == 0, 0, row_end(step - 1))
        token_side(step, before_token, before_row)

        @pl.when((step == n_chip - 3) & is_top)
        def _():
            collect_down(n_chip - 2, early)

        return carry

    lax.fori_loop(0, n_chip, advance, 0)

    @pl.when(is_upper)
    def _():
        own = layer - 1
        landed(hp_all.at[own], hp_recv.at[own])
        landed(a_all.at[others, pl.ds(own, 1)], a_recv.at[own])
        add(own)

    collect_down(jnp.where(is_top, early - 1, chip - 1), 0)

    row = lax.broadcasted_iota(jnp.int32, (8, tokens), 0)
    token = lax.broadcasted_iota(jnp.int32, (8, tokens), 1)
    members = jnp.where(token // SLOT == row, 1.0, 0.0)
    sums = lax.dot_general(
        members,
        total[...],
        (((1,), (1,)), ((), ())),
        precision=lax.Precision.HIGHEST,
        preferred_element_type=F32,
    )
    row = lax.broadcasted_iota(jnp.int32, (every, 128), 0)
    col = lax.broadcasted_iota(jnp.int32, (every, 128), 1)
    joined = jnp.where((row // group) * half + lax.rem(row, half) == col, 1.0, 0.0)
    s_all[layer] = jnp.dot(
        sums, joined, precision=lax.Precision.HIGHEST, preferred_element_type=F32
    )

    def s_copy(k):
        return pltpu.make_async_remote_copy(
            src_ref=s_all.at[layer],
            dst_ref=s_all.at[layer],
            send_sem=s_send.at[k],
            recv_sem=s_recv,
            device_id={"pipe": lax.rem(layer + k, n_pipe)},
            device_id_type=MESH,
        )

    for k in range(1, n_pipe):
        s_copy(k).start()

    landed(rows_all.at[others], rows_send)

    def sent_unit(u, n):
        rows = pl.ds(u, n)
        landed(a_all.at[others, rows], a_send.at[u])

        @pl.when(is_lower)
        def _():
            factor_copy(u, n).wait_send()
            for c in range(CHUNKS):
                pass_copy(u, n, c).wait_send()

        @pl.when(jnp.logical_not(is_top))
        def _():
            for c in range(CHUNKS):
                up_copy(u, n, c).wait_send()

    def sent_pair(below, carry):
        sent_unit(2 * below, 2)
        return carry

    def sent_one(u, carry):
        sent_unit(u, 1)
        return carry

    lax.fori_loop(ALONE, jnp.maximum(chip, ALONE), sent_pair, 0)
    lax.fori_loop(0, jnp.minimum(2 * ALONE, 2 * chip), sent_one, 0)

    @pl.when(is_lower)
    def _():
        for c in range(CHUNKS):
            own_copy(c).wait_send()
        hp_pass(layer).wait_send()

    @pl.when(is_lower & (chip > 0))
    def _():
        part_copy().wait_send()

    @pl.when(is_upper)
    def _():
        landed(a_all.at[others, pl.ds(layer - 1, 1)], a_send.at[layer - 1])

        @pl.when(chip > 0)
        def _():
            landed(k_all.at[others], k_send)

        @pl.when(jnp.logical_not(is_top))
        def _():
            for c in range(CHUNKS):

                @pl.when(pairs_up)
                def _():
                    up_copy(layer - 1, 2, c).wait_send()

                @pl.when(jnp.logical_not(pairs_up))
                def _():
                    up_copy(layer - 1, 1, c).wait_send()
                    up_copy(layer, 1, c).wait_send()

    for target in range(1, n_chip):

        @pl.when(chip < target)
        def _():
            hp_copy(target).wait_send()

        @pl.when(chip >= target)
        def _():
            hp_pass(2 * (target - 1) + core).wait_send()

    for k in range(1, n_pipe):
        s_copy(k).wait_send()
    arrived = s_all.at[pl.ds(0, n_pipe - 1)]
    pltpu.make_async_copy(arrived, arrived, s_recv).wait()
    result = s_all[0]
    for source in range(1, n_pipe):
        result = result + s_all[source]
    result = result[:n_example, :queries] * (ADAPTER_SCALE * SLOT**-0.5)
    example = lane * n_example + lax.broadcasted_iota(jnp.int32, (n_example, queries), 0)
    out_ref[...] = result * jnp.where(example != qe_ref[...], 1.0, 0.0)


def solution(mesh):
    n_dp, n_pipe = mesh.shape["dp"], mesh.shape["pipe"]

    def local(act, cot, down, expand, value, inputs, hidden_cols, inner_cols, lengths, query):
        tokens, width = cot.shape
        rank = down.shape[2]
        queries = hidden_cols.shape[1]
        n_example = tokens // SLOT
        group = 2 * value.shape[1]
        every = group * n_dp
        hbm = pl.BlockSpec(memory_space=pl.ANY)
        vmem = pl.BlockSpec(memory_space=pltpu.VMEM)
        dma = pltpu.SemaphoreType.DMA
        return pl.pallas_call(
            functools.partial(kernel, n_dp, n_pipe),
            out_shape=jax.ShapeDtypeStruct((n_example, queries), F32),
            in_specs=[hbm] * 10,
            out_specs=vmem,
            scratch_shapes=[
                pltpu.VMEM(value.shape, BF16),
                pltpu.VMEM(inputs.shape, BF16),
                pltpu.VMEM(hidden_cols.shape, BF16),
                pltpu.VMEM(inner_cols.shape, BF16),
                pltpu.VMEM((1, n_example), jnp.int32),
                pltpu.VMEM((1, queries), jnp.int32),
                pltpu.VMEM((PIECES, tokens, width // PIECES), BF16),
                pltpu.VMEM((PIECES, tokens, width // PIECES), BF16),
                pltpu.VMEM((width, rank), BF16),
                pltpu.VMEM((rank, width), BF16),
                pltpu.VMEM((n_pipe, group, width), BF16),
                pltpu.VMEM((n_pipe, group, width), BF16),
                pltpu.VMEM((n_pipe, group, width), BF16),
                pltpu.VMEM((n_dp, n_pipe, group, rank), BF16),
                pltpu.VMEM((n_pipe, group, rank), BF16),
                pltpu.VMEM((rank // n_dp, width), BF16),
                pltpu.VMEM((n_dp, rank // n_dp, rank), BF16),
                pltpu.VMEM((n_pipe, every, tokens), BF16),
                pltpu.VMEM((n_dp, group, width), BF16),
                pltpu.VMEM((rank, tokens), F32),
                pltpu.VMEM((rank, tokens), BF16),
                pltpu.VMEM((every, tokens), F32),
                pltpu.VMEM((every, tokens), F32),
                pltpu.VMEM((every, tokens), F32),
                pltpu.VMEM((n_pipe, 8, 128), F32),
                dma((6,)),
                dma((CHUNKS,)),
                dma((CHUNKS,)),
                dma((PIECES,)),
                dma((PIECES,)),
                dma,
                dma,
                dma((n_pipe, CHUNKS)),
                dma((n_pipe, CHUNKS)),
                dma((n_pipe, CHUNKS)),
                dma((n_pipe, CHUNKS)),
                dma((n_pipe,)),
                dma((n_pipe,)),
                dma,
                dma,
                dma,
                dma,
                dma((n_pipe,)),
                dma((n_pipe,)),
                dma((n_pipe // 2,)),
                dma((n_pipe,)),
                dma((n_pipe,)),
                dma((n_pipe,)),
                dma,
                pltpu.SemaphoreType.REGULAR,
            ],
            compiler_params=pltpu.CompilerParams(
                collective_id=0, has_side_effects=True, vmem_limit_bytes=58 << 20
            ),
            name="influence",
        )(
            act,
            cot,
            down,
            expand,
            value,
            inputs,
            hidden_cols,
            inner_cols,
            lengths.reshape(1, n_example),
            query.reshape(1, queries),
        )

    in_specs = (
        P("pipe", "dp", None),
        P("dp", None),
        P("pipe", None, None),
        P("pipe", None, None),
        P("pipe", "dp", None),
        P("pipe", "dp", None),
        P("pipe", None, None),
        P("pipe", None, None),
        P("dp"),
        P(),
    )
    return jax.shard_map(
        local, mesh=mesh, in_specs=in_specs, out_specs=P("dp", None), check_vma=False
    )
```

```python
import functools

import jax
import jax.numpy as jnp
from jax import lax
from jax.experimental import pallas as pl
from jax.experimental.pallas import tpu as pltpu
from jax.sharding import PartitionSpec as P

SLOT = 128
ADAPTER_SCALE = 0.25
MESH = pl.DeviceIdType.MESH
F32 = jnp.float32
BF16 = jnp.bfloat16
CHUNKS = 4
PIECES = 8
ALONE = 1
LOW = 3


def nt(a, b):
    return lax.dot_general(a, b, (((1,), (1,)), ((), ())), preferred_element_type=F32)


def kernel(
    n_dp,
    n_pipe,
    x_hbm,
    cot_hbm,
    d_hbm,
    e_hbm,
    v_hbm,
    i_hbm,
    hc_hbm,
    ic_hbm,
    len_hbm,
    qe_hbm,
    out_ref,
    v_ref,
    i_ref,
    hc_ref,
    ic_ref,
    len_ref,
    qe_ref,
    x_v,
    cot_v,
    d_v,
    e_v,
    z_in,
    y_in,
    sent,
    a_all,
    f_in,
    k_part,
    k_all,
    hp_all,
    rows_all,
    u_acc,
    u_bf,
    own_acc,
    hp_acc,
    total,
    s_all,
    load_small,
    load_e,
    load_d,
    load_cot,
    load_x,
    rows_send,
    rows_recv,
    main_send,
    pass_send,
    z_recv,
    y_recv,
    f_send,
    f_recv,
    part_send,
    part_recv,
    k_send,
    k_recv,
    a_send,
    a_recv,
    hp_send,
    pass_hp,
    hp_recv,
    s_send,
    s_recv,
    go_sem,
):
    lane = lax.axis_index("dp")
    layer = lax.axis_index("pipe")
    core = lax.rem(layer, 2)
    chip = layer // 2
    n_chip = n_pipe // 2
    is_top = chip == n_chip - 1
    width, rank = d_v.shape
    tokens = u_acc.shape[1]
    group = z_in.shape[1]
    half = group // 2
    queries = hc_ref.shape[1]
    every = group * n_dp
    share = rank // n_dp
    wide = width // CHUNKS
    piece = width // PIECES
    n_example = len_ref.shape[1]
    sibling = {"pipe": layer + 1 - 2 * core}
    above = {"pipe": lax.rem(2 * chip + 2, n_pipe)}

    def span(c):
        return slice(c * wide, (c + 1) * wide)

    def remote(src, dst, send_sem, recv_sem, device):
        return pltpu.make_async_remote_copy(
            src_ref=src,
            dst_ref=dst,
            send_sem=send_sem,
            recv_sem=recv_sem,
            device_id=device,
            device_id_type=MESH,
        )

    def landed(ref, sem):
        pltpu.make_async_copy(ref, ref, sem).wait()

    def load_expand(c):
        cols = pl.ds(c * wide, wide)
        return pltpu.make_async_copy(e_hbm.at[0, :, cols], e_v.at[:, cols], load_e.at[c])

    def load_down(c):
        rows = pl.ds(c * wide, wide)
        return pltpu.make_async_copy(d_hbm.at[0, rows, :], d_v.at[rows, :], load_d.at[c])

    def load_cotangent(k):
        cols = pl.ds(pl.multiple_of(k * piece, piece), piece)
        return pltpu.make_async_copy(cot_hbm.at[:, cols], cot_v.at[k], load_cot.at[k])

    def load_activation(k):
        cols = pl.ds(pl.multiple_of(k * piece, piece), piece)
        return pltpu.make_async_copy(x_hbm.at[0, :, cols], x_v.at[k], load_x.at[k])

    small = [
        pltpu.make_async_copy(src, dst, load_small.at[n])
        for n, (src, dst) in enumerate(
            (
                (ic_hbm, ic_ref),
                (v_hbm, v_ref),
                (i_hbm, i_ref),
                (hc_hbm, hc_ref),
                (len_hbm, len_ref),
                (qe_hbm, qe_ref),
            )
        )
    ]
    for copy in small:
        copy.start()
    is_lower = core == 0
    is_upper = core == 1

    @pl.when(is_lower)
    def _():
        for c in range(CHUNKS):
            load_expand(c).start()

    @pl.when(is_upper)
    def _():
        for c in range(CHUNKS):
            load_down(c).start()

    barrier = pltpu.get_barrier_semaphore()
    last = n_pipe - 1
    for k in range(1, n_dp):
        pl.semaphore_signal(
            barrier, 1, device_id={"dp": lax.rem(lane + k, n_dp)}, device_id_type=MESH
        )
    pl.semaphore_signal(barrier, 1, device_id=sibling, device_id_type=MESH)

    @pl.when((core == 0) & (chip > 0))
    def _():
        pl.semaphore_signal(
            barrier, 1, device_id={"pipe": jnp.maximum(layer - 1, 0)}, device_id_type=MESH
        )

    @pl.when(layer < last - 1)
    def _():
        pl.semaphore_signal(barrier, 1, device_id={"pipe": last}, device_id_type=MESH)

    waits_above = jnp.where((core == 1) & (layer < last), 1, 0)
    waits_column = jnp.where(layer == last, n_pipe - 2, 0)
    pl.semaphore_wait(barrier, n_dp + waits_above + waits_column)

    @pl.when(layer == last)
    def _():
        for target in range(last):
            pl.semaphore_signal(go_sem, 1, device_id={"pipe": target}, device_id_type=MESH)

    for copy in small:
        copy.wait()

    v_rows = v_ref[0].astype(F32)
    rows_all[lane] = jnp.concatenate([v_rows, i_ref[0].astype(F32)], axis=0).astype(BF16)

    def lane_at(k):
        return {"dp": lax.rem(lane + k, n_dp)}

    def spread_rows():
        for k in range(1, n_dp):
            remote(
                rows_all.at[lane], rows_all.at[lane], rows_send, rows_recv, lane_at(k)
            ).start()

    row = lax.broadcasted_iota(jnp.int32, (group, queries), 0)
    col = lax.broadcasted_iota(jnp.int32, (group, queries), 1)
    pick = jnp.where((row >= half) & (lane * half + row - half == col), 1.0, 0.0).astype(BF16)
    ic_lane = jnp.dot(pick, ic_ref[0], preferred_element_type=F32).astype(BF16)
    v_wide = jnp.concatenate([v_rows, jnp.zeros_like(v_rows)], axis=0)

    def own_copy(c):
        return remote(
            sent.at[layer, :, span(c)],
            z_in.at[layer, :, span(c)],
            main_send.at[layer, c],
            z_recv.at[layer, c],
            sibling,
        )

    def up_copy(u, n, c):
        rows = pl.ds(u, n)
        return remote(
            sent.at[rows, :, span(c)],
            z_in.at[rows, :, span(c)],
            main_send.at[u, c],
            z_recv.at[u, c],
            above,
        )

    def over_copy(u, n, c):
        rows = pl.ds(u, n)
        return remote(
            sent.at[rows, :, span(c)],
            y_in.at[rows, :, span(c)],
            main_send.at[u, c],
            y_recv.at[u, c],
            sibling,
        )

    def pass_copy(u, n, c):
        rows = pl.ds(u, n)
        return remote(
            z_in.at[rows, :, span(c)],
            z_in.at[rows, :, span(c)],
            pass_send.at[u, c],
            z_recv.at[u, c],
            sibling,
        )

    def factor_copy(u, n):
        rows = pl.ds(u, n)
        return remote(a_all.at[lane, rows], f_in.at[rows], f_send.at[u], f_recv.at[u], sibling)

    def spread_factors(u, n):
        rows = pl.ds(u, n)
        for k in range(1, n_dp):
            remote(
                a_all.at[lane, rows], a_all.at[lane, rows], a_send.at[u], a_recv.at[u], lane_at(k)
            ).start()

    others = pl.ds(0, n_dp - 1)

    def part_copy():
        return remote(
            e_hbm.at[0, pl.ds(pl.multiple_of(lane * share, share), share), :],
            k_part,
            part_send,
            part_recv,
            sibling,
        )

    pairs_up = chip >= ALONE

    @pl.when(is_lower & (chip > 0))
    def _():
        part_copy().start()

    is_low = chip < LOW

    def born(c):
        own = v_wide[:, span(c)] + jnp.dot(ic_lane, e_v[:, span(c)], preferred_element_type=F32)
        sent[layer, :, span(c)] = own.astype(BF16)

    @pl.when(is_lower)
    def _():
        for c in range(CHUNKS):
            load_expand(c).wait()
            load_down(c).start()
            born(c)
            own_copy(c).start()
        for c in range(CHUNKS):
            load_down(c).wait()

        @pl.when(jnp.logical_not(is_low))
        def _():
            spread_rows()

    def take(ref, u, n, c):
        return ref[pl.ds(u, n), :, span(c)].astype(F32).reshape(n * group, wide)

    def down(z, c):
        return jnp.dot(z.astype(BF16), d_v[span(c), :], preferred_element_type=F32)

    def up(factor, c):
        return jnp.dot(factor, e_v[:, span(c)], preferred_element_type=F32)

    def keep(u, n, projected):
        factor = ADAPTER_SCALE * projected
        a_all[lane, pl.ds(u, n)] = factor.reshape(n, group, rank).astype(BF16)
        return factor.astype(BF16)

    def put(u, n, c, moved):
        sent[pl.ds(u, n), :, span(c)] = moved.reshape(n, group, wide).astype(BF16)

    def lower_stage(u, n):
        projected = jnp.zeros((n * group, rank), F32)
        for c in range(CHUNKS):
            up_copy(u, n, c).wait_recv()
            pass_copy(u, n, c).start()
            projected += down(take(z_in, u, n, c), c)
        factor = keep(u, n, projected)
        factor_copy(u, n).start()

        @pl.when(jnp.logical_not(is_top))
        def _():
            for c in range(CHUNKS):
                put(u, n, c, take(z_in, u, n, c) + up(factor, c))
                over_copy(u, n, c).start()

        spread_factors(u, n)

    def upper_stage(u, n, first):
        projected = jnp.zeros((n * group, rank), F32)
        for c in range(CHUNKS):
            pass_copy(u, n, c).wait_recv()
            projected += down(take(z_in, u, n, c), c)
        factor_copy(u, n).wait_recv()

        @pl.when(first)
        def _():
            landed(k_all.at[others], k_recv)

        below = f_in[pl.ds(u, n)].astype(F32).reshape(n * group, rank).astype(BF16)
        projected += jnp.dot(below, k_all[...].reshape(rank, rank), preferred_element_type=F32)
        factor = keep(u, n, projected)

        @pl.when(jnp.logical_not(is_top))
        def _():
            for c in range(CHUNKS):
                over_copy(u, n, c).wait_recv()
                put(u, n, c, take(y_in, u, n, c) + up(factor, c))
                up_copy(u, n, c).start()

        spread_factors(u, n)

    @pl.when(is_upper)
    def _():
        u = layer - 1

        @pl.when(chip > 0)
        def _():
            landed(k_part, part_recv)
            coupled = jnp.zeros((share, rank), F32)
            for c in range(CHUNKS):
                load_down(c).wait()
                load_expand(c).start()
                coupled += jnp.dot(k_part[:, span(c)], d_v[span(c), :], preferred_element_type=F32)
            k_all[lane] = coupled.astype(BF16)
            for k in range(1, n_dp):
                remote(k_all.at[lane], k_all.at[lane], k_send, k_recv, lane_at(k)).start()

        @pl.when(chip == 0)
        def _():
            for c in range(CHUNKS):
                load_down(c).wait()
                load_expand(c).start()

        projected = jnp.zeros((group, rank), F32)
        for c in range(CHUNKS):
            landed(z_in.at[u, :, span(c)], z_recv.at[u, c])
            projected += down(take(z_in, u, 1, c), c)
        factor = keep(u, 1, projected)
        for c in range(CHUNKS):
            load_expand(c).wait()

            @pl.when(jnp.logical_not(is_top))
            def _():
                born(c)
                put(u, 1, c, take(z_in, u, 1, c) + up(factor, c))

                @pl.when(pairs_up)
                def _():
                    up_copy(u, 2, c).start()

                @pl.when(jnp.logical_not(pairs_up))
                def _():
                    up_copy(layer, 1, c).start()
                    up_copy(u, 1, c).start()

        spread_factors(u, 1)

        @pl.when(jnp.logical_not(is_low))
        def _():
            spread_rows()

    for k in range(PIECES):
        load_cotangent(k).start()
    for k in range(PIECES):
        load_activation(k).start()

    def placed(first):
        row = lax.broadcasted_iota(jnp.int32, (every, queries), 0)
        col = lax.broadcasted_iota(jnp.int32, (every, queries), 1)
        within = lax.rem(row, group) - first
        query = (row // group) * half + within
        hit = (within >= 0) & (within < half) & (query == col)
        return jnp.where(hit, 1.0, 0.0).astype(BF16)

    hc_placed = jnp.dot(placed(0), hc_ref[0], preferred_element_type=F32).astype(BF16)
    ic_placed = jnp.dot(placed(half), ic_ref[0], preferred_element_type=F32).astype(BF16)
    def token_part(k):
        load_cotangent(k).wait()
        cols = pl.ds(pl.multiple_of(k * piece, piece), piece)
        u_acc[...] += nt(e_v[:, cols], cot_v[k])

    def row_part(k):
        load_activation(k).wait()
        cols = pl.ds(pl.multiple_of(k * piece, piece), piece)
        gathered = rows_all[:, :, cols].astype(F32).reshape(every, piece)
        of_value = lax.rem(lax.broadcasted_iota(jnp.int32, (every, piece), 0), group) < half
        value_side = jnp.where(of_value, gathered, 0.0).astype(BF16)
        own_acc[...] += nt(value_side, cot_v[k])
        hidden_side = nt(hc_placed, d_v[cols, :])
        input_side = (hidden_side + jnp.where(of_value, 0.0, gathered)).astype(BF16)
        hp_acc[...] += nt(input_side, x_v[k])

    def hp_copy(target):
        return remote(
            hp_all.at[layer],
            hp_all.at[layer],
            hp_send.at[target],
            hp_recv.at[layer],
            {"pipe": 2 * target + core},
        )

    def hp_pass(source):
        return remote(
            hp_all.at[source], hp_all.at[source], pass_hp.at[source], hp_recv.at[source], sibling
        )

    def settle():
        token = lax.broadcasted_iota(jnp.int32, (every, tokens), 1)
        count = jnp.zeros((every, tokens), jnp.int32)
        for e in range(n_example):
            count = jnp.where(token // SLOT == e, len_ref[:, e : e + 1], count)
        live = jnp.where(lax.rem(token, SLOT) < count, 1.0, 0.0)
        hp_all[layer] = (hp_acc[...] * live).astype(BF16)

        @pl.when(layer < last)
        def _():
            pl.semaphore_wait(go_sem, 1)

        for target in range(1, n_chip):

            @pl.when(chip < target)
            def _():
                hp_copy(target).start()

        @pl.when(is_lower)
        def _():
            hp_pass(layer).start()

        u_bf[...] = u_acc[...].astype(BF16)
        own = own_acc[...] + jnp.dot(ic_placed, u_bf[...], preferred_element_type=F32)
        total[...] = own * hp_all[layer].astype(F32)

    def add(source):
        factors = a_all[:, source].astype(F32).reshape(every, rank).astype(BF16)
        total[...] += jnp.dot(factors, u_bf[...], preferred_element_type=F32) * hp_all[
            source
        ].astype(F32)

    def collect(below):
        mine, other = 2 * below + core, 2 * below + 1 - core
        landed(hp_all.at[mine], hp_recv.at[mine])
        hp_pass(mine).start()
        landed(hp_all.at[other], hp_recv.at[other])

        @pl.when(below >= ALONE)
        def _():
            landed(a_all.at[others, pl.ds(2 * below, 2)], a_recv.at[2 * below])

        @pl.when(below < ALONE)
        def _():
            landed(a_all.at[others, pl.ds(2 * below + 1, 1)], a_recv.at[2 * below + 1])

        add(2 * below + 1)

        @pl.when(below < ALONE)
        def _():
            landed(a_all.at[others, pl.ds(2 * below, 1)], a_recv.at[2 * below])

        add(2 * below)

    u_acc[...] = jnp.zeros_like(u_acc)
    own_acc[...] = jnp.zeros_like(own_acc)
    hp_acc[...] = jnp.zeros_like(hp_acc)
    hc_placed = jnp.dot(placed(0), hc_ref[0], preferred_element_type=F32).astype(BF16)
    ic_placed = jnp.dot(placed(half), ic_ref[0], preferred_element_type=F32).astype(BF16)

    def token_end(step):
        late = jnp.where(step >= chip, PIECES, 0)
        return jnp.where(is_low, late, jnp.clip(4 + 4 * step, 0, PIECES))

    def row_end(step):
        late = jnp.where(step >= chip, PIECES, 0)
        return jnp.where(is_low, late, jnp.clip(3 * step - 3, 0, PIECES))

    def token_side(step, before_token, before_row):
        end_token, end_row = token_end(step), row_end(step)

        @pl.when(is_low & (before_token == 0) & (end_token > 0))
        def _():
            spread_rows()

        def token_step(k, carry):
            token_part(k)
            return carry

        def row_step(k, carry):
            row_part(k)
            return carry

        lax.fori_loop(before_token, end_token, token_step, 0)

        @pl.when((before_row == 0) & (end_row > 0))
        def _():
            landed(rows_all.at[others], rows_recv)

        lax.fori_loop(before_row, end_row, row_step, 0)

        @pl.when((before_row < PIECES) & (end_row == PIECES))
        def _():
            settle()

    def stage(u, n, first):
        @pl.when(is_lower)
        def _():
            lower_stage(u, n)

        @pl.when(is_upper)
        def _():
            upper_stage(u, n, first)

    def collect_down(first, last):
        def body(i, carry):
            collect(first - i)
            return carry

        lax.fori_loop(0, jnp.maximum(first - last + 1, 0), body, 0)

    early = 4

    def advance(step, carry):
        @pl.when((step >= 1) & (step <= chip))
        def _():
            below = jnp.maximum(chip - step, 0)

            @pl.when(below >= ALONE)
            def _():
                stage(2 * below, 2, step == 1)

            @pl.when(below < ALONE)
            def _():
                def one(i, carry):
                    stage(2 * below + 1 - i, 1, (step == 1) & (i == 0))
                    return carry

                lax.fori_loop(0, 2, one, 0)

        before_token = jnp.where(step == 0, 0, token_end(step - 1))
        before_row = jnp.where(step == 0, 0, row_end(step - 1))
        token_side(step, before_token, before_row)

        @pl.when((step == n_chip - 3) & is_top)
        def _():
            collect_down(n_chip - 2, early)

        return carry

    lax.fori_loop(0, n_chip, advance, 0)

    @pl.when(is_upper)
    def _():
        own = layer - 1
        landed(hp_all.at[own], hp_recv.at[own])
        landed(a_all.at[others, pl.ds(own, 1)], a_recv.at[own])
        add(own)

    collect_down(jnp.where(is_top, early - 1, chip - 1), 0)

    row = lax.broadcasted_iota(jnp.int32, (8, tokens), 0)
    token = lax.broadcasted_iota(jnp.int32, (8, tokens), 1)
    members = jnp.where(token // SLOT == row, 1.0, 0.0)
    sums = lax.dot_general(
        members,
        total[...],
        (((1,), (1,)), ((), ())),
        precision=lax.Precision.HIGHEST,
        preferred_element_type=F32,
    )
    row = lax.broadcasted_iota(jnp.int32, (every, 128), 0)
    col = lax.broadcasted_iota(jnp.int32, (every, 128), 1)
    joined = jnp.where((row // group) * half + lax.rem(row, half) == col, 1.0, 0.0)
    s_all[layer] = jnp.dot(
        sums, joined, precision=lax.Precision.HIGHEST, preferred_element_type=F32
    )

    def s_copy(k):
        return pltpu.make_async_remote_copy(
            src_ref=s_all.at[layer],
            dst_ref=s_all.at[layer],
            send_sem=s_send.at[k],
            recv_sem=s_recv,
            device_id={"pipe": lax.rem(layer + k, n_pipe)},
            device_id_type=MESH,
        )

    for k in range(1, n_pipe):
        s_copy(k).start()

    landed(rows_all.at[others], rows_send)

    def sent_unit(u, n):
        rows = pl.ds(u, n)
        landed(a_all.at[others, rows], a_send.at[u])

        @pl.when(is_lower)
        def _():
            factor_copy(u, n).wait_send()
            for c in range(CHUNKS):
                pass_copy(u, n, c).wait_send()

        @pl.when(jnp.logical_not(is_top))
        def _():
            for c in range(CHUNKS):
                up_copy(u, n, c).wait_send()

    def sent_pair(below, carry):
        sent_unit(2 * below, 2)
        return carry

    def sent_one(u, carry):
        sent_unit(u, 1)
        return carry

    lax.fori_loop(ALONE, jnp.maximum(chip, ALONE), sent_pair, 0)
    lax.fori_loop(0, jnp.minimum(2 * ALONE, 2 * chip), sent_one, 0)

    @pl.when(is_lower)
    def _():
        for c in range(CHUNKS):
            own_copy(c).wait_send()
        hp_pass(layer).wait_send()

    @pl.when(is_lower & (chip > 0))
    def _():
        part_copy().wait_send()

    @pl.when(is_upper)
    def _():
        landed(a_all.at[others, pl.ds(layer - 1, 1)], a_send.at[layer - 1])

        @pl.when(chip > 0)
        def _():
            landed(k_all.at[others], k_send)

        @pl.when(jnp.logical_not(is_top))
        def _():
            for c in range(CHUNKS):

                @pl.when(pairs_up)
                def _():
                    up_copy(layer - 1, 2, c).wait_send()

                @pl.when(jnp.logical_not(pairs_up))
                def _():
                    up_copy(layer - 1, 1, c).wait_send()
                    up_copy(layer, 1, c).wait_send()

    for target in range(1, n_chip):

        @pl.when(chip < target)
        def _():
            hp_copy(target).wait_send()

        @pl.when(chip >= target)
        def _():
            hp_pass(2 * (target - 1) + core).wait_send()

    for k in range(1, n_pipe):
        s_copy(k).wait_send()
    arrived = s_all.at[pl.ds(0, n_pipe - 1)]
    pltpu.make_async_copy(arrived, arrived, s_recv).wait()
    result = s_all[0]
    for source in range(1, n_pipe):
        result = result + s_all[source]
    result = result[:n_example, :queries] * (ADAPTER_SCALE * SLOT**-0.5)
    example = lane * n_example + lax.broadcasted_iota(jnp.int32, (n_example, queries), 0)
    out_ref[...] = result * jnp.where(example != qe_ref[...], 1.0, 0.0)


def solution(mesh):
    n_dp, n_pipe = mesh.shape["dp"], mesh.shape["pipe"]

    def local(act, cot, down, expand, value, inputs, hidden_cols, inner_cols, lengths, query):
        tokens, width = cot.shape
        rank = down.shape[2]
        queries = hidden_cols.shape[1]
        n_example = tokens // SLOT
        group = 2 * value.shape[1]
        every = group * n_dp
        hbm = pl.BlockSpec(memory_space=pl.ANY)
        vmem = pl.BlockSpec(memory_space=pltpu.VMEM)
        dma = pltpu.SemaphoreType.DMA
        return pl.pallas_call(
            functools.partial(kernel, n_dp, n_pipe),
            out_shape=jax.ShapeDtypeStruct((n_example, queries), F32),
            in_specs=[hbm] * 10,
            out_specs=vmem,
            scratch_shapes=[
                pltpu.VMEM(value.shape, BF16),
                pltpu.VMEM(inputs.shape, BF16),
                pltpu.VMEM(hidden_cols.shape, BF16),
                pltpu.VMEM(inner_cols.shape, BF16),
                pltpu.VMEM((1, n_example), jnp.int32),
                pltpu.VMEM((1, queries), jnp.int32),
                pltpu.VMEM((PIECES, tokens, width // PIECES), BF16),
                pltpu.VMEM((PIECES, tokens, width // PIECES), BF16),
                pltpu.VMEM((width, rank), BF16),
                pltpu.VMEM((rank, width), BF16),
                pltpu.VMEM((n_pipe, group, width), BF16),
                pltpu.VMEM((n_pipe, group, width), BF16),
                pltpu.VMEM((n_pipe, group, width), BF16),
                pltpu.VMEM((n_dp, n_pipe, group, rank), BF16),
                pltpu.VMEM((n_pipe, group, rank), BF16),
                pltpu.VMEM((rank // n_dp, width), BF16),
                pltpu.VMEM((n_dp, rank // n_dp, rank), BF16),
                pltpu.VMEM((n_pipe, every, tokens), BF16),
                pltpu.VMEM((n_dp, group, width), BF16),
                pltpu.VMEM((rank, tokens), F32),
                pltpu.VMEM((rank, tokens), BF16),
                pltpu.VMEM((every, tokens), F32),
                pltpu.VMEM((every, tokens), F32),
                pltpu.VMEM((every, tokens), F32),
                pltpu.VMEM((n_pipe, 8, 128), F32),
                dma((6,)),
                dma((CHUNKS,)),
                dma((CHUNKS,)),
                dma((PIECES,)),
                dma((PIECES,)),
                dma,
                dma,
                dma((n_pipe, CHUNKS)),
                dma((n_pipe, CHUNKS)),
                dma((n_pipe, CHUNKS)),
                dma((n_pipe, CHUNKS)),
                dma((n_pipe,)),
                dma((n_pipe,)),
                dma,
                dma,
                dma,
                dma,
                dma((n_pipe,)),
                dma((n_pipe,)),
                dma((n_pipe // 2,)),
                dma((n_pipe,)),
                dma((n_pipe,)),
                dma((n_pipe,)),
                dma,
                pltpu.SemaphoreType.REGULAR,
            ],
            compiler_params=pltpu.CompilerParams(
                collective_id=0, has_side_effects=True, vmem_limit_bytes=58 << 20
            ),
            name="influence",
        )(
            act,
            cot,
            down,
            expand,
            value,
            inputs,
            hidden_cols,
            inner_cols,
            lengths.reshape(1, n_example),
            query.reshape(1, queries),
        )

    in_specs = (
        P("pipe", "dp", None),
        P("dp", None),
        P("pipe", None, None),
        P("pipe", None, None),
        P("pipe", "dp", None),
        P("pipe", "dp", None),
        P("pipe", None, None),
        P("pipe", None, None),
        P("dp"),
        P(),
    )
    return jax.shard_map(
        local, mesh=mesh, in_specs=in_specs, out_specs=P("dp", None), check_vma=False
    )
```

```python
import functools

import jax
import jax.numpy as jnp
from jax import lax
from jax.experimental import pallas as pl
from jax.experimental.pallas import tpu as pltpu
from jax.sharding import PartitionSpec as P

SLOT = 128
ADAPTER_SCALE = 0.25
MESH = pl.DeviceIdType.MESH
F32 = jnp.float32
BF16 = jnp.bfloat16
CHUNKS = 4
PIECES = 8
ALONE = 1
LOW = 3


def nt(a, b):
    return lax.dot_general(a, b, (((1,), (1,)), ((), ())), preferred_element_type=F32)


def kernel(
    n_dp,
    n_pipe,
    x_hbm,
    cot_hbm,
    d_hbm,
    e_hbm,
    v_hbm,
    i_hbm,
    hc_hbm,
    ic_hbm,
    len_hbm,
    qe_hbm,
    out_ref,
    v_ref,
    i_ref,
    hc_ref,
    ic_ref,
    len_ref,
    qe_ref,
    x_v,
    cot_v,
    d_v,
    e_v,
    z_in,
    y_in,
    sent,
    a_all,
    f_in,
    k_part,
    k_all,
    hp_all,
    rows_all,
    u_acc,
    u_bf,
    own_acc,
    hp_acc,
    total,
    s_all,
    load_small,
    load_e,
    load_d,
    load_cot,
    load_x,
    rows_send,
    rows_recv,
    main_send,
    pass_send,
    z_recv,
    y_recv,
    f_send,
    f_recv,
    part_send,
    part_recv,
    k_send,
    k_recv,
    a_send,
    a_recv,
    hp_send,
    pass_hp,
    hp_recv,
    s_send,
    s_recv,
    go_sem,
):
    lane = lax.axis_index("dp")
    layer = lax.axis_index("pipe")
    core = lax.rem(layer, 2)
    chip = layer // 2
    n_chip = n_pipe // 2
    is_top = chip == n_chip - 1
    width, rank = d_v.shape
    tokens = u_acc.shape[1]
    group = z_in.shape[1]
    half = group // 2
    queries = hc_ref.shape[1]
    every = group * n_dp
    share = rank // n_dp
    wide = width // CHUNKS
    piece = width // PIECES
    n_example = len_ref.shape[1]
    sibling = {"pipe": layer + 1 - 2 * core}
    above = {"pipe": lax.rem(2 * chip + 2, n_pipe)}

    def span(c):
        return slice(c * wide, (c + 1) * wide)

    def remote(src, dst, send_sem, recv_sem, device):
        return pltpu.make_async_remote_copy(
            src_ref=src,
            dst_ref=dst,
            send_sem=send_sem,
            recv_sem=recv_sem,
            device_id=device,
            device_id_type=MESH,
        )

    def landed(ref, sem):
        pltpu.make_async_copy(ref, ref, sem).wait()

    def load_expand(c):
        cols = pl.ds(c * wide, wide)
        return pltpu.make_async_copy(e_hbm.at[0, :, cols], e_v.at[:, cols], load_e.at[c])

    def load_down(c):
        rows = pl.ds(c * wide, wide)
        return pltpu.make_async_copy(d_hbm.at[0, rows, :], d_v.at[rows, :], load_d.at[c])

    def load_cotangent(k):
        cols = pl.ds(pl.multiple_of(k * piece, piece), piece)
        return pltpu.make_async_copy(cot_hbm.at[:, cols], cot_v.at[k], load_cot.at[k])

    def load_activation(k):
        cols = pl.ds(pl.multiple_of(k * piece, piece), piece)
        return pltpu.make_async_copy(x_hbm.at[0, :, cols], x_v.at[k], load_x.at[k])

    small = [
        pltpu.make_async_copy(src, dst, load_small.at[n])
        for n, (src, dst) in enumerate(
            (
                (ic_hbm, ic_ref),
                (v_hbm, v_ref),
                (i_hbm, i_ref),
                (hc_hbm, hc_ref),
                (len_hbm, len_ref),
                (qe_hbm, qe_ref),
            )
        )
    ]
    for copy in small:
        copy.start()
    is_lower = core == 0
    is_upper = core == 1

    @pl.when(is_lower)
    def _():
        for c in range(CHUNKS):
            load_expand(c).start()

    @pl.when(is_upper)
    def _():
        for c in range(CHUNKS):
            load_down(c).start()

    barrier = pltpu.get_barrier_semaphore()
    last = n_pipe - 1
    for k in range(1, n_dp):
        pl.semaphore_signal(
            barrier, 1, device_id={"dp": lax.rem(lane + k, n_dp)}, device_id_type=MESH
        )
    pl.semaphore_signal(barrier, 1, device_id=sibling, device_id_type=MESH)

    @pl.when((core == 0) & (chip > 0))
    def _():
        pl.semaphore_signal(
            barrier, 1, device_id={"pipe": jnp.maximum(layer - 1, 0)}, device_id_type=MESH
        )

    @pl.when(layer < last - 1)
    def _():
        pl.semaphore_signal(barrier, 1, device_id={"pipe": last}, device_id_type=MESH)

    waits_above = jnp.where((core == 1) & (layer < last), 1, 0)
    waits_column = jnp.where(layer == last, n_pipe - 2, 0)
    pl.semaphore_wait(barrier, n_dp + waits_above + waits_column)

    @pl.when(layer == last)
    def _():
        for target in range(last):
            pl.semaphore_signal(go_sem, 1, device_id={"pipe": target}, device_id_type=MESH)

    for copy in small:
        copy.wait()

    v_rows = v_ref[0].astype(F32)
    rows_all[lane] = jnp.concatenate([v_rows, i_ref[0].astype(F32)], axis=0).astype(BF16)

    def lane_at(k):
        return {"dp": lax.rem(lane + k, n_dp)}

    def spread_rows():
        for k in range(1, n_dp):
            remote(
                rows_all.at[lane], rows_all.at[lane], rows_send, rows_recv, lane_at(k)
            ).start()

    row = lax.broadcasted_iota(jnp.int32, (group, queries), 0)
    col = lax.broadcasted_iota(jnp.int32, (group, queries), 1)
    pick = jnp.where((row >= half) & (lane * half + row - half == col), 1.0, 0.0).astype(BF16)
    ic_lane = jnp.dot(pick, ic_ref[0], preferred_element_type=F32).astype(BF16)
    v_wide = jnp.concatenate([v_rows, jnp.zeros_like(v_rows)], axis=0)

    def own_copy(c):
        return remote(
            sent.at[layer, :, span(c)],
            z_in.at[layer, :, span(c)],
            main_send.at[layer, c],
            z_recv.at[layer, c],
            sibling,
        )

    def up_copy(u, n, c):
        rows = pl.ds(u, n)
        return remote(
            sent.at[rows, :, span(c)],
            z_in.at[rows, :, span(c)],
            main_send.at[u, c],
            z_recv.at[u, c],
            above,
        )

    def over_copy(u, n, c):
        rows = pl.ds(u, n)
        return remote(
            sent.at[rows, :, span(c)],
            y_in.at[rows, :, span(c)],
            main_send.at[u, c],
            y_recv.at[u, c],
            sibling,
        )

    def pass_copy(u, n, c):
        rows = pl.ds(u, n)
        return remote(
            z_in.at[rows, :, span(c)],
            z_in.at[rows, :, span(c)],
            pass_send.at[u, c],
            z_recv.at[u, c],
            sibling,
        )

    def factor_copy(u, n):
        rows = pl.ds(u, n)
        return remote(a_all.at[lane, rows], f_in.at[rows], f_send.at[u], f_recv.at[u], sibling)

    def spread_factors(u, n):
        rows = pl.ds(u, n)
        for k in range(1, n_dp):
            remote(
                a_all.at[lane, rows], a_all.at[lane, rows], a_send.at[u], a_recv.at[u], lane_at(k)
            ).start()

    others = pl.ds(0, n_dp - 1)

    def part_copy():
        return remote(
            e_hbm.at[0, pl.ds(pl.multiple_of(lane * share, share), share), :],
            k_part,
            part_send,
            part_recv,
            sibling,
        )

    pairs_up = chip >= ALONE

    @pl.when(is_lower & (chip > 0))
    def _():
        part_copy().start()

    def born(c):
        own = v_wide[:, span(c)] + jnp.dot(ic_lane, e_v[:, span(c)], preferred_element_type=F32)
        sent[layer, :, span(c)] = own.astype(BF16)

    @pl.when(is_lower)
    def _():
        for c in range(CHUNKS):
            load_expand(c).wait()
            load_down(c).start()
            born(c)
            own_copy(c).start()
        spread_rows()
        for c in range(CHUNKS):
            load_down(c).wait()

    def take(ref, u, n, c):
        return ref[pl.ds(u, n), :, span(c)].astype(F32).reshape(n * group, wide)

    def down(z, c):
        return jnp.dot(z.astype(BF16), d_v[span(c), :], preferred_element_type=F32)

    def up(factor, c):
        return jnp.dot(factor, e_v[:, span(c)], preferred_element_type=F32)

    def keep(u, n, projected):
        factor = ADAPTER_SCALE * projected
        a_all[lane, pl.ds(u, n)] = factor.reshape(n, group, rank).astype(BF16)
        return factor.astype(BF16)

    def put(u, n, c, moved):
        sent[pl.ds(u, n), :, span(c)] = moved.reshape(n, group, wide).astype(BF16)

    def lower_stage(u, n):
        projected = jnp.zeros((n * group, rank), F32)
        for c in range(CHUNKS):
            up_copy(u, n, c).wait_recv()
            pass_copy(u, n, c).start()
            projected += down(take(z_in, u, n, c), c)
        factor = keep(u, n, projected)
        factor_copy(u, n).start()

        @pl.when(jnp.logical_not(is_top))
        def _():
            for c in range(CHUNKS):
                put(u, n, c, take(z_in, u, n, c) + up(factor, c))
                over_copy(u, n, c).start()

        spread_factors(u, n)

    def upper_stage(u, n, first):
        projected = jnp.zeros((n * group, rank), F32)
        for c in range(CHUNKS):
            pass_copy(u, n, c).wait_recv()
            projected += down(take(z_in, u, n, c), c)
        factor_copy(u, n).wait_recv()

        @pl.when(first)
        def _():
            landed(k_all.at[others], k_recv)

        below = f_in[pl.ds(u, n)].astype(F32).reshape(n * group, rank).astype(BF16)
        projected += jnp.dot(below, k_all[...].reshape(rank, rank), preferred_element_type=F32)
        factor = keep(u, n, projected)

        @pl.when(jnp.logical_not(is_top))
        def _():
            for c in range(CHUNKS):
                over_copy(u, n, c).wait_recv()
                put(u, n, c, take(y_in, u, n, c) + up(factor, c))
                up_copy(u, n, c).start()

        spread_factors(u, n)

    @pl.when(is_upper)
    def _():
        u = layer - 1

        @pl.when(chip > 0)
        def _():
            landed(k_part, part_recv)
            coupled = jnp.zeros((share, rank), F32)
            for c in range(CHUNKS):
                load_down(c).wait()
                load_expand(c).start()
                coupled += jnp.dot(k_part[:, span(c)], d_v[span(c), :], preferred_element_type=F32)
            k_all[lane] = coupled.astype(BF16)
            for k in range(1, n_dp):
                remote(k_all.at[lane], k_all.at[lane], k_send, k_recv, lane_at(k)).start()

        @pl.when(chip == 0)
        def _():
            for c in range(CHUNKS):
                load_down(c).wait()
                load_expand(c).start()

        projected = jnp.zeros((group, rank), F32)
        for c in range(CHUNKS):
            landed(z_in.at[u, :, span(c)], z_recv.at[u, c])
            projected += down(take(z_in, u, 1, c), c)
        factor = keep(u, 1, projected)
        for c in range(CHUNKS):
            load_expand(c).wait()

            @pl.when(jnp.logical_not(is_top))
            def _():
                born(c)
                put(u, 1, c, take(z_in, u, 1, c) + up(factor, c))

                @pl.when(pairs_up)
                def _():
                    up_copy(u, 2, c).start()

                @pl.when(jnp.logical_not(pairs_up))
                def _():
                    up_copy(layer, 1, c).start()
                    up_copy(u, 1, c).start()

        spread_factors(u, 1)
        spread_rows()

    for k in range(PIECES):
        load_cotangent(k).start()
    for k in range(PIECES):
        load_activation(k).start()

    def placed(first):
        row = lax.broadcasted_iota(jnp.int32, (every, queries), 0)
        col = lax.broadcasted_iota(jnp.int32, (every, queries), 1)
        within = lax.rem(row, group) - first
        query = (row // group) * half + within
        hit = (within >= 0) & (within < half) & (query == col)
        return jnp.where(hit, 1.0, 0.0).astype(BF16)

    hc_placed = jnp.dot(placed(0), hc_ref[0], preferred_element_type=F32).astype(BF16)
    ic_placed = jnp.dot(placed(half), ic_ref[0], preferred_element_type=F32).astype(BF16)
    def token_part(k):
        load_cotangent(k).wait()
        cols = pl.ds(pl.multiple_of(k * piece, piece), piece)
        u_acc[...] += nt(e_v[:, cols], cot_v[k])

    def row_part(k):
        load_activation(k).wait()
        cols = pl.ds(pl.multiple_of(k * piece, piece), piece)
        gathered = rows_all[:, :, cols].astype(F32).reshape(every, piece)
        of_value = lax.rem(lax.broadcasted_iota(jnp.int32, (every, piece), 0), group) < half
        value_side = jnp.where(of_value, gathered, 0.0).astype(BF16)
        own_acc[...] += nt(value_side, cot_v[k])
        hidden_side = nt(hc_placed, d_v[cols, :])
        input_side = (hidden_side + jnp.where(of_value, 0.0, gathered)).astype(BF16)
        hp_acc[...] += nt(input_side, x_v[k])

    def hp_copy(target):
        return remote(
            hp_all.at[layer],
            hp_all.at[layer],
            hp_send.at[target],
            hp_recv.at[layer],
            {"pipe": 2 * target + core},
        )

    def hp_pass(source):
        return remote(
            hp_all.at[source], hp_all.at[source], pass_hp.at[source], hp_recv.at[source], sibling
        )

    def settle():
        token = lax.broadcasted_iota(jnp.int32, (every, tokens), 1)
        count = jnp.zeros((every, tokens), jnp.int32)
        for e in range(n_example):
            count = jnp.where(token // SLOT == e, len_ref[:, e : e + 1], count)
        live = jnp.where(lax.rem(token, SLOT) < count, 1.0, 0.0)
        hp_all[layer] = (hp_acc[...] * live).astype(BF16)

        @pl.when(layer < last)
        def _():
            pl.semaphore_wait(go_sem, 1)

        for target in range(1, n_chip):

            @pl.when(chip < target)
            def _():
                hp_copy(target).start()

        @pl.when(is_lower)
        def _():
            hp_pass(layer).start()

        u_bf[...] = u_acc[...].astype(BF16)
        own = own_acc[...] + jnp.dot(ic_placed, u_bf[...], preferred_element_type=F32)
        total[...] = own * hp_all[layer].astype(F32)

    def add(source):
        factors = a_all[:, source].astype(F32).reshape(every, rank).astype(BF16)
        total[...] += jnp.dot(factors, u_bf[...], preferred_element_type=F32) * hp_all[
            source
        ].astype(F32)

    def collect(below):
        mine, other = 2 * below + core, 2 * below + 1 - core
        landed(hp_all.at[mine], hp_recv.at[mine])
        hp_pass(mine).start()
        landed(hp_all.at[other], hp_recv.at[other])

        @pl.when(below >= ALONE)
        def _():
            landed(a_all.at[others, pl.ds(2 * below, 2)], a_recv.at[2 * below])

        @pl.when(below < ALONE)
        def _():
            landed(a_all.at[others, pl.ds(2 * below + 1, 1)], a_recv.at[2 * below + 1])

        add(2 * below + 1)

        @pl.when(below < ALONE)
        def _():
            landed(a_all.at[others, pl.ds(2 * below, 1)], a_recv.at[2 * below])

        add(2 * below)

    u_acc[...] = jnp.zeros_like(u_acc)
    own_acc[...] = jnp.zeros_like(own_acc)
    hp_acc[...] = jnp.zeros_like(hp_acc)
    hc_placed = jnp.dot(placed(0), hc_ref[0], preferred_element_type=F32).astype(BF16)
    ic_placed = jnp.dot(placed(half), ic_ref[0], preferred_element_type=F32).astype(BF16)

    is_low = chip < LOW

    def token_end(step):
        late = jnp.where(step >= chip, PIECES, 0)
        return jnp.where(is_low, late, jnp.clip(4 + 4 * step, 0, PIECES))

    def row_end(step):
        late = jnp.where(step >= chip, PIECES, 0)
        return jnp.where(is_low, late, jnp.clip(3 * step - 3, 0, PIECES))

    def token_side(step, before_token, before_row):
        end_token, end_row = token_end(step), row_end(step)

        def token_step(k, carry):
            token_part(k)
            return carry

        def row_step(k, carry):
            row_part(k)
            return carry

        lax.fori_loop(before_token, end_token, token_step, 0)

        @pl.when((before_row == 0) & (end_row > 0))
        def _():
            landed(rows_all.at[others], rows_recv)

        lax.fori_loop(before_row, end_row, row_step, 0)

        @pl.when((before_row < PIECES) & (end_row == PIECES))
        def _():
            settle()

    def stage(u, n, first):
        @pl.when(is_lower)
        def _():
            lower_stage(u, n)

        @pl.when(is_upper)
        def _():
            upper_stage(u, n, first)

    def collect_down(first, last):
        def body(i, carry):
            collect(first - i)
            return carry

        lax.fori_loop(0, jnp.maximum(first - last + 1, 0), body, 0)

    early = 4

    def advance(step, carry):
        @pl.when((step >= 1) & (step <= chip))
        def _():
            below = jnp.maximum(chip - step, 0)

            @pl.when(below >= ALONE)
            def _():
                stage(2 * below, 2, step == 1)

            @pl.when(below < ALONE)
            def _():
                def one(i, carry):
                    stage(2 * below + 1 - i, 1, (step == 1) & (i == 0))
                    return carry

                lax.fori_loop(0, 2, one, 0)

        before_token = jnp.where(step == 0, 0, token_end(step - 1))
        before_row = jnp.where(step == 0, 0, row_end(step - 1))
        token_side(step, before_token, before_row)

        @pl.when((step == n_chip - 3) & is_top)
        def _():
            collect_down(n_chip - 2, early)

        return carry

    lax.fori_loop(0, n_chip, advance, 0)

    @pl.when(is_upper)
    def _():
        own = layer - 1
        landed(hp_all.at[own], hp_recv.at[own])
        landed(a_all.at[others, pl.ds(own, 1)], a_recv.at[own])
        add(own)

    collect_down(jnp.where(is_top, early - 1, chip - 1), 0)

    row = lax.broadcasted_iota(jnp.int32, (8, tokens), 0)
    token = lax.broadcasted_iota(jnp.int32, (8, tokens), 1)
    members = jnp.where(token // SLOT == row, 1.0, 0.0)
    sums = lax.dot_general(
        members,
        total[...],
        (((1,), (1,)), ((), ())),
        precision=lax.Precision.HIGHEST,
        preferred_element_type=F32,
    )
    row = lax.broadcasted_iota(jnp.int32, (every, 128), 0)
    col = lax.broadcasted_iota(jnp.int32, (every, 128), 1)
    joined = jnp.where((row // group) * half + lax.rem(row, half) == col, 1.0, 0.0)
    s_all[layer] = jnp.dot(
        sums, joined, precision=lax.Precision.HIGHEST, preferred_element_type=F32
    )

    def s_copy(k):
        return pltpu.make_async_remote_copy(
            src_ref=s_all.at[layer],
            dst_ref=s_all.at[layer],
            send_sem=s_send.at[k],
            recv_sem=s_recv,
            device_id={"pipe": lax.rem(layer + k, n_pipe)},
            device_id_type=MESH,
        )

    for k in range(1, n_pipe):
        s_copy(k).start()

    landed(rows_all.at[others], rows_send)

    def sent_unit(u, n):
        rows = pl.ds(u, n)
        landed(a_all.at[others, rows], a_send.at[u])

        @pl.when(is_lower)
        def _():
            factor_copy(u, n).wait_send()
            for c in range(CHUNKS):
                pass_copy(u, n, c).wait_send()

        @pl.when(jnp.logical_not(is_top))
        def _():
            for c in range(CHUNKS):
                up_copy(u, n, c).wait_send()

    def sent_pair(below, carry):
        sent_unit(2 * below, 2)
        return carry

    def sent_one(u, carry):
        sent_unit(u, 1)
        return carry

    lax.fori_loop(ALONE, jnp.maximum(chip, ALONE), sent_pair, 0)
    lax.fori_loop(0, jnp.minimum(2 * ALONE, 2 * chip), sent_one, 0)

    @pl.when(is_lower)
    def _():
        for c in range(CHUNKS):
            own_copy(c).wait_send()
        hp_pass(layer).wait_send()

    @pl.when(is_lower & (chip > 0))
    def _():
        part_copy().wait_send()

    @pl.when(is_upper)
    def _():
        landed(a_all.at[others, pl.ds(layer - 1, 1)], a_send.at[layer - 1])

        @pl.when(chip > 0)
        def _():
            landed(k_all.at[others], k_send)

        @pl.when(jnp.logical_not(is_top))
        def _():
            for c in range(CHUNKS):

                @pl.when(pairs_up)
                def _():
                    up_copy(layer - 1, 2, c).wait_send()

                @pl.when(jnp.logical_not(pairs_up))
                def _():
                    up_copy(layer - 1, 1, c).wait_send()
                    up_copy(layer, 1, c).wait_send()

    for target in range(1, n_chip):

        @pl.when(chip < target)
        def _():
            hp_copy(target).wait_send()

        @pl.when(chip >= target)
        def _():
            hp_pass(2 * (target - 1) + core).wait_send()

    for k in range(1, n_pipe):
        s_copy(k).wait_send()
    arrived = s_all.at[pl.ds(0, n_pipe - 1)]
    pltpu.make_async_copy(arrived, arrived, s_recv).wait()
    result = s_all[0]
    for source in range(1, n_pipe):
        result = result + s_all[source]
    result = result[:n_example, :queries] * (ADAPTER_SCALE * SLOT**-0.5)
    example = lane * n_example + lax.broadcasted_iota(jnp.int32, (n_example, queries), 0)
    out_ref[...] = result * jnp.where(example != qe_ref[...], 1.0, 0.0)


def solution(mesh):
    n_dp, n_pipe = mesh.shape["dp"], mesh.shape["pipe"]

    def local(act, cot, down, expand, value, inputs, hidden_cols, inner_cols, lengths, query):
        tokens, width = cot.shape
        rank = down.shape[2]
        queries = hidden_cols.shape[1]
        n_example = tokens // SLOT
        group = 2 * value.shape[1]
        every = group * n_dp
        hbm = pl.BlockSpec(memory_space=pl.ANY)
        vmem = pl.BlockSpec(memory_space=pltpu.VMEM)
        dma = pltpu.SemaphoreType.DMA
        return pl.pallas_call(
            functools.partial(kernel, n_dp, n_pipe),
            out_shape=jax.ShapeDtypeStruct((n_example, queries), F32),
            in_specs=[hbm] * 10,
            out_specs=vmem,
            scratch_shapes=[
                pltpu.VMEM(value.shape, BF16),
                pltpu.VMEM(inputs.shape, BF16),
                pltpu.VMEM(hidden_cols.shape, BF16),
                pltpu.VMEM(inner_cols.shape, BF16),
                pltpu.VMEM((1, n_example), jnp.int32),
                pltpu.VMEM((1, queries), jnp.int32),
                pltpu.VMEM((PIECES, tokens, width // PIECES), BF16),
                pltpu.VMEM((PIECES, tokens, width // PIECES), BF16),
                pltpu.VMEM((width, rank), BF16),
                pltpu.VMEM((rank, width), BF16),
                pltpu.VMEM((n_pipe, group, width), BF16),
                pltpu.VMEM((n_pipe, group, width), BF16),
                pltpu.VMEM((n_pipe, group, width), BF16),
                pltpu.VMEM((n_dp, n_pipe, group, rank), BF16),
                pltpu.VMEM((n_pipe, group, rank), BF16),
                pltpu.VMEM((rank // n_dp, width), BF16),
                pltpu.VMEM((n_dp, rank // n_dp, rank), BF16),
                pltpu.VMEM((n_pipe, every, tokens), BF16),
                pltpu.VMEM((n_dp, group, width), BF16),
                pltpu.VMEM((rank, tokens), F32),
                pltpu.VMEM((rank, tokens), BF16),
                pltpu.VMEM((every, tokens), F32),
                pltpu.VMEM((every, tokens), F32),
                pltpu.VMEM((every, tokens), F32),
                pltpu.VMEM((n_pipe, 8, 128), F32),
                dma((6,)),
                dma((CHUNKS,)),
                dma((CHUNKS,)),
                dma((PIECES,)),
                dma((PIECES,)),
                dma,
                dma,
                dma((n_pipe, CHUNKS)),
                dma((n_pipe, CHUNKS)),
                dma((n_pipe, CHUNKS)),
                dma((n_pipe, CHUNKS)),
                dma((n_pipe,)),
                dma((n_pipe,)),
                dma,
                dma,
                dma,
                dma,
                dma((n_pipe,)),
                dma((n_pipe,)),
                dma((n_pipe // 2,)),
                dma((n_pipe,)),
                dma((n_pipe,)),
                dma((n_pipe,)),
                dma,
                pltpu.SemaphoreType.REGULAR,
            ],
            compiler_params=pltpu.CompilerParams(
                collective_id=0, has_side_effects=True, vmem_limit_bytes=58 << 20
            ),
            name="influence",
        )(
            act,
            cot,
            down,
            expand,
            value,
            inputs,
            hidden_cols,
            inner_cols,
            lengths.reshape(1, n_example),
            query.reshape(1, queries),
        )

    in_specs = (
        P("pipe", "dp", None),
        P("dp", None),
        P("pipe", None, None),
        P("pipe", None, None),
        P("pipe", "dp", None),
        P("pipe", "dp", None),
        P("pipe", None, None),
        P("pipe", None, None),
        P("dp"),
        P(),
    )
    return jax.shard_map(
        local, mesh=mesh, in_specs=in_specs, out_specs=P("dp", None), check_vma=False
    )
```
